32 devices in a mesh: groups: 2 (over y), seq: 4 (over x, core), heads: 4 (over z).
Axes of the slice: x: 2, y: 2, z: 4, core: 2. Of those that a mesh axis runs over, the one named last changes fastest.
Arguments:
- tokens: bfloat16 [4096, 8192], P(('groups', 'seq'), 'heads'), parts along dimension 0, may hold values from -6 to 6
- xz_weight: bfloat16 [8192, 32768], P(None, ('heads', 'seq')), may hold values from -0.0625 to 0.0625
- bc_weight: bfloat16 [8192, 2048], P(None, 'heads'), may hold values from -0.0625 to 0.0625
- step_weight: bfloat16 [8192, 256], P(None, 'heads'), may hold values from -0.0625 to 0.0625
- step_bias: float32 [256], P('heads'), may hold values from -4 to -2
- decay_log: float32 [256], P('heads'), may hold values from -5.3 to -0.7
- skip_gain: float32 [256], P('heads'), may hold values from 0.5 to 2
- conv_weight: float32 [4, 16384], P(None, 'heads'), may hold values from -3 to 3
- conv_bias: float32 [16384], P('heads'), may hold values from -3 to 3
- bc_conv_weight: float32 [4, 2048], replicated, may hold values from -3 to 3
- bc_conv_bias: float32 [2048], replicated, may hold values from -3 to 3
- norm_gain: float32 [16384], P('heads'), may hold values from 0.1 to 1.9
- step_bounds: int32 [32], P('groups'), parts along dimension 0, may hold values from 0 to 2047, as said below
- readers: int32 [32], P('groups'), parts along dimension 0, may hold values from 0 to 3, as said below
Outputs:
- mixed: bfloat16 [4096, 16384], P(('groups', 'seq'), 'heads'), parts along dimension 0
- handoff: bfloat16 [8, 4, 256, 64, 128], P(('groups', 'heads'), None, 'seq'), parts along dimension 0
The draws below stay inside these ranges and needn't reach their ends.
There are 2 independent parts, one for each index of `groups`. The reference program is written for one: setup_inputs(seed, part) draws one part's arguments, and reference() takes and returns one part's arrays. A program takes and returns all parts, laid end to end along the dimension named above; an argument that names none is the same for every part. Nothing has to cross between parts.
Inputs may be any that keep to these rules, and one draw needn't show every extreme that they name: `step_bounds`: boundary j * 4 + i, for i < 4, lies in section j: positions j * 512 to (j + 1) * 512 - 1. The first boundary is at position 0 and the last at 2047. `readers`: among the 4 boundaries of each section every reader appears exactly once.
All inputs are finite; a program needn't handle non-finite values.
Results may differ from the reference program's by a relative error of at most 0.0056.
Values may be sent and summed in bfloat16 or wider, within the bound.
A program may use at most 384 MiB of HBM per device.

```python
import jax
import jax.numpy as jnp
from jax import lax

D = 8192
H = 256
P_SIZE = 64
N = 128
G = 8
K = 4
CH = 256
SEC = 512
TRACE = 2048
READERS = 4
BOUNDS = 16


def draw_step_bounds(key, part):
    sections = BOUNDS // READERS
    offsets = jax.random.randint(jax.random.fold_in(key, 11), (sections, READERS), 0, SEC).astype(jnp.int32)
    offsets = offsets.at[0, 0].set(0)
    offsets = offsets.at[sections - 1, READERS - 1].set(SEC - 1)
    section_starts = (jnp.arange(sections, dtype=jnp.int32) * SEC)[:, None]
    return (offsets + section_starts).reshape(BOUNDS).astype(jnp.int32)


def draw_readers(key, part):
    sections = BOUNDS // READERS
    section_keys = jax.random.split(jax.random.fold_in(key, 23), sections)
    assignment = jax.vmap(lambda one_key: jax.random.permutation(one_key, READERS))(section_keys)
    return assignment.reshape(BOUNDS).astype(jnp.int32)


def levels(own_key, shape, cuts, low, top_value):
    level = 1.0
    for dim, blocks in cuts:
        steps = jax.random.uniform(jax.random.fold_in(jax.random.fold_in(own_key, 6), dim), (blocks,), jnp.float32, low / len(cuts), top_value / len(cuts))
        level = level * jnp.repeat(jnp.exp(steps), shape[dim] // blocks).reshape((-1,) + (1,) * (len(shape) - 1 - dim))
    return level


def bell_draw(own_key, shape, scale, reach, cuts=(), kind=jnp.bfloat16):
    result = scale * jax.random.normal(own_key, shape, jnp.float32)
    if cuts:
        result = result * levels(own_key, shape, cuts, -0.22, 0.18)
    return jnp.clip(result, -reach, reach).astype(kind)


def setup_inputs(seed: int = 0, part: int = 0) -> dict:
    keys = jax.random.split(jax.random.key(seed), 15)
    part_keys = jax.random.split(jax.random.fold_in(keys[14], part), 15)
    tokens = bell_draw(part_keys[0], (TRACE, D), 1.0, 6.0, ((0, 4), (1, 4)))
    xz_weight = bell_draw(keys[1], (D, H * 2 * P_SIZE), D ** -0.5, 0.0625, ((1, 16),))
    bc_weight = bell_draw(keys[2], (D, G * 2 * N), D ** -0.5, 0.0625, ((1, 4),))
    step_weight = bell_draw(keys[3], (D, H), D ** -0.5, 0.0625, ((1, 4),))
    step_bias = jnp.clip(-4.0 + 2.0 * jax.random.uniform(keys[4], (H,), jnp.float32) ** levels(keys[4], (H,), ((0, 4),), -0.2, 0.2), -4.0, -2.0)
    decay_log = jnp.clip(-5.3 + 4.6000002 * jax.random.uniform(keys[5], (H,), jnp.float32) ** levels(keys[5], (H,), ((0, 4),), -0.2, 0.2), -5.3, -0.7)
    skip_gain = jnp.clip(0.5 + 1.5 * jax.random.uniform(keys[6], (H,), jnp.float32) ** levels(keys[6], (H,), ((0, 4),), -0.2, 0.2), 0.5, 2.0)
    conv_weight = bell_draw(keys[7], (K, H * P_SIZE), K ** -0.5, 3.0, ((1, 4),), jnp.float32)
    conv_bias = bell_draw(keys[8], (H * P_SIZE,), 0.5, 3.0, ((0, 4),), jnp.float32)
    bc_conv_weight = bell_draw(keys[9], (K, G * 2 * N), K ** -0.5, 3.0, (), jnp.float32)
    bc_conv_bias = bell_draw(keys[10], (G * 2 * N,), 0.5, 3.0, (), jnp.float32)
    norm_gain = jnp.clip(1.0 + 0.18 * jax.random.normal(keys[11], (H * P_SIZE,), jnp.float32), 0.1, 1.9)
    step_bounds = draw_step_bounds(jax.random.fold_in(jax.random.fold_in(keys[14], part), 71), part)
    readers = draw_readers(jax.random.fold_in(jax.random.fold_in(keys[14], part), 71), part)
    return {"tokens": tokens, "xz_weight": xz_weight, "bc_weight": bc_weight, "step_weight": step_weight, "step_bias": step_bias, "decay_log": decay_log, "skip_gain": skip_gain, "conv_weight": conv_weight, "conv_bias": conv_bias, "bc_conv_weight": bc_conv_weight, "bc_conv_bias": bc_conv_bias, "norm_gain": norm_gain, "step_bounds": step_bounds, "readers": readers}


EPSILON = 1e-05
HIGHEST_PRECISION = lax.Precision.HIGHEST

def conv_rows(prefix, raw_rows, kernel, shift_bias):
    row_count = raw_rows.shape[0]
    padded = jnp.concatenate([prefix, raw_rows], axis=0).astype(jnp.float32)
    summed = jnp.broadcast_to(shift_bias[None, :], raw_rows.shape)
    for tap_index in range(kernel.shape[0]):
        summed = summed + kernel[tap_index][None, :] * padded[tap_index:tap_index + row_count]
    return jax.nn.silu(summed).astype(jnp.bfloat16)

def reference(tokens, xz_weight, bc_weight, step_weight, step_bias, decay_log, skip_gain, conv_weight, conv_bias, bc_conv_weight, bc_conv_bias, norm_gain, step_bounds, readers):
    length = tokens.shape[0]
    per_group = H // G
    taps = conv_weight.shape[0]
    xz_rows = jnp.dot(tokens, xz_weight, preferred_element_type=jnp.float32).astype(jnp.bfloat16).reshape(length, H, 2 * P_SIZE)
    inner_raw = xz_rows[:, :, :P_SIZE].reshape(length, H * P_SIZE)
    gate_raw = xz_rows[:, :, P_SIZE:].reshape(length, G, per_group, P_SIZE)
    bc_raw = jnp.dot(tokens, bc_weight, preferred_element_type=jnp.float32).astype(jnp.bfloat16)
    step_size = jax.nn.softplus(jnp.dot(tokens, step_weight, preferred_element_type=jnp.float32) + step_bias[None, :]).reshape(length, G, per_group)
    decay_rate = -jnp.exp(decay_log).reshape(G, per_group)[None] * step_size
    inner_conv = conv_rows(jnp.zeros((taps - 1, H * P_SIZE), jnp.bfloat16), inner_raw, conv_weight, conv_bias).reshape(length, G, per_group, P_SIZE)
    bc_conv = conv_rows(jnp.zeros((taps - 1, G * 2 * N), jnp.bfloat16), bc_raw, bc_conv_weight, bc_conv_bias).reshape(length, G, 2 * N)
    b_input = bc_conv[:, :, :N]
    c_input = bc_conv[:, :, N:]
    blocks = length // CH
    inner_blocks = inner_conv.reshape(blocks, CH, G, per_group, P_SIZE)
    b_blocks = b_input.reshape(blocks, CH, G, N)
    c_blocks = c_input.reshape(blocks, CH, G, N)
    step_blocks = step_size.reshape(blocks, CH, G, per_group)
    cum_blocks = jnp.cumsum(decay_rate.reshape(blocks, CH, G, per_group), axis=1)
    causal = lax.broadcasted_iota(jnp.int32, (CH, CH), 0) >= lax.broadcasted_iota(jnp.int32, (CH, CH), 1)

    def block_step(running, pieces):
        inner_blk, b_blk, c_blk, step_blk, cum_block = pieces
        scores = jnp.einsum('tgn,sgn->gts', c_blk.astype(jnp.float32), b_blk.astype(jnp.float32))
        cum_gap = cum_block[:, None] - cum_block[None, :]
        weight = jnp.where(causal[:, :, None, None], jnp.exp(jnp.minimum(cum_gap, 0.0)), 0.0) * step_blk[None]
        mixing = (weight * jnp.transpose(scores, (1, 2, 0))[:, :, :, None]).astype(jnp.bfloat16)
        intra_part = jnp.einsum('tsgr,sgrp->tgrp', mixing.astype(jnp.float32), inner_blk.astype(jnp.float32))
        outer_part = jnp.exp(cum_block)[..., None] * jnp.einsum('tgn,grpn->tgrp', c_blk.astype(jnp.float32), running, precision=HIGHEST_PRECISION)
        block_total = cum_block[-1]
        carry_weight = jnp.exp(block_total[None] - cum_block) * step_blk
        weighted = (inner_blk.astype(jnp.float32) * carry_weight[..., None]).astype(jnp.bfloat16)
        new_state = jnp.exp(block_total)[..., None, None] * running + jnp.einsum('sgrp,sgn->grpn', weighted.astype(jnp.float32), b_blk.astype(jnp.float32))
        return (new_state, (intra_part + outer_part, running))
    first_state = jnp.zeros((G, per_group, P_SIZE, N), jnp.float32)
    unused, (ssd_blocks, starts) = lax.scan(block_step, first_state, (inner_blocks, b_blocks, c_blocks, step_blocks, cum_blocks))
    ssd = ssd_blocks.reshape(length, G, per_group, P_SIZE) + skip_gain.reshape(G, per_group)[None, :, :, None] * inner_conv.astype(jnp.float32)
    gated = ssd * jax.nn.silu(gate_raw.astype(jnp.float32))
    square_mean = lax.optimization_barrier(jnp.sum(gated * gated, axis=(2, 3))) / (per_group * P_SIZE)
    normed = gated * lax.rsqrt(square_mean + EPSILON)[:, :, None, None] * norm_gain.reshape(G, per_group, P_SIZE)[None]
    mixed = normed.astype(jnp.bfloat16).reshape(length, H * P_SIZE)
    block_positions = lax.broadcasted_iota(jnp.int32, (CH,), 0)

    def one_bound(position):
        block_index = (position // CH).astype(jnp.int32)
        offset = (position - block_index * CH).astype(jnp.int32)
        inner_blk = lax.dynamic_index_in_dim(inner_blocks, block_index, 0, keepdims=False)
        b_blk = lax.dynamic_index_in_dim(b_blocks, block_index, 0, keepdims=False)
        step_blk = lax.dynamic_index_in_dim(step_blocks, block_index, 0, keepdims=False)
        cum_block = lax.dynamic_index_in_dim(cum_blocks, block_index, 0, keepdims=False)
        start_state = lax.dynamic_index_in_dim(starts, block_index, 0, keepdims=False)
        cum_at = lax.dynamic_index_in_dim(cum_block, offset, 0, keepdims=False)
        weight = jnp.where((block_positions <= offset)[:, None, None], jnp.exp(jnp.minimum(cum_at[None] - cum_block, 0.0)), 0.0) * step_blk
        bound_weighted = (inner_blk.astype(jnp.float32) * weight[..., None]).astype(jnp.bfloat16)
        inside = jnp.einsum('sgrp,sgn->grpn', bound_weighted.astype(jnp.float32), b_blk.astype(jnp.float32))
        return (jnp.exp(cum_at)[..., None, None] * start_state + inside).astype(jnp.bfloat16)
    states = lax.map(one_bound, step_bounds)
    sections = step_bounds.shape[0] // READERS
    states = states.reshape(sections, READERS, H, P_SIZE, N)
    order = jnp.argsort(readers.reshape(sections, READERS), axis=1).astype(jnp.int32)
    ordered = jnp.take_along_axis(states, order[:, :, None, None, None], axis=1)
    handoff = jnp.transpose(ordered, (1, 0, 2, 3, 4))
    return (mixed, handoff)
```

```python
import functools

import jax
import jax.numpy as jnp
from jax import lax
from jax.experimental import pallas as pl
from jax.experimental.pallas import tpu as pltpu
from jax.sharding import PartitionSpec as P

H = 256
P_SIZE = 64
N = 128
G = 8
CH = 256
PER_GROUP = H // G
EPSILON = 1e-05


def project(tokens, xz_weight, small_weight, chunks):
    sections, head_devices = lax.axis_size("seq"), lax.axis_size("heads")
    rows = tokens.shape[0] // chunks
    width = tokens.shape[1]
    pieces = [tokens[c * rows : (c + 1) * rows] for c in range(chunks)]
    xz, small = [], []
    for c in range(chunks):
        part = lax.all_gather(pieces[c], ("seq", "heads"), axis=0)
        part = part.reshape(sections, head_devices, rows, width)
        dot = lambda w: lax.dot_general(
            part,
            w.reshape(head_devices, width, w.shape[1]),
            (((1, 3), (0, 1)), ((), ())),
            preferred_element_type=jnp.float32,
        )
        xz.append(dot(xz_weight).astype(jnp.bfloat16))
        small.append(dot(small_weight))
        if c + 2 < chunks:
            pieces[c + 2], xz[c], small[c] = lax.optimization_barrier(
                (pieces[c + 2], xz[c], small[c])
            )
    whole = lambda parts: jnp.concatenate(parts, axis=1).reshape(-1, parts[0].shape[-1])
    return whole(xz), whole(small)


LOG2E = 1.4426950408889634
NT = (((1,), (1,)), ((), ()))


def sigmoid(x):
    return 0.5 * jnp.tanh(0.5 * x) + 0.5


def scan_section(
    j, n_read, bounds_ref, readers_ref, xz_ref, bc_ref, step_ref, conv_ref, head_ref, bconv_ref,
    gated_ref, states_ref, tail, bpad, b_in, c_in, inner, start, cum, stp, scores, mix, outer, gated_t, wt,
):
    f32, bf16 = jnp.float32, jnp.bfloat16
    heads = head_ref.shape[0]
    sec = xz_ref.shape[1]
    n_blk = sec // CH
    taps = 4

    @pl.when(j == 0)
    def _():
        tail[...] = jnp.zeros_like(tail)
        bpad[0:8, :] = jnp.zeros((8, 2 * N), f32)
        start[0] = jnp.zeros_like(start[0])
        mix[...] = jnp.zeros_like(mix)

    bpad[8 : 8 + sec, :] = bc_ref[...].astype(f32)
    for i in range(n_blk):
        y = jnp.broadcast_to(bconv_ref[taps : taps + 1, :], (CH, 2 * N))
        for k in range(taps):
            y = y + bconv_ref[k : k + 1, :] * bpad[i * CH + 5 + k : i * CH + 5 + k + CH, :]
        y = (y * sigmoid(y)).astype(bf16)
        b_in[i] = y[:, :N]
        c_in[i] = y[:, N:]
    bpad[0:8, :] = bpad[sec : sec + 8, :]

    def conv_strip(i, carry):
        row = pl.multiple_of(i * 32, 32)
        src = pl.multiple_of((i // 2) * 128 + (i % 2) * 32, 32)
        raw = xz_ref[pl.ds(src, 32), :]
        both = jnp.concatenate([tail[pl.ds(row, 32), :], raw], axis=1).astype(f32)
        w = conv_ref[pl.ds(row, 32), :]
        y = w[:, 4:5] + w[:, 3:4] * both[:, 128:]
        for d in range(1, taps):
            y = y + w[:, 3 - d : 4 - d] * pltpu.roll(both, d, 1)[:, 128:]
        y = (y * sigmoid(y)).astype(bf16)
        for b in range(n_blk):
            inner[b, pl.ds(row, 32), :] = y[:, b * CH : (b + 1) * CH]
        tail[pl.ds(row, 32), :] = raw[:, sec - 128 :]
        return carry

    lax.fori_loop(0, heads * 2, conv_strip, 0, unroll=2)

    raw = step_ref[...] + head_ref[:, 0:1]
    size = jnp.maximum(raw, 0.0) + jnp.log1p(jnp.exp(-jnp.abs(raw)))
    total = (-LOG2E * jnp.exp(head_ref[:, 1:2])) * size
    lane = lax.broadcasted_iota(jnp.int32, (heads, sec), 1) % CH
    d = 1
    while d < CH:
        total = total + jnp.where(lane >= d, pltpu.roll(total, d, 1), 0.0)
        d *= 2
    for b in range(n_blk):
        cum[b] = total[:, b * CH : (b + 1) * CH]
        stp[b] = size[:, b * CH : (b + 1) * CH]

    row_id = lax.broadcasted_iota(jnp.int32, (CH, CH), 0)
    col_id = lax.broadcasted_iota(jnp.int32, (CH, CH), 1)
    eye = (row_id == col_id).astype(bf16)

    def one_block(b, carry):
        scores[...] = jnp.where(
            row_id <= col_id,
            lax.dot_general(b_in[b], c_in[b], NT, preferred_element_type=f32), 0.0)
        outer[...] = lax.dot_general(start[b].astype(bf16), c_in[b], NT, preferred_element_type=f32)
        a = cum[b]
        s = stp[b]
        a_col = jnp.transpose(jnp.concatenate([a, jnp.zeros((128 - heads, CH), f32)], axis=0))
        grow = jnp.exp2(a)
        last = a[:, CH - 1 : CH]
        carry_row = jnp.exp2(last - a) * s
        keep = jnp.exp2(last)
        for h in range(heads):
            rows = slice(h * 64, (h + 1) * 64)
            m = h % mix.shape[0]
            a_h = a[h : h + 1, :]
            for s0 in range(0, CH, 32):
                lo = (s0 // 128) * 128
                col = a_col[s0 : s0 + 32, h : h + 1]
                gap = jnp.minimum(a_h[:, lo:] - col, 0.0)
                mix[m, s0 : s0 + 32, lo:] = (jnp.exp2(gap) * scores[s0 : s0 + 32, lo:]).astype(bf16)
            x = inner[b, rows, :].astype(f32)
            intra = jnp.dot((x * s[h : h + 1, :]).astype(bf16), mix[m], preferred_element_type=f32)
            wt[rows, :] = (x * carry_row[h : h + 1, :]).astype(bf16)
            gate = xz_ref[h * 128 + 64 : (h + 1) * 128, pl.ds(pl.multiple_of(b * CH, CH), CH)].astype(f32)
            ssd = intra + outer[rows, :] * grow[h : h + 1, :] + head_ref[h : h + 1, 2:3] * x
            gated_t[rows, :] = (ssd * (gate * sigmoid(gate))).astype(bf16)
        span = min(heads * 64, CH)
        for c in range(0, heads * 64, span):
            out = lax.dot_general(eye, gated_t[c : c + span, :], NT, preferred_element_type=f32)
            gated_ref[pl.ds(pl.multiple_of(b * CH, CH), CH), c : c + span] = out.astype(bf16)
        added = jnp.dot(wt[...], b_in[b], preferred_element_type=f32)
        for h in range(heads):
            rows = slice(h * 64, (h + 1) * 64)
            start[b + 1, rows, :] = start[b, rows, :] * keep[h : h + 1, :] + added[rows, :]
        return carry

    lax.fori_loop(0, n_blk, one_block, 0)

    lane_b = lax.broadcasted_iota(jnp.int32, (heads, CH), 1)

    def one_bound(r, carry):
        q = jnp.int32(0)
        for i in range(n_read):
            q = q + jnp.where(readers_ref[j * n_read + i] == r, bounds_ref[j * n_read + i], 0)
        q = q - j * sec
        b = q // CH
        off = q % CH
        a = cum[b]
        at = jnp.sum(jnp.where(lane_b == off, a, 0.0), axis=1, keepdims=True)
        w = jnp.where(lane_b <= off, jnp.exp2(jnp.minimum(at - a, 0.0)), 0.0) * stp[b]
        keep = jnp.exp2(at)
        for h in range(heads):
            rows = slice(h * 64, (h + 1) * 64)
            wt[rows, :] = (inner[b, rows, :].astype(f32) * w[h : h + 1, :]).astype(bf16)
        inside = jnp.dot(wt[...], b_in[b], preferred_element_type=f32)
        for h in range(heads):
            rows = slice(h * 64, (h + 1) * 64)
            states_ref[r, rows, :] = (start[b, rows, :] * keep[h : h + 1, :] + inside[rows, :]).astype(bf16)
        return carry

    lax.fori_loop(0, n_read, one_bound, 0)
    start[0] = start[n_blk]


def scan_scratch(heads, sec):
    f32, bf16 = jnp.float32, jnp.bfloat16
    n_blk = sec // CH
    return [
        pltpu.VMEM((heads * 64, 128), bf16),
        pltpu.VMEM((sec + 8, 2 * N), f32),
        pltpu.VMEM((n_blk, CH, N), bf16),
        pltpu.VMEM((n_blk, CH, N), bf16),
        pltpu.VMEM((n_blk, heads * 64, CH), bf16),
        pltpu.VMEM((n_blk + 1, heads * 64, N), f32),
        pltpu.VMEM((n_blk, heads, CH), f32),
        pltpu.VMEM((n_blk, heads, CH), f32),
        pltpu.VMEM((CH, CH), f32),
        pltpu.VMEM((4, CH, CH), bf16),
        pltpu.VMEM((heads * 64, CH), f32),
        pltpu.VMEM((heads * 64, CH), bf16),
        pltpu.VMEM((heads * 64, CH), bf16),
    ]


def scan_kernel(n_read, *refs):
    refs = list(refs)
    states = refs[9]
    refs[9] = states.at[:, 0]
    scan_section(pl.program_id(0), n_read, *refs)


def scan_call(xz_t, bc_raw, step_t, conv_cols, head_cols, bconv, bounds, readers, sections):
    heads = head_cols.shape[0]
    length = xz_t.shape[1]
    sec = length // sections
    n_read = bounds.shape[0] // sections
    whole = lambda a: pl.BlockSpec(a.shape, lambda j: (0,) * a.ndim)
    smem = pl.BlockSpec(memory_space=pltpu.SMEM)
    return pl.pallas_call(
        functools.partial(scan_kernel, n_read),
        grid=(sections,),
        in_specs=[
            smem,
            smem,
            pl.BlockSpec((heads * 128, sec), lambda j: (0, j)),
            pl.BlockSpec((sec, 2 * N), lambda j: (j, 0)),
            pl.BlockSpec((heads, sec), lambda j: (0, j)),
            whole(conv_cols),
            whole(head_cols),
            whole(bconv),
        ],
        out_specs=[
            pl.BlockSpec((sec, heads * 64), lambda j: (j, 0)),
            pl.BlockSpec((n_read, 1, heads * 64, N), lambda j: (0, j, 0, 0)),
        ],
        out_shape=[
            jax.ShapeDtypeStruct((length, heads * 64), jnp.bfloat16),
            jax.ShapeDtypeStruct((n_read, sections, heads * 64, N), jnp.bfloat16),
        ],
        scratch_shapes=scan_scratch(heads, sec),
        compiler_params=pltpu.CompilerParams(vmem_limit_bytes=40 * 1024 * 1024),
        name="scan",
    )(bounds, readers, xz_t, bc_raw, step_t, conv_cols, head_cols, bconv)


def norm_kernel(x_ref, gain_ref, o_ref):
    sources, rows, width = x_ref.shape
    per = (PER_GROUP * P_SIZE) // width
    for g in range(sources // per):
        part = [x_ref[g * per + i].astype(jnp.float32) for i in range(per)]
        square = sum(jnp.sum(p * p, axis=1, keepdims=True) for p in part)
        scale = lax.rsqrt(square / (PER_GROUP * P_SIZE) + EPSILON)
        for i, p in enumerate(part):
            cols = slice((g * per + i) * width, (g * per + i + 1) * width)
            o_ref[:, cols] = (p * scale * gain_ref[:, cols]).astype(jnp.bfloat16)


def norm_call(gathered, gain):
    sources, rows, width = gathered.shape
    tile = 64
    return pl.pallas_call(
        norm_kernel,
        grid=(rows // tile,),
        in_specs=[
            pl.BlockSpec((sources, tile, width), lambda i: (0, i, 0)),
            pl.BlockSpec((1, sources * width), lambda i: (0, 0)),
        ],
        out_specs=pl.BlockSpec((tile, sources * width), lambda i: (i, 0)),
        out_shape=jax.ShapeDtypeStruct((rows, sources * width), jnp.bfloat16),
        compiler_params=pltpu.CompilerParams(vmem_limit_bytes=32 * 1024 * 1024),
        name="norm",
    )(gathered, gain)


def fast_shards(
    tokens,
    xz_weight,
    bc_weight,
    step_weight,
    step_bias,
    decay_log,
    skip_gain,
    conv_weight,
    conv_bias,
    bc_conv_weight,
    bc_conv_bias,
    norm_gain,
    step_bounds,
    readers,
):
    head_devices = lax.axis_size("heads")
    sections = lax.axis_size("seq")
    section = lax.axis_index("seq")
    head_block = lax.axis_index("heads")
    block_heads = H // head_devices
    mine = block_heads // sections
    first_mine = section * mine
    group = (head_block * block_heads + first_mine) // PER_GROUP
    own = lambda a, width, axis: lax.dynamic_slice_in_dim(a, first_mine * width, mine * width, axis)
    conv_cols = jnp.transpose(
        jnp.concatenate([own(conv_weight, P_SIZE, 1), own(conv_bias, P_SIZE, 0)[None], jnp.zeros((3, mine * P_SIZE), jnp.float32)], axis=0)
    )
    head_cols = jnp.stack([own(a, 1, 0) for a in (step_bias, decay_log, skip_gain)], axis=1)
    pick = lambda a, axis: lax.dynamic_slice_in_dim(a, group * 2 * N, 2 * N, axis)
    bconv = jnp.concatenate([pick(bc_conv_weight, 1), pick(bc_conv_bias, 0)[None], jnp.zeros((3, 2 * N), jnp.float32)], axis=0)

    width_bc = bc_weight.shape[1]
    whole_group = width_bc >= 2 * N
    if whole_group:
        bc_weight = lax.dynamic_slice_in_dim(bc_weight, group * 2 * N - head_block * width_bc, 2 * N, 1)
    bc_width = bc_weight.shape[1]
    small_weight = jnp.concatenate([bc_weight, own(step_weight, 1, 1)], axis=1)
    xz, small = project(tokens, xz_weight, small_weight, 4)
    bc_raw = small[:, :bc_width].astype(jnp.bfloat16)
    if not whole_group:
        bc_raw = lax.all_gather(bc_raw, "heads", axis=1, tiled=True)
        bc_raw = lax.dynamic_slice_in_dim(bc_raw, group * 2 * N, 2 * N, 1)
    step_t = jnp.transpose(small[:, bc_width:])
    xz_t = jnp.transpose(xz)

    gated, states = scan_call(xz_t, bc_raw, step_t, conv_cols, head_cols, bconv, step_bounds, readers, sections)
    states = states.reshape(-1, sections, mine, P_SIZE, N)
    handoff = exchange_states(states)
    gathered = lax.all_to_all(gated.reshape(sections, -1, mine * P_SIZE), "seq", split_axis=0, concat_axis=0, tiled=True)
    if block_heads % PER_GROUP == 0:
        return (norm_call(gathered, norm_gain[None]), handoff)
    return (norm_split(gathered, norm_gain), handoff)


def norm_split(gathered, gain):
    wide = jnp.moveaxis(gathered, 0, 1).reshape(gathered.shape[1], -1).astype(jnp.float32)
    first_group = lax.axis_index("heads") * wide.shape[1] // (PER_GROUP * P_SIZE)
    at_group = lax.broadcasted_iota(jnp.int32, (1, G), 1) == first_group
    square = jnp.sum(jnp.square(wide), axis=1, keepdims=True)
    square = lax.psum(jnp.where(at_group, square, 0.0), "heads")
    square = jnp.sum(jnp.where(at_group, square, 0.0), axis=1, keepdims=True)
    scale = lax.rsqrt(square / (PER_GROUP * P_SIZE) + EPSILON)
    return (wide * scale * gain[None]).astype(jnp.bfloat16)


def exchange_states(states):
    head_devices, sections = lax.axis_size("heads"), lax.axis_size("seq")
    section, head_block = lax.axis_index("seq"), lax.axis_index("heads")
    mine = states.shape[2]
    sub = head_devices // sections
    rank = section * sub + head_block % sub
    pieces = []
    for d in range(head_devices):
        pairs = [
            (s * head_devices + k, (k // sub) * head_devices + (s * sub + k % sub + d) % head_devices)
            for s in range(sections)
            for k in range(head_devices)
        ]
        piece = lax.dynamic_index_in_dim(states, (rank + d) % head_devices, 0, False)
        pieces.append(lax.ppermute(piece, ("seq", "heads"), pairs))
    backward = jnp.stack(pieces[::-1] + pieces[::-1])
    by_rank = lax.dynamic_slice_in_dim(backward, head_devices - 1 - head_block, head_devices, 0)
    by_rank = by_rank.reshape(sections, sub, sections, mine, P_SIZE, N)
    return jnp.transpose(by_rank, (2, 1, 0, 3, 4, 5)).reshape(1, sections, sub * sections * mine, P_SIZE, N)


def solution(mesh):
    in_specs = (
        P(("groups", "seq"), "heads"),
        P(None, ("heads", "seq")),
        P(None, "heads"),
        P(None, "heads"),
        P("heads"),
        P("heads"),
        P("heads"),
        P(None, "heads"),
        P("heads"),
        P(),
        P(),
        P("heads"),
        P("groups"),
        P("groups"),
    )
    out_specs = (P(("groups", "seq"), "heads"), P(("groups", "heads"), None, "seq", None, None))
    return jax.shard_map(fast_shards, mesh=mesh, in_specs=in_specs, out_specs=out_specs, check_vma=False)
```

```python
import functools

import jax
import jax.numpy as jnp
from jax import lax
from jax.experimental import pallas as pl
from jax.experimental.pallas import tpu as pltpu
from jax.sharding import PartitionSpec as P

H = 256
P_SIZE = 64
N = 128
G = 8
CH = 256
PER_GROUP = H // G
EPSILON = 1e-05


def project(tokens, xz_weight, small_weight, chunks):
    sections, head_devices = lax.axis_size("seq"), lax.axis_size("heads")
    rows = tokens.shape[0] // chunks
    width = tokens.shape[1]
    pieces = [tokens[c * rows : (c + 1) * rows] for c in range(chunks)]
    xz, small = [], []
    for c in range(chunks):
        part = lax.all_gather(pieces[c], ("seq", "heads"), axis=0)
        part = part.reshape(sections, head_devices, rows, width)
        dot = lambda w: lax.dot_general(
            part,
            w.reshape(head_devices, width, w.shape[1]),
            (((1, 3), (0, 1)), ((), ())),
            preferred_element_type=jnp.float32,
        )
        xz.append(dot(xz_weight).astype(jnp.bfloat16))
        small.append(dot(small_weight))
        if c + 2 < chunks:
            pieces[c + 2], xz[c], small[c] = lax.optimization_barrier(
                (pieces[c + 2], xz[c], small[c])
            )
    whole = lambda parts: jnp.concatenate(parts, axis=1).reshape(-1, parts[0].shape[-1])
    return whole(xz), whole(small)


LOG2E = 1.4426950408889634
NT = (((1,), (1,)), ((), ()))


def sigmoid(x):
    return 0.5 * jnp.tanh(0.5 * x) + 0.5


def scan_section(
    j, n_read, bounds_ref, readers_ref, xz_ref, bc_ref, step_ref, conv_ref, head_ref, bconv_ref,
    gated_ref, states_ref, tail, bpad, b_in, c_in, inner, start, cum, stp, scores, mix, outer, gated_t, wt,
):
    f32, bf16 = jnp.float32, jnp.bfloat16
    heads = head_ref.shape[0]
    sec = xz_ref.shape[1]
    n_blk = sec // CH
    taps = 4

    @pl.when(j == 0)
    def _():
        tail[...] = jnp.zeros_like(tail)
        bpad[0:8, :] = jnp.zeros((8, 2 * N), f32)
        start[0] = jnp.zeros_like(start[0])
        mix[...] = jnp.zeros_like(mix)

    bpad[8 : 8 + sec, :] = bc_ref[...].astype(f32)
    for i in range(n_blk):
        y = jnp.broadcast_to(bconv_ref[taps : taps + 1, :], (CH, 2 * N))
        for k in range(taps):
            y = y + bconv_ref[k : k + 1, :] * bpad[i * CH + 5 + k : i * CH + 5 + k + CH, :]
        y = (y * sigmoid(y)).astype(bf16)
        b_in[i] = y[:, :N]
        c_in[i] = y[:, N:]
    bpad[0:8, :] = bpad[sec : sec + 8, :]

    def conv_strip(i, carry):
        row = pl.multiple_of(i * 32, 32)
        src = pl.multiple_of((i // 2) * 128 + (i % 2) * 32, 32)
        raw = xz_ref[pl.ds(src, 32), :]
        both = jnp.concatenate([tail[pl.ds(row, 32), :], raw], axis=1).astype(f32)
        w = conv_ref[pl.ds(row, 32), :]
        y = w[:, 4:5] + w[:, 3:4] * both[:, 128:]
        for d in range(1, taps):
            y = y + w[:, 3 - d : 4 - d] * pltpu.roll(both, d, 1)[:, 128:]
        y = (y * sigmoid(y)).astype(bf16)
        for b in range(n_blk):
            inner[b, pl.ds(row, 32), :] = y[:, b * CH : (b + 1) * CH]
        tail[pl.ds(row, 32), :] = raw[:, sec - 128 :]
        return carry

    lax.fori_loop(0, heads * 2, conv_strip, 0, unroll=2)

    raw = step_ref[...] + head_ref[:, 0:1]
    size = jnp.maximum(raw, 0.0) + jnp.log1p(jnp.exp(-jnp.abs(raw)))
    total = (-LOG2E * jnp.exp(head_ref[:, 1:2])) * size
    lane = lax.broadcasted_iota(jnp.int32, (heads, sec), 1) % CH
    d = 1
    while d < CH:
        total = total + jnp.where(lane >= d, pltpu.roll(total, d, 1), 0.0)
        d *= 2
    for b in range(n_blk):
        cum[b] = total[:, b * CH : (b + 1) * CH]
        stp[b] = size[:, b * CH : (b + 1) * CH]

    row_id = lax.broadcasted_iota(jnp.int32, (CH, CH), 0)
    col_id = lax.broadcasted_iota(jnp.int32, (CH, CH), 1)
    eye = (row_id == col_id).astype(bf16)

    def one_block(b, carry):
        scores[...] = jnp.where(
            row_id <= col_id,
            lax.dot_general(b_in[b], c_in[b], NT, preferred_element_type=f32), 0.0)
        outer[...] = lax.dot_general(start[b].astype(bf16), c_in[b], NT, preferred_element_type=f32)
        a = cum[b]
        s = stp[b]
        a_col = jnp.transpose(jnp.concatenate([a, jnp.zeros((128 - heads, CH), f32)], axis=0))
        grow = jnp.exp2(a)
        last = a[:, CH - 1 : CH]
        carry_row = jnp.exp2(last - a) * s
        keep = jnp.exp2(last)
        for h in range(heads):
            rows = slice(h * 64, (h + 1) * 64)
            m = h % mix.shape[0]
            a_h = a[h : h + 1, :]
            for s0 in range(0, CH, 32):
                lo = (s0 // 128) * 128
                col = a_col[s0 : s0 + 32, h : h + 1]
                gap = jnp.minimum(a_h[:, lo:] - col, 0.0)
                mix[m, s0 : s0 + 32, lo:] = (jnp.exp2(gap) * scores[s0 : s0 + 32, lo:]).astype(bf16)
            x = inner[b, rows, :].astype(f32)
            intra = jnp.dot((x * s[h : h + 1, :]).astype(bf16), mix[m], preferred_element_type=f32)
            wt[rows, :] = (x * carry_row[h : h + 1, :]).astype(bf16)
            gate = xz_ref[h * 128 + 64 : (h + 1) * 128, pl.ds(pl.multiple_of(b * CH, CH), CH)].astype(f32)
            ssd = intra + outer[rows, :] * grow[h : h + 1, :] + head_ref[h : h + 1, 2:3] * x
            gated_t[rows, :] = (ssd * (gate * sigmoid(gate))).astype(bf16)
        span = min(heads * 64, CH)
        for c in range(0, heads * 64, span):
            out = lax.dot_general(eye, gated_t[c : c + span, :], NT, preferred_element_type=f32)
            gated_ref[pl.ds(pl.multiple_of(b * CH, CH), CH), c : c + span] = out.astype(bf16)
        added = jnp.dot(wt[...], b_in[b], preferred_element_type=f32)
        for h in range(heads):
            rows = slice(h * 64, (h + 1) * 64)
            start[b + 1, rows, :] = start[b, rows, :] * keep[h : h + 1, :] + added[rows, :]
        return carry

    lax.fori_loop(0, n_blk, one_block, 0)

    lane_b = lax.broadcasted_iota(jnp.int32, (heads, CH), 1)

    def one_bound(r, carry):
        q = jnp.int32(0)
        for i in range(n_read):
            q = q + jnp.where(readers_ref[j * n_read + i] == r, bounds_ref[j * n_read + i], 0)
        q = q - j * sec
        b = q // CH
        off = q % CH
        a = cum[b]
        at = jnp.sum(jnp.where(lane_b == off, a, 0.0), axis=1, keepdims=True)
        w = jnp.where(lane_b <= off, jnp.exp2(jnp.minimum(at - a, 0.0)), 0.0) * stp[b]
        keep = jnp.exp2(at)
        for h in range(heads):
            rows = slice(h * 64, (h + 1) * 64)
            wt[rows, :] = (inner[b, rows, :].astype(f32) * w[h : h + 1, :]).astype(bf16)
        inside = jnp.dot(wt[...], b_in[b], preferred_element_type=f32)
        for h in range(heads):
            rows = slice(h * 64, (h + 1) * 64)
            states_ref[r, rows, :] = (start[b, rows, :] * keep[h : h + 1, :] + inside[rows, :]).astype(bf16)
        return carry

    lax.fori_loop(0, n_read, one_bound, 0)
    start[0] = start[n_blk]


def scan_scratch(heads, sec):
    f32, bf16 = jnp.float32, jnp.bfloat16
    n_blk = sec // CH
    return [
        pltpu.VMEM((heads * 64, 128), bf16),
        pltpu.VMEM((sec + 8, 2 * N), f32),
        pltpu.VMEM((n_blk, CH, N), bf16),
        pltpu.VMEM((n_blk, CH, N), bf16),
        pltpu.VMEM((n_blk, heads * 64, CH), bf16),
        pltpu.VMEM((n_blk + 1, heads * 64, N), f32),
        pltpu.VMEM((n_blk, heads, CH), f32),
        pltpu.VMEM((n_blk, heads, CH), f32),
        pltpu.VMEM((CH, CH), f32),
        pltpu.VMEM((4, CH, CH), bf16),
        pltpu.VMEM((heads * 64, CH), f32),
        pltpu.VMEM((heads * 64, CH), bf16),
        pltpu.VMEM((heads * 64, CH), bf16),
    ]


def scan_kernel(n_read, *refs):
    refs = list(refs)
    states = refs[9]
    refs[9] = states.at[:, 0]
    scan_section(pl.program_id(0), n_read, *refs)


def scan_call(xz_t, bc_raw, step_t, conv_cols, head_cols, bconv, bounds, readers, sections):
    heads = head_cols.shape[0]
    length = xz_t.shape[1]
    sec = length // sections
    n_read = bounds.shape[0] // sections
    whole = lambda a: pl.BlockSpec(a.shape, lambda j: (0,) * a.ndim)
    smem = pl.BlockSpec(memory_space=pltpu.SMEM)
    return pl.pallas_call(
        functools.partial(scan_kernel, n_read),
        grid=(sections,),
        in_specs=[
            smem,
            smem,
            pl.BlockSpec((heads * 128, sec), lambda j: (0, j)),
            pl.BlockSpec((sec, 2 * N), lambda j: (j, 0)),
            pl.BlockSpec((heads, sec), lambda j: (0, j)),
            whole(conv_cols),
            whole(head_cols),
            whole(bconv),
        ],
        out_specs=[
            pl.BlockSpec((sec, heads * 64), lambda j: (j, 0)),
            pl.BlockSpec((n_read, 1, heads * 64, N), lambda j: (0, j, 0, 0)),
        ],
        out_shape=[
            jax.ShapeDtypeStruct((length, heads * 64), jnp.bfloat16),
            jax.ShapeDtypeStruct((n_read, sections, heads * 64, N), jnp.bfloat16),
        ],
        scratch_shapes=scan_scratch(heads, sec),
        compiler_params=pltpu.CompilerParams(vmem_limit_bytes=40 * 1024 * 1024),
        name="scan",
    )(bounds, readers, xz_t, bc_raw, step_t, conv_cols, head_cols, bconv)


def norm_kernel(x_ref, gain_ref, o_ref):
    sources, rows, width = x_ref.shape
    per = (PER_GROUP * P_SIZE) // width
    for g in range(sources // per):
        part = [x_ref[g * per + i].astype(jnp.float32) for i in range(per)]
        square = sum(jnp.sum(p * p, axis=1, keepdims=True) for p in part)
        scale = lax.rsqrt(square / (PER_GROUP * P_SIZE) + EPSILON)
        for i, p in enumerate(part):
            cols = slice((g * per + i) * width, (g * per + i + 1) * width)
            o_ref[:, cols] = (p * scale * gain_ref[:, cols]).astype(jnp.bfloat16)


def norm_call(gathered, gain):
    sources, rows, width = gathered.shape
    tile = 64
    return pl.pallas_call(
        norm_kernel,
        grid=(rows // tile,),
        in_specs=[
            pl.BlockSpec((sources, tile, width), lambda i: (0, i, 0)),
            pl.BlockSpec((1, sources * width), lambda i: (0, 0)),
        ],
        out_specs=pl.BlockSpec((tile, sources * width), lambda i: (i, 0)),
        out_shape=jax.ShapeDtypeStruct((rows, sources * width), jnp.bfloat16),
        compiler_params=pltpu.CompilerParams(vmem_limit_bytes=32 * 1024 * 1024),
        name="norm",
    )(gathered, gain)


MESH = pl.DeviceIdType.MESH


def nearest_first(z, k, count):
    h = jnp.int32(0)
    for at in range(count):
        order = sorted(range(count), key=lambda q: (abs(q - at), q))
        for i, q in enumerate(order):
            if q:
                h = h + jnp.where((z == at) & (k == i), q, 0)
    return h


def gather_project_kernel(
    pieces, tok, xw, bw, sw, xz_out, bc_out, st_out, every,
    wx, wb, ws, tile, ax, ab, ast, ox, ob, ost,
    recv, up_sem, down_sem, x_sem, c_sem, w_sem, tile_sem, out_sem,
):
    f32, bf16 = jnp.float32, jnp.bfloat16
    s, z = lax.axis_index("seq"), lax.axis_index("heads")
    line = lax.axis_size("heads")
    other = (s + 2) % 4
    sib = s + 1 - 2 * (s % 2)
    far = (sib + 2) % 4
    rows_all, depth = tok.shape
    rows = rows_all // pieces
    part = lambda p: pl.ds(pl.multiple_of(p * rows, rows), rows)
    below, above = z > 0, z < line - 1

    barrier = pltpu.get_barrier_semaphore()
    for partner in (other, sib):
        pl.semaphore_signal(barrier, inc=1, device_id={"seq": partner}, device_id_type=MESH)

    @pl.when(above)
    def _():
        pl.semaphore_signal(barrier, inc=1, device_id={"heads": z + 1}, device_id_type=MESH)

    @pl.when(below)
    def _():
        pl.semaphore_signal(barrier, inc=1, device_id={"heads": z - 1}, device_id_type=MESH)

    pl.semaphore_wait(barrier, 2 + above.astype(jnp.int32) + below.astype(jnp.int32))

    def copy(src, sec, h, p, sem, to):
        return pltpu.make_async_remote_copy(
            src_ref=src, dst_ref=every.at[h, sec, part(p)], send_sem=sem, recv_sem=recv.at[sec, h, p],
            device_id=to, device_id_type=MESH,
        )

    held = lambda sec, h, p: every.at[h, sec, part(p)]
    go_up = lambda src, h, p: copy(src, s, h, p, up_sem.at[h, p], {"heads": z + 1})
    go_down = lambda src, h, p: copy(src, s, h, p, down_sem.at[h, p], {"heads": z - 1})
    go_x = lambda src, h, p: copy(src, s, h, p, x_sem.at[h, p], {"seq": other})
    go_c = lambda src, sec, i, h, p: copy(src, sec, h, p, c_sem.at[i, h, p], {"seq": sib})
    arrived = lambda sec, h, p: copy(held(sec, h, p), sec, h, p, x_sem.at[h, p], {"seq": other}).wait_recv()

    def weights(h, slot):
        src = pl.ds(pl.multiple_of(h * depth, depth), depth)
        return [
            pltpu.make_async_copy(xw.at[src], wx.at[slot], w_sem.at[slot, 0]),
            pltpu.make_async_copy(
                bw.at[src, pl.ds(pl.multiple_of((s // 2) * 2 * N, 2 * N), 2 * N)], wb.at[slot], w_sem.at[slot, 1]),
            pltpu.make_async_copy(sw.at[src], ws.at[slot], w_sem.at[slot, 2]),
        ]

    load = lambda src, b: pltpu.make_async_copy(src, tile.at[b], tile_sem.at[b])

    def send_own(p):
        own = tok.at[part(p)]

        @pl.when(above)
        def _():
            go_up(own, z, p).start()

        @pl.when(below)
        def _():
            go_down(own, z, p).start()

        go_x(own, z, p).start()
        go_c(own, s, 0, z, p).start()

    for p in range(pieces):
        send_own(p)
    for k in range(2):
        for c in weights(nearest_first(z, k, line), k):
            c.start()

    ab[...] = jnp.zeros_like(ab)
    ast[...] = jnp.zeros_like(ast)

    def clear(i, carry):
        ax[i // 8, pl.ds(pl.multiple_of((i % 8) * (rows_all // 8), rows_all // 8), rows_all // 8), :] = jnp.zeros(
            (rows_all // 8, ax.shape[2]), f32)
        return carry

    lax.fori_loop(0, 4 * 8, clear, 0)

    wide = min(256, ax.shape[2])

    def multiply(b, slot, sec, p):
        def one(n, carry):
            cols = pl.ds(pl.multiple_of(n * wide, wide), wide)
            ax[sec, part(p), cols] += jnp.dot(tile[b], wx[slot, :, cols], preferred_element_type=f32)
            return carry

        lax.fori_loop(0, ax.shape[2] // wide, one, 0)
        ab[sec, part(p), :] += jnp.dot(tile[b], wb[slot], preferred_element_type=f32)
        cut = ws.shape[2]
        ast[sec, part(p), 0:cut] += jnp.dot(tile[b], ws[slot], preferred_element_type=f32)

    mine = st_out.shape[0]
    eye = (
        lax.broadcasted_iota(jnp.int32, (wide, wide), 0) == lax.broadcasted_iota(jnp.int32, (wide, wide), 1)
    ).astype(bf16)

    def results(q, sec, p):
        at = pl.ds(pl.multiple_of(sec * rows_all + p * rows, rows), rows)
        return [
            pltpu.make_async_copy(ox.at[q], xz_out.at[:, at], out_sem.at[q, 0]),
            pltpu.make_async_copy(ob.at[q], bc_out.at[at], out_sem.at[q, 1]),
            pltpu.make_async_copy(
                ost.at[q, pl.ds(pl.multiple_of(s * mine, 8), mine)], st_out.at[:, at], out_sem.at[q, 2]),
        ]

    def finish(q, sec, p):
        def one(n, carry):
            cols = pl.ds(pl.multiple_of(n * wide, wide), wide)
            block = ax[sec, part(p), cols].astype(bf16)
            turned = lax.dot_general(eye, block, NT, preferred_element_type=f32)
            ox[q, cols, :] = turned.astype(bf16)
            return carry

        lax.fori_loop(0, ax.shape[2] // wide, one, 0)
        ob[q] = ab[sec, part(p), :].astype(bf16)
        ost[q] = jnp.transpose(ast[sec, part(p), :])
        for c in results(q, sec, p):
            c.start()

    def step(i, carry):
        u, p = i // pieces, i % pieces
        for sign in (-1, 1):
            h = z + sign * u

            @pl.when((u >= 1) & (h >= 0) & (h < line))
            def _():
                arrived(s, h, p)
                src = held(s, h, p)
                if sign < 0:
                    @pl.when(above)
                    def _():
                        go_up(src, h, p).start()
                else:
                    @pl.when(below)
                    def _():
                        go_down(src, h, p).start()
                go_x(src, h, p).start()
                go_c(src, s, 0, h, p).start()

        h_new = nearest_first(z, u, line)
        h_old = nearest_first(z, u - 1, line)
        new, old = u < line, u >= 1

        @pl.when(old)
        def _():
            arrived(other, h_old, p)
            go_c(held(other, h_old, p), other, 1, h_old, p).start()
            load(held(other, h_old, p), 1).start()

        @pl.when(u == 0)
        def _():
            load(tok.at[part(p)], 0).start()

        @pl.when(new & old)
        def _():
            load(held(s, h_new, p), 0).start()

        @pl.when(new & (p == 0))
        def _():
            for c in weights(h_new, u % 2):
                c.wait()

        @pl.when(new)
        def _():
            load(held(s, h_new, p), 0).wait()
            multiply(0, u % 2, s, p)
            arrived(sib, h_new, p)
            load(held(sib, h_new, p), 2).start()

        @pl.when(old)
        def _():
            load(held(other, h_old, p), 1).wait()
            multiply(1, (u - 1) % 2, other, p)
            arrived(far, h_old, p)
            load(held(far, h_old, p), 3).start()

        @pl.when(new)
        def _():
            load(held(sib, h_new, p), 2).wait()
            multiply(2, u % 2, sib, p)

        @pl.when(old)
        def _():
            load(held(far, h_old, p), 3).wait()
            multiply(3, (u - 1) % 2, far, p)

        @pl.when(old & (u < line - 1) & (p == pieces - 1))
        def _():
            for c in weights(nearest_first(z, u + 1, line), (u + 1) % 2):
                c.start()

        @pl.when(u >= line - 1)
        def _():
            last = u == line
            first_sec, second_sec = jnp.where(last, other, s), jnp.where(last, far, sib)

            def one(q, carry):
                sec = jnp.where(q == 0, first_sec, second_sec)

                @pl.when(i > (line - 1) * pieces)
                def _():
                    for c in results(q, sec, p):
                        c.wait()

                finish(q, sec, p)
                return carry

            lax.fori_loop(0, 2, one, 0)

        return carry

    lax.fori_loop(0, (line + 1) * pieces, step, 0)

    for q in range(2):
        for c in results(q, s, 0):
            c.wait()

    def drain(i, carry):
        h, p = i // pieces, i % pieces
        src = held(s, h, p)

        @pl.when(above & (h <= z))
        def _():
            go_up(src, h, p).wait_send()

        @pl.when(below & (h >= z))
        def _():
            go_down(src, h, p).wait_send()

        go_x(src, h, p).wait_send()
        go_c(src, s, 0, h, p).wait_send()
        go_c(src, s, 1, h, p).wait_send()
        return carry

    lax.fori_loop(0, line * pieces, drain, 0)


def gather_project(tokens, xz_weight, bc_weight, step_weight, mine):
    pieces = 2
    sections, line = lax.axis_size("seq"), lax.axis_size("heads")
    rows_all, depth = tokens.shape
    rows = rows_all // pieces
    width = xz_weight.shape[1]
    steps = step_weight.shape[1]
    length = rows_all * sections
    f32, bf16 = jnp.float32, jnp.bfloat16
    hbm = pl.BlockSpec(memory_space=pl.ANY)
    dma = pltpu.SemaphoreType.DMA
    wide = min(256, width)
    flops = 2 * length * depth * line * (width + 2 * N + steps)
    return pl.pallas_call(
        functools.partial(gather_project_kernel, pieces),
        in_specs=[hbm] * 4,
        out_specs=[hbm] * 4,
        out_shape=[
            jax.ShapeDtypeStruct((width, length), bf16),
            jax.ShapeDtypeStruct((length, 2 * N), bf16),
            jax.ShapeDtypeStruct((mine, length), f32),
            jax.ShapeDtypeStruct((line, sections, rows_all, depth), bf16),
        ],
        scratch_shapes=[
            pltpu.VMEM((2, depth, width), bf16),
            pltpu.VMEM((2, depth, 2 * N), bf16),
            pltpu.VMEM((2, depth, steps), bf16),
            pltpu.VMEM((4, rows, depth), bf16),
            pltpu.VMEM((sections, rows_all, width), f32),
            pltpu.VMEM((sections, rows_all, 2 * N), f32),
            pltpu.VMEM((sections, rows_all, 128), f32),
            pltpu.VMEM((2, width, rows), bf16),
            pltpu.VMEM((2, rows, 2 * N), bf16),
            pltpu.VMEM((2, 128, rows), f32),
            dma((sections, line, pieces)),
            dma((line, pieces)),
            dma((line, pieces)),
            dma((line, pieces)),
            dma((2, line, pieces)),
            dma((2, 3)),
            dma((4,)),
            dma((2, 3)),
        ],
        compiler_params=pltpu.CompilerParams(
            collective_id=0, has_side_effects=True, vmem_limit_bytes=60 * 1024 * 1024),
        cost_estimate=pl.CostEstimate(flops=flops, bytes_accessed=100_000_000, transcendentals=0),
        name="gather_project",
    )(tokens, xz_weight, bc_weight, step_weight)[:3]


def fast_shards(
    tokens,
    xz_weight,
    bc_weight,
    step_weight,
    step_bias,
    decay_log,
    skip_gain,
    conv_weight,
    conv_bias,
    bc_conv_weight,
    bc_conv_bias,
    norm_gain,
    step_bounds,
    readers,
):
    head_devices = lax.axis_size("heads")
    sections = lax.axis_size("seq")
    section = lax.axis_index("seq")
    head_block = lax.axis_index("heads")
    block_heads = H // head_devices
    mine = block_heads // sections
    first_mine = section * mine
    group = (head_block * block_heads + first_mine) // PER_GROUP
    own = lambda a, width, axis: lax.dynamic_slice_in_dim(a, first_mine * width, mine * width, axis)
    conv_cols = jnp.transpose(
        jnp.concatenate([own(conv_weight, P_SIZE, 1), own(conv_bias, P_SIZE, 0)[None], jnp.zeros((3, mine * P_SIZE), jnp.float32)], axis=0)
    )
    head_cols = jnp.stack([own(a, 1, 0) for a in (step_bias, decay_log, skip_gain)], axis=1)
    pick = lambda a, axis: lax.dynamic_slice_in_dim(a, group * 2 * N, 2 * N, axis)
    bconv = jnp.concatenate([pick(bc_conv_weight, 1), pick(bc_conv_bias, 0)[None], jnp.zeros((3, 2 * N), jnp.float32)], axis=0)

    if head_devices == 4 and sections == 4:
        xz_t, bc_raw, step_t = gather_project(tokens, xz_weight, bc_weight, step_weight, mine)
    else:
        small_step = own(step_weight, 1, 1)
        xz_t, bc_raw, step_t = project_parts(tokens, xz_weight, bc_weight, small_step, group)

    gated, states = scan_call(xz_t, bc_raw, step_t, conv_cols, head_cols, bconv, step_bounds, readers, sections)
    states = states.reshape(-1, sections, mine, P_SIZE, N)
    handoff = exchange_states(states)
    gathered = lax.all_to_all(gated.reshape(sections, -1, mine * P_SIZE), "seq", split_axis=0, concat_axis=0, tiled=True)
    if block_heads % PER_GROUP == 0:
        return (norm_call(gathered, norm_gain[None]), handoff)
    return (norm_split(gathered, norm_gain), handoff)


def project_parts(tokens, xz_weight, bc_weight, step_weight, group):
    head_block = lax.axis_index("heads")
    width_bc = bc_weight.shape[1]
    whole_group = width_bc >= 2 * N
    if whole_group:
        bc_weight = lax.dynamic_slice_in_dim(bc_weight, group * 2 * N - head_block * width_bc, 2 * N, 1)
    bc_width = bc_weight.shape[1]
    xz, small = project(tokens, xz_weight, jnp.concatenate([bc_weight, step_weight], axis=1), 4)
    bc_raw = small[:, :bc_width].astype(jnp.bfloat16)
    if not whole_group:
        bc_raw = lax.all_gather(bc_raw, "heads", axis=1, tiled=True)
        bc_raw = lax.dynamic_slice_in_dim(bc_raw, group * 2 * N, 2 * N, 1)
    return jnp.transpose(xz), bc_raw, jnp.transpose(small[:, bc_width:])


def norm_split(gathered, gain):
    wide = jnp.moveaxis(gathered, 0, 1).reshape(gathered.shape[1], -1).astype(jnp.float32)
    first_group = lax.axis_index("heads") * wide.shape[1] // (PER_GROUP * P_SIZE)
    at_group = lax.broadcasted_iota(jnp.int32, (1, G), 1) == first_group
    square = jnp.sum(jnp.square(wide), axis=1, keepdims=True)
    square = lax.psum(jnp.where(at_group, square, 0.0), "heads")
    square = jnp.sum(jnp.where(at_group, square, 0.0), axis=1, keepdims=True)
    scale = lax.rsqrt(square / (PER_GROUP * P_SIZE) + EPSILON)
    return (wide * scale * gain[None]).astype(jnp.bfloat16)


def exchange_states(states):
    head_devices, sections = lax.axis_size("heads"), lax.axis_size("seq")
    section, head_block = lax.axis_index("seq"), lax.axis_index("heads")
    mine = states.shape[2]
    sub = head_devices // sections
    rank = section * sub + head_block % sub
    pieces = []
    for d in range(head_devices):
        pairs = [
            (s * head_devices + k, (k // sub) * head_devices + (s * sub + k % sub + d) % head_devices)
            for s in range(sections)
            for k in range(head_devices)
        ]
        piece = lax.dynamic_index_in_dim(states, (rank + d) % head_devices, 0, False)
        pieces.append(lax.ppermute(piece, ("seq", "heads"), pairs))
    backward = jnp.stack(pieces[::-1] + pieces[::-1])
    by_rank = lax.dynamic_slice_in_dim(backward, head_devices - 1 - head_block, head_devices, 0)
    by_rank = by_rank.reshape(sections, sub, sections, mine, P_SIZE, N)
    return jnp.transpose(by_rank, (2, 1, 0, 3, 4, 5)).reshape(1, sections, sub * sections * mine, P_SIZE, N)


def solution(mesh):
    in_specs = (
        P(("groups", "seq"), "heads"),
        P(None, ("heads", "seq")),
        P(None, "heads"),
        P(None, "heads"),
        P("heads"),
        P("heads"),
        P("heads"),
        P(None, "heads"),
        P("heads"),
        P(),
        P(),
        P("heads"),
        P("groups"),
        P("groups"),
    )
    out_specs = (P(("groups", "seq"), "heads"), P(("groups", "heads"), None, "seq", None, None))
    return jax.shard_map(fast_shards, mesh=mesh, in_specs=in_specs, out_specs=out_specs, check_vma=False)
```

```python
import functools

import jax
import jax.numpy as jnp
from jax import lax
from jax.experimental import pallas as pl
from jax.experimental.pallas import tpu as pltpu
from jax.sharding import PartitionSpec as P

H = 256
P_SIZE = 64
N = 128
G = 8
CH = 256
PER_GROUP = H // G
EPSILON = 1e-05


def project(tokens, xz_weight, small_weight, chunks):
    sections, head_devices = lax.axis_size("seq"), lax.axis_size("heads")
    rows = tokens.shape[0] // chunks
    width = tokens.shape[1]
    pieces = [tokens[c * rows : (c + 1) * rows] for c in range(chunks)]
    xz, small = [], []
    for c in range(chunks):
        part = lax.all_gather(pieces[c], ("seq", "heads"), axis=0)
        part = part.reshape(sections, head_devices, rows, width)
        dot = lambda w: lax.dot_general(
            part,
            w.reshape(head_devices, width, w.shape[1]),
            (((1, 3), (0, 1)), ((), ())),
            preferred_element_type=jnp.float32,
        )
        xz.append(dot(xz_weight).astype(jnp.bfloat16))
        small.append(dot(small_weight))
        if c + 2 < chunks:
            pieces[c + 2], xz[c], small[c] = lax.optimization_barrier(
                (pieces[c + 2], xz[c], small[c])
            )
    whole = lambda parts: jnp.concatenate(parts, axis=1).reshape(-1, parts[0].shape[-1])
    return whole(xz), whole(small)


MESH = pl.DeviceIdType.MESH
SPAN = 2048


def nearest_first(z, k, count):
    h = jnp.int32(0)
    for at in range(count):
        order = sorted(range(count), key=lambda q: (abs(q - at), q))
        for i, q in enumerate(order):
            if q:
                h = h + jnp.where((z == at) & (k == i), q, 0)
    return h


def gather_project_kernel(
    pieces, tok, xw, bw, sw, xz_out, bc_out, st_out, every,
    wx, wb, ws, tile, ax, ab, ast, ox, ob, ost,
    recv, up_sem, down_sem, x_sem, c_sem, on_sem, w_sem, tile_sem, out_sem,
):
    f32, bf16 = jnp.float32, jnp.bfloat16
    s, z = lax.axis_index("seq"), lax.axis_index("heads")
    line = lax.axis_size("heads")
    other = (s + 2) % 4
    sib = s + 1 - 2 * (s % 2)
    far = (sib + 2) % 4
    rows_all, depth = tok.shape
    halves = pieces // 2
    rows = rows_all // halves
    strip = rows_all // pieces
    part = lambda p: pl.ds(pl.multiple_of(p * strip, strip), strip)
    half = lambda n: pl.ds(pl.multiple_of(n * rows, rows), rows)
    below, above = z > 0, z < line - 1

    barrier = pltpu.get_barrier_semaphore()
    for partner in (other, sib):
        pl.semaphore_signal(barrier, inc=1, device_id={"seq": partner}, device_id_type=MESH)

    @pl.when(above)
    def _():
        pl.semaphore_signal(barrier, inc=1, device_id={"heads": z + 1}, device_id_type=MESH)

    @pl.when(below)
    def _():
        pl.semaphore_signal(barrier, inc=1, device_id={"heads": z - 1}, device_id_type=MESH)

    pl.semaphore_wait(barrier, 2 + above.astype(jnp.int32) + below.astype(jnp.int32))

    def copy(src, sec, h, p, sem, to):
        return pltpu.make_async_remote_copy(
            src_ref=src, dst_ref=every.at[h, sec, part(p)], send_sem=sem, recv_sem=recv.at[sec, h, p],
            device_id=to, device_id_type=MESH,
        )

    held = lambda sec, h, p: every.at[h, sec, part(p)]
    go_up = lambda src, h, p: copy(src, s, h, p, up_sem.at[h, p], {"heads": z + 1})
    go_down = lambda src, h, p: copy(src, s, h, p, down_sem.at[h, p], {"heads": z - 1})
    go_x = lambda src, h, p: copy(src, s, h, p, x_sem.at[h, p], {"seq": other})
    go_c = lambda src, sec, i, h, p: copy(src, sec, h, p, c_sem.at[i, h, p], {"seq": sib})
    def by_line(h, p):
        return (p % 2 == 1) & (((h == line - 1) & (z != line - 1)) | ((h == 0) & (z != 0)))

    def go_on(end, n, p):
        return copy(held(other, end, p), other, end, p, on_sem.at[n, p], {"heads": z + 1 if end == 0 else z - 1})

    arrived = lambda sec, h, p: copy(held(sec, h, p), sec, h, p, x_sem.at[h, p], {"seq": other}).wait_recv()

    def weights(h, slot):
        src = pl.ds(pl.multiple_of(h * depth, depth), depth)
        return [
            pltpu.make_async_copy(xw.at[src], wx.at[slot], w_sem.at[slot, 0]),
            pltpu.make_async_copy(
                bw.at[src, pl.ds(pl.multiple_of((s // 2) * 2 * N, 2 * N), 2 * N)], wb.at[slot], w_sem.at[slot, 1]),
            pltpu.make_async_copy(sw.at[src], ws.at[slot], w_sem.at[slot, 2]),
        ]

    load = lambda src, b, n: pltpu.make_async_copy(src, tile.at[b, pl.ds(n * rows, rows)], tile_sem.at[b, n])

    def send_own(p):
        own = tok.at[part(p)]

        @pl.when(above)
        def _():
            go_up(own, z, p).start()

        @pl.when(below)
        def _():
            go_down(own, z, p).start()

        go_x(own, z, p).start()
        go_c(own, s, 0, z, p).start()

    for p in range(pieces):
        send_own(p)
    for k in range(2):
        for c in weights(nearest_first(z, k, line), k):
            c.start()

    ab[...] = jnp.zeros_like(ab)
    ast[...] = jnp.zeros_like(ast)

    def clear(i, carry):
        ax[i // 8, pl.ds(pl.multiple_of((i % 8) * (rows_all // 8), rows_all // 8), rows_all // 8), :] = jnp.zeros(
            (rows_all // 8, ax.shape[2]), f32)
        return carry

    lax.fori_loop(0, 4 * 8, clear, 0)

    wide = min(256, ax.shape[2])
    span = min(SPAN, ax.shape[2])

    def multiply(b, slot, pair, p):
        def add(acc, w, cols):
            both = jnp.dot(tile[b], w, preferred_element_type=f32)
            for n, sec in enumerate(pair):
                acc[sec, half(p), cols] += both[n * rows : (n + 1) * rows]

        def one(n, carry):
            cols = pl.ds(pl.multiple_of(n * span, span), span)
            add(ax, wx[slot, :, cols], cols)
            return carry

        lax.fori_loop(0, ax.shape[2] // span, one, 0)
        add(ab, wb[slot], slice(None))
        add(ast, ws[slot], slice(0, ws.shape[2]))

    mine = st_out.shape[0]
    eye = (
        lax.broadcasted_iota(jnp.int32, (wide, wide), 0) == lax.broadcasted_iota(jnp.int32, (wide, wide), 1)
    ).astype(bf16)

    def results(q, sec, p):
        at = pl.ds(pl.multiple_of(sec * rows_all + p * rows, rows), rows)
        return [
            pltpu.make_async_copy(ox.at[q], xz_out.at[:, at], out_sem.at[q, 0]),
            pltpu.make_async_copy(ob.at[q], bc_out.at[at], out_sem.at[q, 1]),
            pltpu.make_async_copy(
                ost.at[q, pl.ds(pl.multiple_of(s * mine, 8), mine)], st_out.at[:, at], out_sem.at[q, 2]),
        ]

    def finish(q, sec, p):
        def one(n, carry):
            cols = pl.ds(pl.multiple_of(n * wide, wide), wide)
            block = ax[sec, half(p), cols].astype(bf16)
            turned = lax.dot_general(eye, block, NT, preferred_element_type=f32)
            ox[q, cols, :] = turned.astype(bf16)
            return carry

        lax.fori_loop(0, ax.shape[2] // wide, one, 0, unroll=True)
        ob[q] = ab[sec, half(p), :].astype(bf16)
        ost[q] = jnp.transpose(ast[sec, half(p), :])
        for c in results(q, sec, p):
            c.start()

    def step(i, carry):
        u, n = i // halves, i % halves
        h_new = nearest_first(z, u, line)
        h_old = nearest_first(z, u - 1, line)
        new, old = u < line, u >= 1
        rows_of = lambda sec, h: every.at[h, sec, half(n)]

        def pass_on(p):
            for sign in (-1, 1):
                h = z + sign * u

                @pl.when((u >= 1) & (h >= 0) & (h < line))
                def _():
                    arrived(s, h, p)
                    src = held(s, h, p)
                    if sign < 0:
                        @pl.when(above)
                        def _():
                            go_up(src, h, p).start()
                    else:
                        @pl.when(below)
                        def _():
                            go_down(src, h, p).start()

                    @pl.when(jnp.logical_not(by_line(h, p)))
                    def _():
                        go_x(src, h, p).start()

                    go_c(src, s, 0, h, p).start()

            @pl.when(old & jnp.logical_not(by_line(h_old, p)))
            def _():
                arrived(other, h_old, p)
                go_c(held(other, h_old, p), other, 1, h_old, p).start()

            for end, at, on, sem in ((line - 1, line - z, below, 1), (0, z + 1, above, 0)):
                @pl.when((u == jnp.where(z == end, 1, at)) & (p % 2 == 1))
                def _():
                    @pl.when(z != end)
                    def _():
                        arrived(other, end, p)
                        go_c(held(other, end, p), other, 1, end, p).start()

                    @pl.when(on)
                    def _():
                        go_on(end, sem, p).start()

        def pass_two(m, carry):
            pass_on(2 * n + m)
            return carry

        lax.fori_loop(0, 2, pass_two, 0)

        @pl.when(u == 0)
        def _():
            load(tok.at[half(n)], 0, 0).start()

        @pl.when(new & old)
        def _():
            load(rows_of(s, h_new), 0, 0).start()

        @pl.when(old)
        def _():
            load(rows_of(other, h_old), 1, 0).start()

        @pl.when(new & (n == 0))
        def _():
            for c in weights(h_new, u % 2):
                c.wait()

        @pl.when(old)
        def _():
            for m in range(2):
                arrived(far, h_old, 2 * n + m)
            load(rows_of(far, h_old), 1, 1).start()

        @pl.when(new)
        def _():
            for m in range(2):
                arrived(sib, h_new, 2 * n + m)
            load(rows_of(sib, h_new), 0, 1).start()
            for m in range(2):
                load(rows_of(sib, h_new), 0, m).wait()
            multiply(0, u % 2, (s, sib), n)

        @pl.when(old)
        def _():
            for m in range(2):
                load(rows_of(far, h_old), 1, m).wait()
            multiply(1, (u - 1) % 2, (other, far), n)

        @pl.when(old & (u < line - 1) & (n == halves - 1))
        def _():
            for c in weights(nearest_first(z, u + 1, line), (u + 1) % 2):
                c.start()

        @pl.when(u >= line - 1)
        def _():
            last = u == line
            first_sec, second_sec = jnp.where(last, other, s), jnp.where(last, far, sib)

            def one(q, carry):
                sec = jnp.where(q == 0, first_sec, second_sec)

                @pl.when(i > (line - 1) * halves)
                def _():
                    for c in results(q, sec, n):
                        c.wait()

                finish(q, sec, n)
                return carry

            lax.fori_loop(0, 2, one, 0)

        return carry

    lax.fori_loop(0, (line + 1) * halves, step, 0)

    for q in range(2):
        for c in results(q, s, 0):
            c.wait()

    def drain(i, carry):
        h, p = i // pieces, i % pieces
        src = held(s, h, p)

        @pl.when(above & (h <= z))
        def _():
            go_up(src, h, p).wait_send()

        @pl.when(below & (h >= z))
        def _():
            go_down(src, h, p).wait_send()

        @pl.when(jnp.logical_not(by_line(h, p)))
        def _():
            go_x(src, h, p).wait_send()

        go_c(src, s, 0, h, p).wait_send()
        go_c(src, s, 1, h, p).wait_send()
        return carry

    lax.fori_loop(0, line * pieces, drain, 0)

    for p in range(1, pieces, 2):
        @pl.when(above)
        def _():
            go_on(0, 0, p).wait_send()

        @pl.when(below)
        def _():
            go_on(line - 1, 1, p).wait_send()


def gather_project(tokens, xz_weight, bc_weight, step_weight, mine):
    pieces = 4
    sections, line = lax.axis_size("seq"), lax.axis_size("heads")
    rows_all, depth = tokens.shape
    rows = rows_all // (pieces // 2)
    width = xz_weight.shape[1]
    steps = step_weight.shape[1]
    length = rows_all * sections
    f32, bf16 = jnp.float32, jnp.bfloat16
    hbm = pl.BlockSpec(memory_space=pl.ANY)
    dma = pltpu.SemaphoreType.DMA
    wide = min(256, width)
    flops = 2 * length * depth * line * (width + 2 * N + steps)
    return pl.pallas_call(
        functools.partial(gather_project_kernel, pieces),
        in_specs=[hbm] * 4,
        out_specs=[hbm] * 4,
        out_shape=[
            jax.ShapeDtypeStruct((width, length), bf16),
            jax.ShapeDtypeStruct((length, 2 * N), bf16),
            jax.ShapeDtypeStruct((mine, length), f32),
            jax.ShapeDtypeStruct((line, sections, rows_all, depth), bf16),
        ],
        scratch_shapes=[
            pltpu.VMEM((2, depth, width), bf16),
            pltpu.VMEM((2, depth, 2 * N), bf16),
            pltpu.VMEM((2, depth, steps), bf16),
            pltpu.VMEM((2, 2 * rows, depth), bf16),
            pltpu.VMEM((sections, rows_all, width), f32),
            pltpu.VMEM((sections, rows_all, 2 * N), f32),
            pltpu.VMEM((sections, rows_all, 128), f32),
            pltpu.VMEM((2, width, rows), bf16),
            pltpu.VMEM((2, rows, 2 * N), bf16),
            pltpu.VMEM((2, 128, rows), f32),
            dma((sections, line, pieces)),
            dma((line, pieces)),
            dma((line, pieces)),
            dma((line, pieces)),
            dma((2, line, pieces)),
            dma((2, pieces)),
            dma((2, 3)),
            dma((2, 2)),
            dma((2, 3)),
        ],
        compiler_params=pltpu.CompilerParams(
            collective_id=0, has_side_effects=True, vmem_limit_bytes=60 * 1024 * 1024),
        cost_estimate=pl.CostEstimate(flops=flops, bytes_accessed=100_000_000, transcendentals=0),
        name="gather_project",
    )(tokens, xz_weight, bc_weight, step_weight)[:3]


LOG2E = 1.4426950408889634
NT = (((1,), (1,)), ((), ()))


def sigmoid(x):
    return 0.5 * jnp.tanh(0.5 * x) + 0.5


def scan_states(
    j, n_read, bounds_ref, readers_ref, xz_ref, bc_ref, step_ref, conv_ref, head_ref, bconv_ref,
    tail, bpad, b_in, c_in, inner, start, cum, stp, wt, states, send,
):
    f32, bf16 = jnp.float32, jnp.bfloat16
    heads = head_ref.shape[0]
    sec = xz_ref.shape[1]
    n_blk = sec // CH
    first = j * n_blk
    taps = 4

    @pl.when(j == 0)
    def _():
        tail[...] = jnp.zeros_like(tail)
        bpad[0:8, :] = jnp.zeros((8, 2 * N), f32)
        start[0] = jnp.zeros(start.shape[1:], f32)

    bpad[8 : 8 + sec, :] = bc_ref[...].astype(f32)
    for i in range(n_blk):
        y = jnp.broadcast_to(bconv_ref[taps : taps + 1, :], (CH, 2 * N))
        for k in range(taps):
            y = y + bconv_ref[k : k + 1, :] * bpad[i * CH + 5 + k : i * CH + 5 + k + CH, :]
        y = (y * sigmoid(y)).astype(bf16)
        b_in[first + i] = y[:, :N]
        c_in[first + i] = y[:, N:]
    bpad[0:8, :] = bpad[sec : sec + 8, :]

    def conv_strip(i, carry):
        row = pl.multiple_of(i * 32, 32)
        src = pl.multiple_of((i // 2) * 128 + (i % 2) * 32, 32)
        raw = xz_ref[pl.ds(src, 32), :]
        both = jnp.concatenate([tail[pl.ds(row, 32), :], raw], axis=1).astype(f32)
        w = conv_ref[pl.ds(row, 32), :]
        y = w[:, 4:5] + w[:, 3:4] * both[:, 128:]
        for d in range(1, taps):
            y = y + w[:, 3 - d : 4 - d] * pltpu.roll(both, d, 1)[:, 128:]
        y = (y * sigmoid(y)).astype(bf16)
        for b in range(n_blk):
            inner[first + b, pl.ds(row, 32), :] = y[:, b * CH : (b + 1) * CH]
        tail[pl.ds(row, 32), :] = raw[:, sec - 128 :]
        return carry

    lax.fori_loop(0, heads * 2, conv_strip, 0, unroll=2)

    raw = step_ref[...] + head_ref[:, 0:1]
    size = jnp.maximum(raw, 0.0) + jnp.log1p(jnp.exp(-jnp.abs(raw)))
    total = (-LOG2E * jnp.exp(head_ref[:, 1:2])) * size
    lane = lax.broadcasted_iota(jnp.int32, (heads, sec), 1) % CH
    d = 1
    while d < CH:
        total = total + jnp.where(lane >= d, pltpu.roll(total, d, 1), 0.0)
        d *= 2
    for b in range(n_blk):
        cum[first + b] = total[:, b * CH : (b + 1) * CH]
        stp[first + b] = size[:, b * CH : (b + 1) * CH]

    def one_block(i, carry):
        b = first + i
        a = cum[b]
        last = a[:, CH - 1 : CH]
        w = jnp.exp2(last - a) * stp[b]
        keep = jnp.exp2(last)
        for h in range(heads):
            rows = slice(h * 64, (h + 1) * 64)
            wt[0, rows, :] = (inner[b, rows, :].astype(f32) * w[h : h + 1, :]).astype(bf16)
        added = jnp.dot(wt[0], b_in[b], preferred_element_type=f32)
        for h in range(heads):
            rows = slice(h * 64, (h + 1) * 64)
            start[b + 1, rows, :] = start[b, rows, :] * keep[h : h + 1, :] + added[rows, :]
        return carry

    lax.fori_loop(0, n_blk, one_block, 0)

    lane_b = lax.broadcasted_iota(jnp.int32, (heads, CH), 1)

    def one_bound(k, carry):
        r = (lax.axis_index("heads") + n_read // 2 + k) % n_read
        q = jnp.int32(0)
        for i in range(n_read):
            q = q + jnp.where(readers_ref[j * n_read + i] == r, bounds_ref[j * n_read + i], 0)
        b = q // CH
        off = q % CH
        a = cum[b]
        at = jnp.sum(jnp.where(lane_b == off, a, 0.0), axis=1, keepdims=True)
        w = jnp.where(lane_b <= off, jnp.exp2(jnp.minimum(at - a, 0.0)), 0.0) * stp[b]
        keep = jnp.exp2(at)
        slot = k % 2
        for h in range(heads):
            rows = slice(h * 64, (h + 1) * 64)
            wt[slot, rows, :] = (inner[b, rows, :].astype(f32) * w[h : h + 1, :]).astype(bf16)
        inside = jnp.dot(wt[slot], b_in[b], preferred_element_type=f32)
        for h in range(heads):
            rows = slice(h * 64, (h + 1) * 64)
            states[r, j, rows, :] = (start[b, rows, :] * keep[h : h + 1, :] + inside[rows, :]).astype(bf16)
        send(r)
        return carry

    lax.fori_loop(0, n_read, one_bound, 0)


def scan_outputs(j, xz_ref, head_ref, b_in, c_in, inner, start, cum, stp, scores, mix, outer, gated_t, gated):
    f32, bf16 = jnp.float32, jnp.bfloat16
    heads = head_ref.shape[0]
    n_blk = xz_ref.shape[1] // CH
    row_id = lax.broadcasted_iota(jnp.int32, (CH, CH), 0)
    col_id = lax.broadcasted_iota(jnp.int32, (CH, CH), 1)
    eye = (row_id == col_id).astype(bf16)

    @pl.when(j == 0)
    def _():
        mix[...] = jnp.zeros_like(mix)

    def one_block(i, carry):
        b = j * n_blk + i
        lanes = pl.ds(pl.multiple_of(i * CH, CH), CH)
        scores[...] = jnp.where(
            row_id <= col_id,
            lax.dot_general(b_in[b], c_in[b], NT, preferred_element_type=f32), 0.0)
        outer[...] = lax.dot_general(start[b].astype(bf16), c_in[b], NT, preferred_element_type=f32)
        a = cum[b]
        s = stp[b]
        a_col = jnp.transpose(jnp.concatenate([a, jnp.zeros((128 - heads, CH), f32)], axis=0))
        grow = jnp.exp2(a)
        for h in range(heads):
            rows = slice(h * 64, (h + 1) * 64)
            m = h % mix.shape[0]
            a_h = a[h : h + 1, :]
            for s0 in range(0, CH, 32):
                lo = (s0 // 128) * 128
                col = a_col[s0 : s0 + 32, h : h + 1]
                gap = jnp.minimum(a_h[:, lo:] - col, 0.0)
                mix[m, s0 : s0 + 32, lo:] = (jnp.exp2(gap) * scores[s0 : s0 + 32, lo:]).astype(bf16)
            x = inner[b, rows, :].astype(f32)
            intra = jnp.dot((x * s[h : h + 1, :]).astype(bf16), mix[m], preferred_element_type=f32)
            gate = xz_ref[h * 128 + 64 : (h + 1) * 128, lanes].astype(f32)
            ssd = intra + outer[rows, :] * grow[h : h + 1, :] + head_ref[h : h + 1, 2:3] * x
            gated_t[rows, :] = (ssd * (gate * sigmoid(gate))).astype(bf16)
        span = min(heads * 64, CH)
        for c in range(0, heads * 64, span):
            out = lax.dot_general(eye, gated_t[c : c + span, :], NT, preferred_element_type=f32)
            gated[j, lanes, c : c + span] = out.astype(bf16)
        return carry

    lax.fori_loop(0, n_blk, one_block, 0)


def scan_kernel(n_read, with_norm, *refs):
    bounds_ref, readers_ref, xz_ref, bc_ref, step_ref, conv_ref, head_ref, bconv_ref, gain_ref, result, handoff = refs[:11]
    (tail, bpad, b_in, c_in, inner, start, cum, stp, wt, states, scores, mix, outer, gated_t, gated,
     state_send, state_recv, state_here, gated_send, gated_recv, gated_here, out_sem) = refs[11:33]
    landing, normed = refs[33:] if with_norm else (result, None)
    sections, line = lax.axis_size("seq"), lax.axis_size("heads")
    s, z = lax.axis_index("seq"), lax.axis_index("heads")
    sub = line // sections
    i = pl.program_id(0)
    j = i % sections
    size = states.shape[2]
    to_sec = z // sub
    row = (z % sub) * sections + s

    def place(at, sec):
        return handoff.at[sec, pl.ds(pl.multiple_of(at * size, size), size)]

    def state_copy(r, sec):
        return pltpu.make_async_remote_copy(
            src_ref=states.at[r, sec], dst_ref=place(row, sec), send_sem=state_send.at[r, sec],
            recv_sem=state_recv.at[row, sec], device_id={"seq": to_sec, "heads": r}, device_id_type=MESH)

    def state_keep(sec):
        return pltpu.make_async_copy(states.at[z, sec], place(row, sec), state_here.at[sec])

    def gated_copy(sec, source):
        return pltpu.make_async_remote_copy(
            src_ref=gated.at[sec], dst_ref=landing.at[source], send_sem=gated_send.at[sec],
            recv_sem=gated_recv.at[source], device_id={"seq": sec}, device_id_type=MESH)

    gated_keep = lambda: pltpu.make_async_copy(gated.at[s], landing.at[s], gated_here.at[0])
    mine_too = to_sec == s

    @pl.when(i == 0)
    def _():
        barrier = pltpu.get_barrier_semaphore()
        for sec in range(sections):
            for k in range(sub):
                h = s * sub + k

                @pl.when((sec != s) | (h != z))
                def _():
                    pl.semaphore_signal(barrier, inc=1, device_id={"seq": sec, "heads": h}, device_id_type=MESH)

            @pl.when(sec != s)
            def _():
                pl.semaphore_signal(barrier, inc=1, device_id={"seq": sec}, device_id_type=MESH)

        pl.semaphore_wait(barrier, line + sections - 1 - mine_too.astype(jnp.int32))

    def send(r):
        @pl.when(mine_too & (r == z))
        def _():
            state_keep(j).start()

        @pl.when(jnp.logical_not(mine_too & (r == z)))
        def _():
            state_copy(r, j).start()

    @pl.when(i < sections)
    def _():
        scan_states(
            j, n_read, bounds_ref, readers_ref, xz_ref, bc_ref, step_ref, conv_ref, head_ref, bconv_ref,
            tail, bpad, b_in, c_in, inner, start, cum, stp, wt, states, send)

    @pl.when(i >= sections)
    def _():
        scan_outputs(j, xz_ref, head_ref, b_in, c_in, inner, start, cum, stp, scores, mix, outer, gated_t, gated)

        @pl.when(j == s)
        def _():
            gated_keep().start()

        @pl.when(j != s)
        def _():
            gated_copy(j, s).start()

    @pl.when(i == 2 * sections - 1)
    def _():
        gated_keep().wait()
        for sec in range(sections):
            @pl.when(sec != s)
            def _():
                gated_copy(sec, sec).wait_recv()

        if with_norm:
            norm_rows(landing, gain_ref, normed, result, out_sem)

        def drain(n, carry):
            r, sec = n // sections, n % sections

            @pl.when(jnp.logical_not(mine_too & (r == z)))
            def _():
                state_copy(r, sec).wait_send()

            return carry

        lax.fori_loop(0, n_read * sections, drain, 0)

        @pl.when(mine_too)
        def _():
            for sec in range(sections):
                state_keep(sec).wait()

        def arrive(n, carry):
            at, sec = n // sections, n % sections
            here = mine_too & (at == row)

            @pl.when(jnp.logical_not(here))
            def _():
                pltpu.make_async_remote_copy(
                    src_ref=states.at[0, sec], dst_ref=place(at, sec), send_sem=state_send.at[0, sec],
                    recv_sem=state_recv.at[at, sec], device_id={"seq": to_sec}, device_id_type=MESH).wait_recv()

            return carry

        lax.fori_loop(0, sub * sections * sections, arrive, 0)
        for sec in range(sections):
            @pl.when(sec != s)
            def _():
                gated_copy(sec, s).wait_send()


def norm_rows(x_ref, gain_ref, normed, result, out_sem):
    sources, rows_all, width = x_ref.shape
    per = (PER_GROUP * P_SIZE) // width
    tiles = out_sem.shape[0]
    tile = rows_all // tiles

    def one(t, carry):
        rows = pl.ds(pl.multiple_of(t * tile, tile), tile)
        for g in range(sources // per):
            square = jnp.zeros((tile, 1), jnp.float32)
            for n in range(per):
                p = x_ref[g * per + n, rows, :].astype(jnp.float32)
                square = square + jnp.sum(p * p, axis=1, keepdims=True)
            scale = lax.rsqrt(square / (PER_GROUP * P_SIZE) + EPSILON)
            for n in range(per):
                cols = slice((g * per + n) * width, (g * per + n + 1) * width)
                p = x_ref[g * per + n, rows, :].astype(jnp.float32)
                normed[rows, cols] = (p * scale * gain_ref[:, cols]).astype(jnp.bfloat16)
        pltpu.make_async_copy(normed.at[rows], result.at[rows], out_sem.at[t]).start()
        return carry

    lax.fori_loop(0, tiles, one, 0)

    def wait(t, carry):
        rows = pl.ds(pl.multiple_of(t * tile, tile), tile)
        pltpu.make_async_copy(normed.at[rows], result.at[rows], out_sem.at[t]).wait()
        return carry

    lax.fori_loop(0, tiles, wait, 0)


def scan_call(xz_t, bc_raw, step_t, conv_cols, head_cols, bconv, gain, bounds, readers):
    sections, line = lax.axis_size("seq"), lax.axis_size("heads")
    heads = head_cols.shape[0]
    length = xz_t.shape[1]
    sec = length // sections
    n_read = bounds.shape[0] // sections
    sub = line // sections
    n_blk, blocks = sec // CH, length // CH
    with_norm = sections * heads % PER_GROUP == 0
    f32, bf16 = jnp.float32, jnp.bfloat16
    dma = pltpu.SemaphoreType.DMA
    whole = lambda a: pl.BlockSpec(a.shape, lambda i: (0,) * a.ndim)
    smem = pl.BlockSpec(memory_space=pltpu.SMEM)
    hbm = pl.BlockSpec(memory_space=pl.ANY)
    width = heads * 64
    result = (sec, sections * width) if with_norm else (sections, sec, width)
    tiles = 16
    scratch = [
        pltpu.VMEM((width, 128), bf16),
        pltpu.VMEM((sec + 8, 2 * N), f32),
        pltpu.VMEM((blocks, CH, N), bf16),
        pltpu.VMEM((blocks, CH, N), bf16),
        pltpu.VMEM((blocks, width, CH), bf16),
        pltpu.VMEM((blocks + 1, width, N), f32),
        pltpu.VMEM((blocks, heads, CH), f32),
        pltpu.VMEM((blocks, heads, CH), f32),
        pltpu.VMEM((2, width, CH), bf16),
        pltpu.VMEM((n_read, sections, width, N), bf16),
        pltpu.VMEM((CH, CH), f32),
        pltpu.VMEM((4, CH, CH), bf16),
        pltpu.VMEM((width, CH), f32),
        pltpu.VMEM((width, CH), bf16),
        pltpu.VMEM((sections, sec, width), bf16),
        dma((n_read, sections)),
        dma((sub * sections, sections)),
        dma((sections,)),
        dma((sections,)),
        dma((sections,)),
        dma((1,)),
        dma((tiles,)),
    ]
    if with_norm:
        scratch += [pltpu.VMEM((sections, sec, width), bf16), pltpu.VMEM(result, bf16)]
    return pl.pallas_call(
        functools.partial(scan_kernel, n_read, with_norm),
        grid=(2 * sections,),
        in_specs=[
            smem,
            smem,
            pl.BlockSpec((heads * 128, sec), lambda i: (0, i % sections)),
            pl.BlockSpec((sec, 2 * N), lambda i: (jnp.minimum(i, sections - 1), 0)),
            pl.BlockSpec((heads, sec), lambda i: (0, jnp.minimum(i, sections - 1))),
            whole(conv_cols),
            whole(head_cols),
            whole(bconv),
            whole(gain),
        ],
        out_specs=[hbm, hbm],
        out_shape=[
            jax.ShapeDtypeStruct(result, bf16),
            jax.ShapeDtypeStruct((sections, sub * sections * width, N), bf16),
        ],
        scratch_shapes=scratch,
        compiler_params=pltpu.CompilerParams(
            collective_id=1, has_side_effects=True, vmem_limit_bytes=56 * 1024 * 1024),
        cost_estimate=pl.CostEstimate(flops=10_000_000_000, bytes_accessed=30_000_000, transcendentals=0),
        name="scan",
    )(bounds, readers, xz_t, bc_raw, step_t, conv_cols, head_cols, bconv, gain)


def fast_shards(
    tokens,
    xz_weight,
    bc_weight,
    step_weight,
    step_bias,
    decay_log,
    skip_gain,
    conv_weight,
    conv_bias,
    bc_conv_weight,
    bc_conv_bias,
    norm_gain,
    step_bounds,
    readers,
):
    head_devices = lax.axis_size("heads")
    sections = lax.axis_size("seq")
    section = lax.axis_index("seq")
    head_block = lax.axis_index("heads")
    block_heads = H // head_devices
    mine = block_heads // sections
    first_mine = section * mine
    group = (head_block * block_heads + first_mine) // PER_GROUP
    own = lambda a, width, axis: lax.dynamic_slice_in_dim(a, first_mine * width, mine * width, axis)
    conv_cols = jnp.transpose(
        jnp.concatenate([own(conv_weight, P_SIZE, 1), own(conv_bias, P_SIZE, 0)[None], jnp.zeros((3, mine * P_SIZE), jnp.float32)], axis=0)
    )
    head_cols = jnp.stack([own(a, 1, 0) for a in (step_bias, decay_log, skip_gain)], axis=1)
    pick = lambda a, axis: lax.dynamic_slice_in_dim(a, group * 2 * N, 2 * N, axis)
    bconv = jnp.concatenate([pick(bc_conv_weight, 1), pick(bc_conv_bias, 0)[None], jnp.zeros((3, 2 * N), jnp.float32)], axis=0)

    if head_devices == 4 and sections == 4:
        xz_t, bc_raw, step_t = gather_project(tokens, xz_weight, bc_weight, step_weight, mine)
    else:
        small_step = own(step_weight, 1, 1)
        xz_t, bc_raw, step_t = project_parts(tokens, xz_weight, bc_weight, small_step, group)

    result, handoff = scan_call(
        xz_t, bc_raw, step_t, conv_cols, head_cols, bconv, norm_gain[None], step_bounds, readers)
    handoff = handoff.reshape(1, sections, -1, P_SIZE, N)
    mixed = result if block_heads % PER_GROUP == 0 else norm_split(result, norm_gain)
    return (mixed, handoff)


def project_parts(tokens, xz_weight, bc_weight, step_weight, group):
    head_block = lax.axis_index("heads")
    width_bc = bc_weight.shape[1]
    whole_group = width_bc >= 2 * N
    if whole_group:
        bc_weight = lax.dynamic_slice_in_dim(bc_weight, group * 2 * N - head_block * width_bc, 2 * N, 1)
    bc_width = bc_weight.shape[1]
    xz, small = project(tokens, xz_weight, jnp.concatenate([bc_weight, step_weight], axis=1), 4)
    bc_raw = small[:, :bc_width].astype(jnp.bfloat16)
    if not whole_group:
        bc_raw = lax.all_gather(bc_raw, "heads", axis=1, tiled=True)
        bc_raw = lax.dynamic_slice_in_dim(bc_raw, group * 2 * N, 2 * N, 1)
    return jnp.transpose(xz), bc_raw, jnp.transpose(small[:, bc_width:])


def norm_split(gathered, gain):
    wide = jnp.moveaxis(gathered, 0, 1).reshape(gathered.shape[1], -1).astype(jnp.float32)
    first_group = lax.axis_index("heads") * wide.shape[1] // (PER_GROUP * P_SIZE)
    at_group = lax.broadcasted_iota(jnp.int32, (1, G), 1) == first_group
    square = jnp.sum(jnp.square(wide), axis=1, keepdims=True)
    square = lax.psum(jnp.where(at_group, square, 0.0), "heads")
    square = jnp.sum(jnp.where(at_group, square, 0.0), axis=1, keepdims=True)
    scale = lax.rsqrt(square / (PER_GROUP * P_SIZE) + EPSILON)
    return (wide * scale * gain[None]).astype(jnp.bfloat16)


def solution(mesh):
    in_specs = (
        P(("groups", "seq"), "heads"),
        P(None, ("heads", "seq")),
        P(None, "heads"),
        P(None, "heads"),
        P("heads"),
        P("heads"),
        P("heads"),
        P(None, "heads"),
        P("heads"),
        P(),
        P(),
        P("heads"),
        P("groups"),
        P("groups"),
    )
    out_specs = (P(("groups", "seq"), "heads"), P(("groups", "heads"), None, "seq", None, None))
    return jax.shard_map(fast_shards, mesh=mesh, in_specs=in_specs, out_specs=out_specs, check_vma=False)
```

```python
import functools

import jax
import jax.numpy as jnp
from jax import lax
from jax.experimental import pallas as pl
from jax.experimental.pallas import tpu as pltpu
from jax.sharding import PartitionSpec as P

H = 256
P_SIZE = 64
N = 128
G = 8
CH = 256
PER_GROUP = H // G
EPSILON = 1e-05


def project(tokens, xz_weight, small_weight, chunks):
    sections, head_devices = lax.axis_size("seq"), lax.axis_size("heads")
    rows = tokens.shape[0] // chunks
    width = tokens.shape[1]
    pieces = [tokens[c * rows : (c + 1) * rows] for c in range(chunks)]
    xz, small = [], []
    for c in range(chunks):
        part = lax.all_gather(pieces[c], ("seq", "heads"), axis=0)
        part = part.reshape(sections, head_devices, rows, width)
        dot = lambda w: lax.dot_general(
            part,
            w.reshape(head_devices, width, w.shape[1]),
            (((1, 3), (0, 1)), ((), ())),
            preferred_element_type=jnp.float32,
        )
        xz.append(dot(xz_weight).astype(jnp.bfloat16))
        small.append(dot(small_weight))
        if c + 2 < chunks:
            pieces[c + 2], xz[c], small[c] = lax.optimization_barrier(
                (pieces[c + 2], xz[c], small[c])
            )
    whole = lambda parts: jnp.concatenate(parts, axis=1).reshape(-1, parts[0].shape[-1])
    return whole(xz), whole(small)


MESH = pl.DeviceIdType.MESH
SPAN = 2048


def nearest_first(z, k, count):
    h = jnp.int32(0)
    for at in range(count):
        order = sorted(range(count), key=lambda q: (abs(q - at), min(q, count - 1 - q)))
        for i, q in enumerate(order):
            if q:
                h = h + jnp.where((z == at) & (k == i), q, 0)
    return h


def gather_project_kernel(
    pieces, tok, xw, bw, sw, xz_out, bc_out, st_out, every,
    wx, wb, ws, tile, ax, ab, ast, ox, ob, ost,
    recv, up_sem, down_sem, x_sem, c_sem, on_sem, w_sem, tile_sem, out_sem,
):
    f32, bf16 = jnp.float32, jnp.bfloat16
    s, z = lax.axis_index("seq"), lax.axis_index("heads")
    line = lax.axis_size("heads")
    other = (s + 2) % 4
    sib = s + 1 - 2 * (s % 2)
    far = (sib + 2) % 4
    rows_all, depth = tok.shape
    halves = pieces // 2
    rows = rows_all // halves
    strip = rows_all // pieces
    part = lambda p: pl.ds(pl.multiple_of(p * strip, strip), strip)
    half = lambda n: pl.ds(pl.multiple_of(n * rows, rows), rows)
    below, above = z > 0, z < line - 1

    barrier = pltpu.get_barrier_semaphore()
    for partner in (other, sib):
        pl.semaphore_signal(barrier, inc=1, device_id={"seq": partner}, device_id_type=MESH)

    @pl.when(above)
    def _():
        pl.semaphore_signal(barrier, inc=1, device_id={"heads": z + 1}, device_id_type=MESH)

    @pl.when(below)
    def _():
        pl.semaphore_signal(barrier, inc=1, device_id={"heads": z - 1}, device_id_type=MESH)

    pl.semaphore_wait(barrier, 2 + above.astype(jnp.int32) + below.astype(jnp.int32))

    def copy(src, sec, h, p, sem, to):
        return pltpu.make_async_remote_copy(
            src_ref=src, dst_ref=every.at[h, sec, part(p)], send_sem=sem, recv_sem=recv.at[sec, h, p],
            device_id=to, device_id_type=MESH,
        )

    held = lambda sec, h, p: every.at[h, sec, part(p)]
    go_up = lambda src, h, p: copy(src, s, h, p, up_sem.at[h, p], {"heads": z + 1})
    go_down = lambda src, h, p: copy(src, s, h, p, down_sem.at[h, p], {"heads": z - 1})
    go_x = lambda src, h, p: copy(src, s, h, p, x_sem.at[h, p], {"seq": other})
    go_c = lambda src, sec, i, h, p: copy(src, sec, h, p, c_sem.at[i, h, p], {"seq": sib})
    def by_line(h, p):
        return (p % 2 == 1) & (((h == line - 1) & (z != line - 1)) | ((h == 0) & (z != 0)))

    def go_on(end, n, p):
        return copy(held(other, end, p), other, end, p, on_sem.at[n, p], {"heads": z + 1 if end == 0 else z - 1})

    arrived = lambda sec, h, p: copy(held(sec, h, p), sec, h, p, x_sem.at[h, p], {"seq": other}).wait_recv()

    def weights(h, slot):
        src = pl.ds(pl.multiple_of(h * depth, depth), depth)
        return [
            pltpu.make_async_copy(xw.at[src], wx.at[slot], w_sem.at[slot, 0]),
            pltpu.make_async_copy(
                bw.at[src, pl.ds(pl.multiple_of((s // 2) * 2 * N, 2 * N), 2 * N)], wb.at[slot], w_sem.at[slot, 1]),
            pltpu.make_async_copy(sw.at[:, src], ws.at[slot], w_sem.at[slot, 2]),
        ]

    load = lambda src, b, n: pltpu.make_async_copy(src, tile.at[b, pl.ds(n * rows, rows)], tile_sem.at[b, n])

    def send_own(p):
        own = tok.at[part(p)]

        @pl.when(above)
        def _():
            go_up(own, z, p).start()

        @pl.when(below)
        def _():
            go_down(own, z, p).start()

        go_x(own, z, p).start()
        go_c(own, s, 0, z, p).start()

    for p in range(pieces):
        send_own(p)
    for k in range(2):
        for c in weights(nearest_first(z, k, line), k):
            c.start()

    ab[...] = jnp.zeros_like(ab)
    ast[...] = jnp.zeros_like(ast)

    def clear(i, carry):
        ax[i // 8, pl.ds(pl.multiple_of((i % 8) * (rows_all // 8), rows_all // 8), rows_all // 8), :] = jnp.zeros(
            (rows_all // 8, ax.shape[2]), f32)
        return carry

    lax.fori_loop(0, 4 * 8, clear, 0)

    wide = min(256, ax.shape[2])
    span = min(SPAN, ax.shape[2])

    def multiply(b, slot, pair, p):
        def add(acc, w, cols, turned=False):
            dims = NT if turned else (((1,), (0,)), ((), ()))
            both = lax.dot_general(tile[b], w, dims, preferred_element_type=f32)
            for n, sec in enumerate(pair):
                acc[sec, half(p), cols] += both[n * rows : (n + 1) * rows]

        def one(n, carry):
            cols = pl.ds(pl.multiple_of(n * span, span), span)
            add(ax, wx[slot, :, cols], cols)
            return carry

        lax.fori_loop(0, ax.shape[2] // span, one, 0)
        add(ab, wb[slot], slice(None))
        add(ast, ws[slot], slice(0, ws.shape[1]), True)

    mine = st_out.shape[0]
    eye = (
        lax.broadcasted_iota(jnp.int32, (wide, wide), 0) == lax.broadcasted_iota(jnp.int32, (wide, wide), 1)
    ).astype(bf16)

    def results(q, sec, p):
        at = pl.ds(pl.multiple_of(sec * rows_all + p * rows, rows), rows)
        return [
            pltpu.make_async_copy(ox.at[q], xz_out.at[:, at], out_sem.at[q, 0]),
            pltpu.make_async_copy(ob.at[q], bc_out.at[at], out_sem.at[q, 1]),
            pltpu.make_async_copy(
                ost.at[q, pl.ds(pl.multiple_of(s * mine, 8), mine)], st_out.at[:, at], out_sem.at[q, 2]),
        ]

    def finish(q, sec, p):
        def one(n, carry):
            cols = pl.ds(pl.multiple_of(n * wide, wide), wide)
            block = ax[sec, half(p), cols].astype(bf16)
            turned = lax.dot_general(eye, block, NT, preferred_element_type=f32)
            ox[q, cols, :] = turned.astype(bf16)
            return carry

        lax.fori_loop(0, ax.shape[2] // wide, one, 0, unroll=True)
        ob[q] = ab[sec, half(p), :].astype(bf16)
        ost[q] = jnp.transpose(ast[sec, half(p), :])
        for c in results(q, sec, p):
            c.start()

    def step(i, carry):
        u, n = i // halves, i % halves
        h_new = nearest_first(z, u, line)
        h_old = nearest_first(z, u - 1, line)
        new, old = u < line, u >= 1
        rows_of = lambda sec, h: every.at[h, sec, half(n)]

        def pass_on(p):
            for turn in (1, -1):
                sign = turn * jnp.where(2 * z < line, -1, 1)
                h = z + sign * u

                @pl.when((u >= 1) & (h >= 0) & (h < line))
                def _():
                    arrived(s, h, p)
                    src = held(s, h, p)

                    @pl.when((sign < 0) & above)
                    def _():
                        go_up(src, h, p).start()

                    @pl.when((sign > 0) & below)
                    def _():
                        go_down(src, h, p).start()

                    @pl.when(jnp.logical_not(by_line(h, p)))
                    def _():
                        go_x(src, h, p).start()

                    go_c(src, s, 0, h, p).start()

            @pl.when(old & jnp.logical_not(by_line(h_old, p)))
            def _():
                arrived(other, h_old, p)
                go_c(held(other, h_old, p), other, 1, h_old, p).start()

            for end, at, on, sem in ((line - 1, line - z, below, 1), (0, z + 1, above, 0)):
                @pl.when((u == jnp.where(z == end, 1, at)) & (p % 2 == 1))
                def _():
                    @pl.when(z != end)
                    def _():
                        arrived(other, end, p)
                        go_c(held(other, end, p), other, 1, end, p).start()

                    @pl.when(on)
                    def _():
                        go_on(end, sem, p).start()

        def pass_two(m, carry):
            pass_on(2 * n + m)
            return carry

        lax.fori_loop(0, 2, pass_two, 0)

        @pl.when(u == 0)
        def _():
            load(tok.at[half(n)], 0, 0).start()

        @pl.when(new & old)
        def _():
            load(rows_of(s, h_new), 0, 0).start()

        @pl.when(old)
        def _():
            load(rows_of(other, h_old), 1, 0).start()

        @pl.when(new & (n == 0))
        def _():
            for c in weights(h_new, u % 2):
                c.wait()

        @pl.when(old)
        def _():
            for m in range(2):
                arrived(far, h_old, 2 * n + m)
            load(rows_of(far, h_old), 1, 1).start()

        @pl.when(new)
        def _():
            for m in range(2):
                arrived(sib, h_new, 2 * n + m)
            load(rows_of(sib, h_new), 0, 1).start()
            for m in range(2):
                load(rows_of(sib, h_new), 0, m).wait()
            multiply(0, u % 2, (s, sib), n)

        @pl.when(old)
        def _():
            for m in range(2):
                load(rows_of(far, h_old), 1, m).wait()
            multiply(1, (u - 1) % 2, (other, far), n)

        @pl.when(old & (u < line - 1) & (n == halves - 1))
        def _():
            for c in weights(nearest_first(z, u + 1, line), (u + 1) % 2):
                c.start()

        @pl.when(u >= line - 1)
        def _():
            last = u == line
            first_sec, second_sec = jnp.where(last, other, s), jnp.where(last, far, sib)

            def one(q, carry):
                sec = jnp.where(q == 0, first_sec, second_sec)

                @pl.when(i > (line - 1) * halves)
                def _():
                    for c in results(q, sec, n):
                        c.wait()

                finish(q, sec, n)
                return carry

            lax.fori_loop(0, 2, one, 0)

        return carry

    lax.fori_loop(0, (line + 1) * halves, step, 0)

    for q in range(2):
        for c in results(q, s, 0):
            c.wait()

    def drain(i, carry):
        h, p = i // pieces, i % pieces
        src = held(s, h, p)

        @pl.when(above & (h <= z))
        def _():
            go_up(src, h, p).wait_send()

        @pl.when(below & (h >= z))
        def _():
            go_down(src, h, p).wait_send()

        @pl.when(jnp.logical_not(by_line(h, p)))
        def _():
            go_x(src, h, p).wait_send()

        go_c(src, s, 0, h, p).wait_send()
        go_c(src, s, 1, h, p).wait_send()
        return carry

    lax.fori_loop(0, line * pieces, drain, 0)

    for p in range(1, pieces, 2):
        @pl.when(above)
        def _():
            go_on(0, 0, p).wait_send()

        @pl.when(below)
        def _():
            go_on(line - 1, 1, p).wait_send()


def gather_project(tokens, xz_weight, bc_weight, step_weight, mine):
    pieces = 4
    sections, line = lax.axis_size("seq"), lax.axis_size("heads")
    rows_all, depth = tokens.shape
    rows = rows_all // (pieces // 2)
    width = xz_weight.shape[1]
    steps = step_weight.shape[1]
    length = rows_all * sections
    f32, bf16 = jnp.float32, jnp.bfloat16
    hbm = pl.BlockSpec(memory_space=pl.ANY)
    dma = pltpu.SemaphoreType.DMA
    wide = min(256, width)
    flops = 2 * length * depth * line * (width + 2 * N + steps)
    return pl.pallas_call(
        functools.partial(gather_project_kernel, pieces),
        in_specs=[hbm] * 4,
        out_specs=[hbm] * 4,
        out_shape=[
            jax.ShapeDtypeStruct((width, length), bf16),
            jax.ShapeDtypeStruct((length, 2 * N), bf16),
            jax.ShapeDtypeStruct((mine, length), f32),
            jax.ShapeDtypeStruct((line, sections, rows_all, depth), bf16),
        ],
        scratch_shapes=[
            pltpu.VMEM((2, depth, width), bf16),
            pltpu.VMEM((2, depth, 2 * N), bf16),
            pltpu.VMEM((2, steps, depth), bf16),
            pltpu.VMEM((2, 2 * rows, depth), bf16),
            pltpu.VMEM((sections, rows_all, width), f32),
            pltpu.VMEM((sections, rows_all, 2 * N), f32),
            pltpu.VMEM((sections, rows_all, 128), f32),
            pltpu.VMEM((2, width, rows), bf16),
            pltpu.VMEM((2, rows, 2 * N), bf16),
            pltpu.VMEM((2, 128, rows), f32),
            dma((sections, line, pieces)),
            dma((line, pieces)),
            dma((line, pieces)),
            dma((line, pieces)),
            dma((2, line, pieces)),
            dma((2, pieces)),
            dma((2, 3)),
            dma((2, 2)),
            dma((2, 3)),
        ],
        compiler_params=pltpu.CompilerParams(
            collective_id=0, has_side_effects=True, vmem_limit_bytes=60 * 1024 * 1024),
        cost_estimate=pl.CostEstimate(flops=flops, bytes_accessed=100_000_000, transcendentals=0),
        name="gather_project",
    )(tokens, xz_weight, bc_weight, jnp.transpose(step_weight))[:3]


LOG2E = 1.4426950408889634
NT = (((1,), (1,)), ((), ()))


def sigmoid(x):
    return 0.5 * jnp.tanh(0.5 * x) + 0.5


def scan_states(
    j, n_read, bounds_ref, readers_ref, xz_ref, bc_ref, step_ref, conv_ref, head_ref, bconv_ref,
    tail, bpad, b_in, c_in, inner, start, cum, stp, wt, states, send,
):
    f32, bf16 = jnp.float32, jnp.bfloat16
    heads = head_ref.shape[0]
    sec = xz_ref.shape[1]
    n_blk = sec // CH
    first = j * n_blk
    taps = 4

    @pl.when(j == 0)
    def _():
        tail[...] = jnp.zeros_like(tail)
        bpad[0:8, :] = jnp.zeros((8, 2 * N), f32)
        start[0] = jnp.zeros(start.shape[1:], f32)

    bpad[8 : 8 + sec, :] = bc_ref[...].astype(f32)
    for i in range(n_blk):
        y = jnp.broadcast_to(bconv_ref[taps : taps + 1, :], (CH, 2 * N))
        for k in range(taps):
            y = y + bconv_ref[k : k + 1, :] * bpad[i * CH + 5 + k : i * CH + 5 + k + CH, :]
        y = (y * sigmoid(y)).astype(bf16)
        b_in[first + i] = y[:, :N]
        c_in[first + i] = y[:, N:]
    bpad[0:8, :] = bpad[sec : sec + 8, :]

    def conv_strip(i, carry):
        row = pl.multiple_of(i * 32, 32)
        src = pl.multiple_of((i // 2) * 128 + (i % 2) * 32, 32)
        raw = xz_ref[pl.ds(src, 32), :]
        both = jnp.concatenate([tail[pl.ds(row, 32), :], raw], axis=1).astype(f32)
        w = conv_ref[pl.ds(row, 32), :]
        y = w[:, 4:5] + w[:, 3:4] * both[:, 128:]
        for d in range(1, taps):
            y = y + w[:, 3 - d : 4 - d] * pltpu.roll(both, d, 1)[:, 128:]
        y = (y * sigmoid(y)).astype(bf16)
        for b in range(n_blk):
            inner[first + b, pl.ds(row, 32), :] = y[:, b * CH : (b + 1) * CH]
        tail[pl.ds(row, 32), :] = raw[:, sec - 128 :]
        return carry

    lax.fori_loop(0, heads * 2, conv_strip, 0, unroll=2)

    raw = step_ref[...] + head_ref[:, 0:1]
    size = jnp.maximum(raw, 0.0) + jnp.log1p(jnp.exp(-jnp.abs(raw)))
    total = (-LOG2E * jnp.exp(head_ref[:, 1:2])) * size
    lane = lax.broadcasted_iota(jnp.int32, (heads, sec), 1) % CH
    d = 1
    while d < CH:
        total = total + jnp.where(lane >= d, pltpu.roll(total, d, 1), 0.0)
        d *= 2
    for b in range(n_blk):
        cum[first + b] = total[:, b * CH : (b + 1) * CH]
        stp[first + b] = size[:, b * CH : (b + 1) * CH]

    def one_block(i, carry):
        b = first + i
        a = cum[b]
        last = a[:, CH - 1 : CH]
        w = jnp.exp2(last - a) * stp[b]
        keep = jnp.exp2(last)
        for h in range(heads):
            rows = slice(h * 64, (h + 1) * 64)
            wt[0, rows, :] = (inner[b, rows, :].astype(f32) * w[h : h + 1, :]).astype(bf16)
        added = jnp.dot(wt[0], b_in[b], preferred_element_type=f32)
        for h in range(heads):
            rows = slice(h * 64, (h + 1) * 64)
            start[b + 1, rows, :] = start[b, rows, :] * keep[h : h + 1, :] + added[rows, :]
        return carry

    lax.fori_loop(0, n_blk, one_block, 0)

    lane_b = lax.broadcasted_iota(jnp.int32, (heads, CH), 1)

    def one_bound(k, carry):
        r = (lax.axis_index("heads") + n_read // 2 + k) % n_read
        q = jnp.int32(0)
        for i in range(n_read):
            q = q + jnp.where(readers_ref[j * n_read + i] == r, bounds_ref[j * n_read + i], 0)
        b = q // CH
        off = q % CH
        a = cum[b]
        at = jnp.sum(jnp.where(lane_b == off, a, 0.0), axis=1, keepdims=True)
        w = jnp.where(lane_b <= off, jnp.exp2(jnp.minimum(at - a, 0.0)), 0.0) * stp[b]
        keep = jnp.exp2(at)
        slot = k % 2
        for h in range(heads):
            rows = slice(h * 64, (h + 1) * 64)
            wt[slot, rows, :] = (inner[b, rows, :].astype(f32) * w[h : h + 1, :]).astype(bf16)
        inside = jnp.dot(wt[slot], b_in[b], preferred_element_type=f32)
        for h in range(heads):
            rows = slice(h * 64, (h + 1) * 64)
            states[r, j, rows, :] = (start[b, rows, :] * keep[h : h + 1, :] + inside[rows, :]).astype(bf16)
        send(r)
        return carry

    lax.fori_loop(0, n_read, one_bound, 0)


def scan_outputs(j, xz_ref, head_ref, b_in, c_in, inner, start, cum, stp, scores, mix, outer, gated_t, gated):
    f32, bf16 = jnp.float32, jnp.bfloat16
    heads = head_ref.shape[0]
    n_blk = xz_ref.shape[1] // CH
    row_id = lax.broadcasted_iota(jnp.int32, (CH, CH), 0)
    col_id = lax.broadcasted_iota(jnp.int32, (CH, CH), 1)
    eye = (row_id == col_id).astype(bf16)

    @pl.when(j == 0)
    def _():
        mix[...] = jnp.zeros_like(mix)

    def one_block(i, carry):
        b = j * n_blk + i
        lanes = pl.ds(pl.multiple_of(i * CH, CH), CH)
        scores[...] = jnp.where(
            row_id <= col_id,
            lax.dot_general(b_in[b], c_in[b], NT, preferred_element_type=f32), 0.0)
        outer[...] = lax.dot_general(start[b].astype(bf16), c_in[b], NT, preferred_element_type=f32)
        a = cum[b]
        s = stp[b]
        a_col = jnp.transpose(jnp.concatenate([a, jnp.zeros((128 - heads, CH), f32)], axis=0))
        grow = jnp.exp2(a)
        for h in range(heads):
            rows = slice(h * 64, (h + 1) * 64)
            m = h % mix.shape[0]
            a_h = a[h : h + 1, :]
            for s0 in range(0, CH, 32):
                lo = (s0 // 128) * 128
                col = a_col[s0 : s0 + 32, h : h + 1]
                gap = jnp.minimum(a_h[:, lo:] - col, 0.0)
                mix[m, s0 : s0 + 32, lo:] = (jnp.exp2(gap) * scores[s0 : s0 + 32, lo:]).astype(bf16)
            x = inner[b, rows, :].astype(f32)
            intra = jnp.dot((x * s[h : h + 1, :]).astype(bf16), mix[m], preferred_element_type=f32)
            gate = xz_ref[h * 128 + 64 : (h + 1) * 128, lanes].astype(f32)
            ssd = intra + outer[rows, :] * grow[h : h + 1, :] + head_ref[h : h + 1, 2:3] * x
            gated_t[rows, :] = (ssd * (gate * sigmoid(gate))).astype(bf16)
        span = min(heads * 64, CH)
        for c in range(0, heads * 64, span):
            out = lax.dot_general(eye, gated_t[c : c + span, :], NT, preferred_element_type=f32)
            gated[j, lanes, c : c + span] = out.astype(bf16)
        return carry

    lax.fori_loop(0, n_blk, one_block, 0)


def scan_kernel(n_read, with_norm, *refs):
    (bounds_ref, readers_ref, xz_ref, bc_ref, step_ref, conv_ref, conv_bias_ref, head_ref, bconv_ref, bconv_bias_ref, gain_ref,
     result, handoff) = refs[:13]
    (tail, bpad, b_in, c_in, inner, start, cum, stp, wt, states, scores, mix, outer, gated_t, gated,
     state_send, state_recv, state_here, gated_send, gated_recv, gated_here, out_sem, conv_cols, head_cols, bconv) = refs[13:38]
    landing, normed = refs[38:] if with_norm else (result, None)
    sections, line = lax.axis_size("seq"), lax.axis_size("heads")
    s, z = lax.axis_index("seq"), lax.axis_index("heads")
    sub = line // sections
    j = pl.program_id(0)
    size = states.shape[2]
    to_sec = z // sub
    row = (z % sub) * sections + s

    def prepare():
        heads = head_cols.shape[0]
        taps, width = 4, heads * 64
        cols = pl.ds(pl.multiple_of(s * width, 128), width)
        stack = jnp.concatenate(
            [conv_ref[:, cols], conv_bias_ref[:, cols], jnp.zeros((123, width), jnp.float32)], axis=0)
        conv_cols[...] = jnp.transpose(stack)
        turned = jnp.transpose(head_ref[...])
        head_cols[...] = pltpu.roll(turned, (128 - s * heads) % 128, 0)[0:heads, :]
        group = (z * heads * sections + s * heads) // PER_GROUP
        lanes = pl.ds(pl.multiple_of(group * 2 * N, 2 * N), 2 * N)
        bconv[0:taps, :] = bconv_ref[:, lanes]
        bconv[taps : taps + 1, :] = bconv_bias_ref[:, lanes]

    def place(at, sec):
        return handoff.at[sec, pl.ds(pl.multiple_of(at * size, size), size)]

    def state_copy(r, sec):
        return pltpu.make_async_remote_copy(
            src_ref=states.at[r, sec], dst_ref=place(row, sec), send_sem=state_send.at[r, sec],
            recv_sem=state_recv.at[row, sec], device_id={"seq": to_sec, "heads": r}, device_id_type=MESH)

    def state_keep(sec):
        return pltpu.make_async_copy(states.at[z, sec], place(row, sec), state_here.at[sec])

    def gated_copy(sec, source):
        return pltpu.make_async_remote_copy(
            src_ref=gated.at[sec], dst_ref=landing.at[source], send_sem=gated_send.at[sec],
            recv_sem=gated_recv.at[source], device_id={"seq": sec}, device_id_type=MESH)

    gated_keep = lambda: pltpu.make_async_copy(gated.at[s], landing.at[s], gated_here.at[0])
    mine_too = to_sec == s

    @pl.when(j == 0)
    def _():
        prepare()
        barrier = pltpu.get_barrier_semaphore()
        for sec in range(sections):
            for k in range(sub):
                h = s * sub + k

                @pl.when((sec != s) | (h != z))
                def _():
                    pl.semaphore_signal(barrier, inc=1, device_id={"seq": sec, "heads": h}, device_id_type=MESH)

            @pl.when(sec != s)
            def _():
                pl.semaphore_signal(barrier, inc=1, device_id={"seq": sec}, device_id_type=MESH)

        pl.semaphore_wait(barrier, line + sections - 1 - mine_too.astype(jnp.int32))

    def send(r):
        @pl.when(mine_too & (r == z))
        def _():
            state_keep(j).start()

        @pl.when(jnp.logical_not(mine_too & (r == z)))
        def _():
            state_copy(r, j).start()

    scan_states(
        j, n_read, bounds_ref, readers_ref, xz_ref, bc_ref, step_ref, conv_cols, head_cols, bconv,
        tail, bpad, b_in, c_in, inner, start, cum, stp, wt, states, send)
    scan_outputs(j, xz_ref, head_cols, b_in, c_in, inner, start, cum, stp, scores, mix, outer, gated_t, gated)

    @pl.when(j == s)
    def _():
        gated_keep().start()

    @pl.when(j != s)
    def _():
        gated_copy(j, s).start()

    @pl.when(j == sections - 1)
    def _():
        gated_keep().wait()
        for sec in range(sections):
            @pl.when(sec != s)
            def _():
                gated_copy(sec, sec).wait_recv()

        if with_norm:
            norm_rows(landing, gain_ref, normed, result, out_sem)

        def drain(n, carry):
            r, sec = n // sections, n % sections

            @pl.when(jnp.logical_not(mine_too & (r == z)))
            def _():
                state_copy(r, sec).wait_send()

            return carry

        lax.fori_loop(0, n_read * sections, drain, 0)

        @pl.when(mine_too)
        def _():
            for sec in range(sections):
                state_keep(sec).wait()

        def arrive(n, carry):
            at, sec = n // sections, n % sections
            here = mine_too & (at == row)

            @pl.when(jnp.logical_not(here))
            def _():
                pltpu.make_async_remote_copy(
                    src_ref=states.at[0, sec], dst_ref=place(at, sec), send_sem=state_send.at[0, sec],
                    recv_sem=state_recv.at[at, sec], device_id={"seq": to_sec}, device_id_type=MESH).wait_recv()

            return carry

        lax.fori_loop(0, sub * sections * sections, arrive, 0)
        for sec in range(sections):
            @pl.when(sec != s)
            def _():
                gated_copy(sec, s).wait_send()


def norm_rows(x_ref, gain_ref, normed, result, out_sem):
    sources, rows_all, width = x_ref.shape
    per = (PER_GROUP * P_SIZE) // width
    tiles = out_sem.shape[0]
    tile = rows_all // tiles

    def one(t, carry):
        rows = pl.ds(pl.multiple_of(t * tile, tile), tile)
        for g in range(sources // per):
            square = jnp.zeros((tile, 1), jnp.float32)
            for n in range(per):
                p = x_ref[g * per + n, rows, :].astype(jnp.float32)
                square = square + jnp.sum(p * p, axis=1, keepdims=True)
            scale = lax.rsqrt(square / (PER_GROUP * P_SIZE) + EPSILON)
            for n in range(per):
                cols = slice((g * per + n) * width, (g * per + n + 1) * width)
                p = x_ref[g * per + n, rows, :].astype(jnp.float32)
                normed[rows, cols] = (p * scale * gain_ref[:, cols]).astype(jnp.bfloat16)
        pltpu.make_async_copy(normed.at[rows], result.at[rows], out_sem.at[t]).start()
        return carry

    lax.fori_loop(0, tiles, one, 0)

    def wait(t, carry):
        rows = pl.ds(pl.multiple_of(t * tile, tile), tile)
        pltpu.make_async_copy(normed.at[rows], result.at[rows], out_sem.at[t]).wait()
        return carry

    lax.fori_loop(0, tiles, wait, 0)


def scan_call(xz_t, bc_raw, step_t, conv, conv_bias, head_rows, bconv, bconv_bias, gain, bounds, readers):
    sections, line = lax.axis_size("seq"), lax.axis_size("heads")
    heads = step_t.shape[0]
    length = xz_t.shape[1]
    sec = length // sections
    n_read = bounds.shape[0] // sections
    sub = line // sections
    n_blk, blocks = sec // CH, length // CH
    with_norm = sections * heads % PER_GROUP == 0
    f32, bf16 = jnp.float32, jnp.bfloat16
    dma = pltpu.SemaphoreType.DMA
    whole = lambda a: pl.BlockSpec(a.shape, lambda i: (0,) * a.ndim)
    smem = pl.BlockSpec(memory_space=pltpu.SMEM)
    hbm = pl.BlockSpec(memory_space=pl.ANY)
    width = heads * 64
    result = (sec, sections * width) if with_norm else (sections, sec, width)
    tiles = 16
    scratch = [
        pltpu.VMEM((width, 128), bf16),
        pltpu.VMEM((sec + 8, 2 * N), f32),
        pltpu.VMEM((blocks, CH, N), bf16),
        pltpu.VMEM((blocks, CH, N), bf16),
        pltpu.VMEM((blocks, width, CH), bf16),
        pltpu.VMEM((blocks + 1, width, N), f32),
        pltpu.VMEM((blocks, heads, CH), f32),
        pltpu.VMEM((blocks, heads, CH), f32),
        pltpu.VMEM((2, width, CH), bf16),
        pltpu.VMEM((n_read, sections, width, N), bf16),
        pltpu.VMEM((CH, CH), f32),
        pltpu.VMEM((4, CH, CH), bf16),
        pltpu.VMEM((width, CH), f32),
        pltpu.VMEM((width, CH), bf16),
        pltpu.VMEM((sections, sec, width), bf16),
        dma((n_read, sections)),
        dma((sub * sections, sections)),
        dma((sections,)),
        dma((sections,)),
        dma((sections,)),
        dma((1,)),
        dma((tiles,)),
        pltpu.VMEM((width, 128), f32),
        pltpu.VMEM((heads, 128), f32),
        pltpu.VMEM((8, 2 * N), f32),
    ]
    if with_norm:
        scratch += [pltpu.VMEM((sections, sec, width), bf16), pltpu.VMEM(result, bf16)]
    return pl.pallas_call(
        functools.partial(scan_kernel, n_read, with_norm),
        grid=(sections,),
        in_specs=[
            smem,
            smem,
            pl.BlockSpec((heads * 128, sec), lambda i: (0, i)),
            pl.BlockSpec((sec, 2 * N), lambda i: (i, 0)),
            pl.BlockSpec((heads, sec), lambda i: (0, i)),
            whole(conv),
            whole(conv_bias),
            whole(head_rows),
            whole(bconv),
            whole(bconv_bias),
            whole(gain),
        ],
        out_specs=[hbm, hbm],
        out_shape=[
            jax.ShapeDtypeStruct(result, bf16),
            jax.ShapeDtypeStruct((sections, sub * sections * width, N), bf16),
        ],
        scratch_shapes=scratch,
        compiler_params=pltpu.CompilerParams(
            collective_id=1, has_side_effects=True, vmem_limit_bytes=56 * 1024 * 1024),
        cost_estimate=pl.CostEstimate(flops=10_000_000_000, bytes_accessed=30_000_000, transcendentals=0),
        name="scan",
    )(bounds, readers, xz_t, bc_raw, step_t, conv, conv_bias, head_rows, bconv, bconv_bias, gain)


def fast_shards(
    tokens,
    xz_weight,
    bc_weight,
    step_weight,
    step_bias,
    decay_log,
    skip_gain,
    conv_weight,
    conv_bias,
    bc_conv_weight,
    bc_conv_bias,
    norm_gain,
    step_bounds,
    readers,
):
    head_devices = lax.axis_size("heads")
    sections = lax.axis_size("seq")
    section = lax.axis_index("seq")
    head_block = lax.axis_index("heads")
    block_heads = H // head_devices
    mine = block_heads // sections
    first_mine = section * mine
    group = (head_block * block_heads + first_mine) // PER_GROUP
    own = lambda a, width, axis: lax.dynamic_slice_in_dim(a, first_mine * width, mine * width, axis)
    head_rows = jnp.pad(jnp.stack([step_bias, decay_log, skip_gain]), ((0, 125), (0, 128 - block_heads)))

    if head_devices == 4 and sections == 4:
        xz_t, bc_raw, step_t = gather_project(tokens, xz_weight, bc_weight, step_weight, mine)
    else:
        small_step = own(step_weight, 1, 1)
        xz_t, bc_raw, step_t = project_parts(tokens, xz_weight, bc_weight, small_step, group)

    result, handoff = scan_call(
        xz_t, bc_raw, step_t, conv_weight, conv_bias[None], head_rows, bc_conv_weight, bc_conv_bias[None],
        norm_gain[None], step_bounds, readers)
    handoff = handoff.reshape(1, sections, -1, P_SIZE, N)
    mixed = result if block_heads % PER_GROUP == 0 else norm_split(result, norm_gain)
    return (mixed, handoff)


def project_parts(tokens, xz_weight, bc_weight, step_weight, group):
    head_block = lax.axis_index("heads")
    width_bc = bc_weight.shape[1]
    whole_group = width_bc >= 2 * N
    if whole_group:
        bc_weight = lax.dynamic_slice_in_dim(bc_weight, group * 2 * N - head_block * width_bc, 2 * N, 1)
    bc_width = bc_weight.shape[1]
    xz, small = project(tokens, xz_weight, jnp.concatenate([bc_weight, step_weight], axis=1), 4)
    bc_raw = small[:, :bc_width].astype(jnp.bfloat16)
    if not whole_group:
        bc_raw = lax.all_gather(bc_raw, "heads", axis=1, tiled=True)
        bc_raw = lax.dynamic_slice_in_dim(bc_raw, group * 2 * N, 2 * N, 1)
    return jnp.transpose(xz), bc_raw, jnp.transpose(small[:, bc_width:])


def norm_split(gathered, gain):
    wide = jnp.moveaxis(gathered, 0, 1).reshape(gathered.shape[1], -1).astype(jnp.float32)
    first_group = lax.axis_index("heads") * wide.shape[1] // (PER_GROUP * P_SIZE)
    at_group = lax.broadcasted_iota(jnp.int32, (1, G), 1) == first_group
    square = jnp.sum(jnp.square(wide), axis=1, keepdims=True)
    square = lax.psum(jnp.where(at_group, square, 0.0), "heads")
    square = jnp.sum(jnp.where(at_group, square, 0.0), axis=1, keepdims=True)
    scale = lax.rsqrt(square / (PER_GROUP * P_SIZE) + EPSILON)
    return (wide * scale * gain[None]).astype(jnp.bfloat16)


def solution(mesh):
    in_specs = (
        P(("groups", "seq"), "heads"),
        P(None, ("heads", "seq")),
        P(None, "heads"),
        P(None, "heads"),
        P("heads"),
        P("heads"),
        P("heads"),
        P(None, "heads"),
        P("heads"),
        P(),
        P(),
        P("heads"),
        P("groups"),
        P("groups"),
    )
    out_specs = (P(("groups", "seq"), "heads"), P(("groups", "heads"), None, "seq", None, None))
    return jax.shard_map(fast_shards, mesh=mesh, in_specs=in_specs, out_specs=out_specs, check_vma=False)
```

```python
import functools

import jax
import jax.numpy as jnp
from jax import lax
from jax.experimental import pallas as pl
from jax.experimental.pallas import tpu as pltpu
from jax.sharding import PartitionSpec as P

H = 256
P_SIZE = 64
N = 128
G = 8
CH = 256
PER_GROUP = H // G
EPSILON = 1e-05


def project(tokens, xz_weight, small_weight, chunks):
    sections, head_devices = lax.axis_size("seq"), lax.axis_size("heads")
    rows = tokens.shape[0] // chunks
    width = tokens.shape[1]
    pieces = [tokens[c * rows : (c + 1) * rows] for c in range(chunks)]
    xz, small = [], []
    for c in range(chunks):
        part = lax.all_gather(pieces[c], ("seq", "heads"), axis=0)
        part = part.reshape(sections, head_devices, rows, width)
        dot = lambda w: lax.dot_general(
            part,
            w.reshape(head_devices, width, w.shape[1]),
            (((1, 3), (0, 1)), ((), ())),
            preferred_element_type=jnp.float32,
        )
        xz.append(dot(xz_weight).astype(jnp.bfloat16))
        small.append(dot(small_weight))
        if c + 2 < chunks:
            pieces[c + 2], xz[c], small[c] = lax.optimization_barrier(
                (pieces[c + 2], xz[c], small[c])
            )
    whole = lambda parts: jnp.concatenate(parts, axis=1).reshape(-1, parts[0].shape[-1])
    return whole(xz), whole(small)


MESH = pl.DeviceIdType.MESH
SPAN = 2048


def nearest_first(z, k, count):
    h = jnp.int32(0)
    for at in range(count):
        order = sorted(range(count), key=lambda q: (abs(q - at), min(q, count - 1 - q)))
        for i, q in enumerate(order):
            if q:
                h = h + jnp.where((z == at) & (k == i), q, 0)
    return h


def gather_project_kernel(
    pieces, tok, xw, bw, sw, xz_out, bc_out, st_out, every,
    wx, wb, ws, tile, ax, ab, ast, ox, ob, ost,
    recv, up_sem, down_sem, x_sem, c_sem, on_sem, w_sem, tile_sem, out_sem,
):
    f32, bf16 = jnp.float32, jnp.bfloat16
    s, z = lax.axis_index("seq"), lax.axis_index("heads")
    line = lax.axis_size("heads")
    other = (s + 2) % 4
    sib = s + 1 - 2 * (s % 2)
    far = (sib + 2) % 4
    rows_all, depth = tok.shape
    halves = pieces // 2
    rows = rows_all // halves
    strip = rows_all // pieces
    part = lambda p: pl.ds(pl.multiple_of(p * strip, strip), strip)
    half = lambda n: pl.ds(pl.multiple_of(n * rows, rows), rows)
    below, above = z > 0, z < line - 1

    barrier = pltpu.get_barrier_semaphore()
    for partner in (other, sib):
        pl.semaphore_signal(barrier, inc=1, device_id={"seq": partner}, device_id_type=MESH)

    @pl.when(above)
    def _():
        pl.semaphore_signal(barrier, inc=1, device_id={"heads": z + 1}, device_id_type=MESH)

    @pl.when(below)
    def _():
        pl.semaphore_signal(barrier, inc=1, device_id={"heads": z - 1}, device_id_type=MESH)

    pl.semaphore_wait(barrier, 2 + above.astype(jnp.int32) + below.astype(jnp.int32))

    def copy(src, sec, h, p, sem, to):
        return pltpu.make_async_remote_copy(
            src_ref=src, dst_ref=every.at[h, sec, part(p)], send_sem=sem, recv_sem=recv.at[sec, h, p],
            device_id=to, device_id_type=MESH,
        )

    held = lambda sec, h, p: every.at[h, sec, part(p)]
    go_up = lambda src, h, p: copy(src, s, h, p, up_sem.at[h, p], {"heads": z + 1})
    go_down = lambda src, h, p: copy(src, s, h, p, down_sem.at[h, p], {"heads": z - 1})
    go_x = lambda src, h, p: copy(src, s, h, p, x_sem.at[h, p], {"seq": other})
    go_c = lambda src, sec, i, h, p: copy(src, sec, h, p, c_sem.at[i, h, p], {"seq": sib})
    def by_line(h, p):
        return (p % 2 == 1) & (((h == line - 1) & (z != line - 1)) | ((h == 0) & (z != 0)))

    def go_on(end, n, p):
        return copy(held(other, end, p), other, end, p, on_sem.at[n, p], {"heads": z + 1 if end == 0 else z - 1})

    arrived = lambda sec, h, p: copy(held(sec, h, p), sec, h, p, x_sem.at[h, p], {"seq": other}).wait_recv()

    def weights(h, slot):
        src = pl.ds(pl.multiple_of(h * depth, depth), depth)
        return [
            pltpu.make_async_copy(xw.at[src], wx.at[slot], w_sem.at[slot, 0]),
            pltpu.make_async_copy(
                bw.at[src, pl.ds(pl.multiple_of((s // 2) * 2 * N, 2 * N), 2 * N)], wb.at[slot], w_sem.at[slot, 1]),
            pltpu.make_async_copy(sw.at[:, src], ws.at[slot], w_sem.at[slot, 2]),
        ]

    load = lambda src, b, n: pltpu.make_async_copy(src, tile.at[b, pl.ds(n * rows, rows)], tile_sem.at[b, n])

    def send_own(p):
        own = tok.at[part(p)]

        @pl.when(above)
        def _():
            go_up(own, z, p).start()

        @pl.when(below)
        def _():
            go_down(own, z, p).start()

        go_x(own, z, p).start()
        go_c(own, s, 0, z, p).start()

    for p in range(pieces):
        send_own(p)
    for k in range(2):
        for c in weights(nearest_first(z, k, line), k):
            c.start()

    ab[...] = jnp.zeros_like(ab)
    ast[...] = jnp.zeros_like(ast)

    def clear(i, carry):
        ax[i // 8, pl.ds(pl.multiple_of((i % 8) * (rows_all // 8), rows_all // 8), rows_all // 8), :] = jnp.zeros(
            (rows_all // 8, ax.shape[2]), f32)
        return carry

    lax.fori_loop(0, 4 * 8, clear, 0)

    wide = min(256, ax.shape[2])
    span = min(SPAN, ax.shape[2])

    def multiply(b, slot, pair, p, first=0, between=None):
        block = pl.ds(first * rows, len(pair) * rows)

        def add(acc, w, cols, turned=False):
            dims = NT if turned else (((1,), (0,)), ((), ()))
            both = lax.dot_general(tile[b, block, :], w, dims, preferred_element_type=f32)
            for n, sec in enumerate(pair):
                acc[sec, half(p), cols] += both[n * rows : (n + 1) * rows]

        def one(n, carry):
            cols = pl.ds(pl.multiple_of(n * span, span), span)
            add(ax, wx[slot, :, cols], cols)
            return carry

        lax.fori_loop(0, ax.shape[2] // span, one, 0)
        if between is not None:
            between()
        add(ab, wb[slot], slice(None))
        add(ast, ws[slot], slice(0, ws.shape[1]), True)

    mine = st_out.shape[0]
    eye = (
        lax.broadcasted_iota(jnp.int32, (wide, wide), 0) == lax.broadcasted_iota(jnp.int32, (wide, wide), 1)
    ).astype(bf16)

    def results(q, sec, p):
        at = pl.ds(pl.multiple_of(sec * rows_all + p * rows, rows), rows)
        return [
            pltpu.make_async_copy(ox.at[q], xz_out.at[:, at], out_sem.at[q, 0]),
            pltpu.make_async_copy(ob.at[q], bc_out.at[at], out_sem.at[q, 1]),
            pltpu.make_async_copy(
                ost.at[q, pl.ds(pl.multiple_of(s * mine, 8), mine)], st_out.at[:, at], out_sem.at[q, 2]),
        ]

    def finish(q, sec, p):
        def one(n, carry):
            cols = pl.ds(pl.multiple_of(n * wide, wide), wide)
            block = ax[sec, half(p), cols].astype(bf16)
            turned = lax.dot_general(eye, block, NT, preferred_element_type=f32)
            ox[q, cols, :] = turned.astype(bf16)
            return carry

        lax.fori_loop(0, ax.shape[2] // wide, one, 0, unroll=True)
        ob[q] = ab[sec, half(p), :].astype(bf16)
        ost[q] = jnp.transpose(ast[sec, half(p), :])
        for c in results(q, sec, p):
            c.start()

    def step(i, carry):
        u, n = i // halves, i % halves
        h_new = nearest_first(z, u, line)
        h_old = nearest_first(z, u - 1, line)
        new, old = u < line, u >= 1
        rows_of = lambda sec, h: every.at[h, sec, half(n)]

        def pass_on(p):
            for turn in (1, -1):
                sign = turn * jnp.where(2 * z < line, -1, 1)
                h = z + sign * u

                @pl.when((u >= 1) & (h >= 0) & (h < line))
                def _():
                    arrived(s, h, p)
                    src = held(s, h, p)

                    @pl.when((sign < 0) & above)
                    def _():
                        go_up(src, h, p).start()

                    @pl.when((sign > 0) & below)
                    def _():
                        go_down(src, h, p).start()

                    @pl.when(jnp.logical_not(by_line(h, p)))
                    def _():
                        go_x(src, h, p).start()

                    go_c(src, s, 0, h, p).start()

            @pl.when(old & jnp.logical_not(by_line(h_old, p)))
            def _():
                arrived(other, h_old, p)
                go_c(held(other, h_old, p), other, 1, h_old, p).start()

            for end, at, on, sem in ((line - 1, line - z, below, 1), (0, z + 1, above, 0)):
                @pl.when((u == jnp.where(z == end, 1, at)) & (p % 2 == 1))
                def _():
                    @pl.when(z != end)
                    def _():
                        arrived(other, end, p)
                        go_c(held(other, end, p), other, 1, end, p).start()

                    @pl.when(on)
                    def _():
                        go_on(end, sem, p).start()

        def pass_two(m, carry):
            pass_on(2 * n + m)
            return carry

        lax.fori_loop(0, 2, pass_two, 0)

        @pl.when(u == 0)
        def _():
            load(tok.at[half(n)], 0, 0).start()

        @pl.when(new & old)
        def _():
            load(rows_of(s, h_new), 0, 0).start()

        @pl.when(old)
        def _():
            load(rows_of(other, h_old), 1, 0).start()

        @pl.when(new & (n == 0))
        def _():
            for c in weights(h_new, u % 2):
                c.wait()

        def take_far():
            for m in range(2):
                arrived(far, h_old, 2 * n + m)
            load(rows_of(far, h_old), 1, 1).start()

        pl.when(old & new)(take_far)

        @pl.when(new)
        def _():
            for m in range(2):
                arrived(sib, h_new, 2 * n + m)
            load(rows_of(sib, h_new), 0, 1).start()
            for m in range(2):
                load(rows_of(sib, h_new), 0, m).wait()
            multiply(0, u % 2, (s, sib), n)

        @pl.when(old & new)
        def _():
            for m in range(2):
                load(rows_of(far, h_old), 1, m).wait()
            multiply(1, (u - 1) % 2, (other, far), n)

        @pl.when(jnp.logical_not(new))
        def _():
            load(rows_of(other, h_old), 1, 0).wait()
            multiply(1, (u - 1) % 2, (other,), n, 0, take_far)
            load(rows_of(far, h_old), 1, 1).wait()
            multiply(1, (u - 1) % 2, (far,), n, 1)

        @pl.when(old & (u < line - 1) & (n == halves - 1))
        def _():
            for c in weights(nearest_first(z, u + 1, line), (u + 1) % 2):
                c.start()

        @pl.when(u >= line - 1)
        def _():
            last = u == line
            first_sec, second_sec = jnp.where(last, other, s), jnp.where(last, far, sib)

            def one(q, carry):
                sec = jnp.where(q == 0, first_sec, second_sec)

                @pl.when(i > (line - 1) * halves)
                def _():
                    for c in results(q, sec, n):
                        c.wait()

                finish(q, sec, n)
                return carry

            lax.fori_loop(0, 2, one, 0)

        return carry

    lax.fori_loop(0, (line + 1) * halves, step, 0)

    for q in range(2):
        for c in results(q, s, 0):
            c.wait()

    def drain(i, carry):
        h, p = i // pieces, i % pieces
        src = held(s, h, p)

        @pl.when(above & (h <= z))
        def _():
            go_up(src, h, p).wait_send()

        @pl.when(below & (h >= z))
        def _():
            go_down(src, h, p).wait_send()

        @pl.when(jnp.logical_not(by_line(h, p)))
        def _():
            go_x(src, h, p).wait_send()

        go_c(src, s, 0, h, p).wait_send()
        go_c(src, s, 1, h, p).wait_send()
        return carry

    lax.fori_loop(0, line * pieces, drain, 0)

    for p in range(1, pieces, 2):
        @pl.when(above)
        def _():
            go_on(0, 0, p).wait_send()

        @pl.when(below)
        def _():
            go_on(line - 1, 1, p).wait_send()


def gather_project(tokens, xz_weight, bc_weight, step_weight, mine):
    pieces = 4
    sections, line = lax.axis_size("seq"), lax.axis_size("heads")
    rows_all, depth = tokens.shape
    rows = rows_all // (pieces // 2)
    width = xz_weight.shape[1]
    steps = step_weight.shape[1]
    length = rows_all * sections
    f32, bf16 = jnp.float32, jnp.bfloat16
    hbm = pl.BlockSpec(memory_space=pl.ANY)
    dma = pltpu.SemaphoreType.DMA
    wide = min(256, width)
    flops = 2 * length * depth * line * (width + 2 * N + steps)
    return pl.pallas_call(
        functools.partial(gather_project_kernel, pieces),
        in_specs=[hbm] * 4,
        out_specs=[hbm] * 4,
        out_shape=[
            jax.ShapeDtypeStruct((width, length), bf16),
            jax.ShapeDtypeStruct((length, 2 * N), bf16),
            jax.ShapeDtypeStruct((mine, length), f32),
            jax.ShapeDtypeStruct((line, sections, rows_all, depth), bf16),
        ],
        scratch_shapes=[
            pltpu.VMEM((2, depth, width), bf16),
            pltpu.VMEM((2, depth, 2 * N), bf16),
            pltpu.VMEM((2, steps, depth), bf16),
            pltpu.VMEM((2, 2 * rows, depth), bf16),
            pltpu.VMEM((sections, rows_all, width), f32),
            pltpu.VMEM((sections, rows_all, 2 * N), f32),
            pltpu.VMEM((sections, rows_all, 128), f32),
            pltpu.VMEM((2, width, rows), bf16),
            pltpu.VMEM((2, rows, 2 * N), bf16),
            pltpu.VMEM((2, 128, rows), f32),
            dma((sections, line, pieces)),
            dma((line, pieces)),
            dma((line, pieces)),
            dma((line, pieces)),
            dma((2, line, pieces)),
            dma((2, pieces)),
            dma((2, 3)),
            dma((2, 2)),
            dma((2, 3)),
        ],
        compiler_params=pltpu.CompilerParams(
            collective_id=0, has_side_effects=True, vmem_limit_bytes=60 * 1024 * 1024),
        cost_estimate=pl.CostEstimate(flops=flops, bytes_accessed=100_000_000, transcendentals=0),
        name="gather_project",
    )(tokens, xz_weight, bc_weight, jnp.transpose(step_weight))[:3]


LOG2E = 1.4426950408889634
NT = (((1,), (1,)), ((), ()))


def sigmoid(x):
    return 0.5 * jnp.tanh(0.5 * x) + 0.5


def scan_states(
    j, n_read, bounds_ref, readers_ref, xz_ref, bc_ref, step_ref, conv_ref, head_ref, bconv_ref,
    tail, bpad, b_in, c_in, inner, start, cum, stp, wt, states, send,
):
    f32, bf16 = jnp.float32, jnp.bfloat16
    heads = head_ref.shape[0]
    sec = xz_ref.shape[1]
    n_blk = sec // CH
    first = j * n_blk
    taps = 4

    @pl.when(j == 0)
    def _():
        tail[...] = jnp.zeros_like(tail)
        bpad[0:8, :] = jnp.zeros((8, 2 * N), f32)
        start[0] = jnp.zeros(start.shape[1:], f32)

    bpad[8 : 8 + sec, :] = bc_ref[...].astype(f32)
    for i in range(n_blk):
        y = jnp.broadcast_to(bconv_ref[taps : taps + 1, :], (CH, 2 * N))
        for k in range(taps):
            y = y + bconv_ref[k : k + 1, :] * bpad[i * CH + 5 + k : i * CH + 5 + k + CH, :]
        y = (y * sigmoid(y)).astype(bf16)
        b_in[first + i] = y[:, :N]
        c_in[first + i] = y[:, N:]
    bpad[0:8, :] = bpad[sec : sec + 8, :]

    def conv_strip(i, carry):
        row = pl.multiple_of(i * 32, 32)
        src = pl.multiple_of((i // 2) * 128 + (i % 2) * 32, 32)
        raw = xz_ref[pl.ds(src, 32), :]
        both = jnp.concatenate([tail[pl.ds(row, 32), :], raw], axis=1).astype(f32)
        w = conv_ref[pl.ds(row, 32), :]
        y = w[:, 4:5] + w[:, 3:4] * both[:, 128:]
        for d in range(1, taps):
            y = y + w[:, 3 - d : 4 - d] * pltpu.roll(both, d, 1)[:, 128:]
        y = (y * sigmoid(y)).astype(bf16)
        for b in range(n_blk):
            inner[first + b, pl.ds(row, 32), :] = y[:, b * CH : (b + 1) * CH]
        tail[pl.ds(row, 32), :] = raw[:, sec - 128 :]
        return carry

    lax.fori_loop(0, heads * 2, conv_strip, 0, unroll=2)

    raw = step_ref[...] + head_ref[:, 0:1]
    size = jnp.maximum(raw, 0.0) + jnp.log1p(jnp.exp(-jnp.abs(raw)))
    total = (-LOG2E * jnp.exp(head_ref[:, 1:2])) * size
    lane = lax.broadcasted_iota(jnp.int32, (heads, sec), 1) % CH
    d = 1
    while d < CH:
        total = total + jnp.where(lane >= d, pltpu.roll(total, d, 1), 0.0)
        d *= 2
    for b in range(n_blk):
        cum[first + b] = total[:, b * CH : (b + 1) * CH]
        stp[first + b] = size[:, b * CH : (b + 1) * CH]

    def one_block(i, carry):
        b = first + i
        a = cum[b]
        last = a[:, CH - 1 : CH]
        w = jnp.exp2(last - a) * stp[b]
        keep = jnp.exp2(last)
        for h in range(heads):
            rows = slice(h * 64, (h + 1) * 64)
            wt[0, rows, :] = (inner[b, rows, :].astype(f32) * w[h : h + 1, :]).astype(bf16)
        added = jnp.dot(wt[0], b_in[b], preferred_element_type=f32)
        for h in range(heads):
            rows = slice(h * 64, (h + 1) * 64)
            start[b + 1, rows, :] = start[b, rows, :] * keep[h : h + 1, :] + added[rows, :]
        return carry

    lax.fori_loop(0, n_blk, one_block, 0)

    lane_b = lax.broadcasted_iota(jnp.int32, (heads, CH), 1)

    def one_bound(k, carry):
        r = (lax.axis_index("heads") + n_read // 2 + k) % n_read
        q = jnp.int32(0)
        for i in range(n_read):
            q = q + jnp.where(readers_ref[j * n_read + i] == r, bounds_ref[j * n_read + i], 0)
        b = q // CH
        off = q % CH
        a = cum[b]
        at = jnp.sum(jnp.where(lane_b == off, a, 0.0), axis=1, keepdims=True)
        w = jnp.where(lane_b <= off, jnp.exp2(jnp.minimum(at - a, 0.0)), 0.0) * stp[b]
        keep = jnp.exp2(at)
        slot = k % 2
        for h in range(heads):
            rows = slice(h * 64, (h + 1) * 64)
            wt[slot, rows, :] = (inner[b, rows, :].astype(f32) * w[h : h + 1, :]).astype(bf16)
        inside = jnp.dot(wt[slot], b_in[b], preferred_element_type=f32)
        for h in range(heads):
            rows = slice(h * 64, (h + 1) * 64)
            states[r, j, rows, :] = (start[b, rows, :] * keep[h : h + 1, :] + inside[rows, :]).astype(bf16)
        send(r)
        return carry

    lax.fori_loop(0, n_read, one_bound, 0)


def scan_outputs(j, xz_ref, head_ref, b_in, c_in, inner, start, cum, stp, scores, mix, outer, gated_t, gated):
    f32, bf16 = jnp.float32, jnp.bfloat16
    heads = head_ref.shape[0]
    n_blk = xz_ref.shape[1] // CH
    row_id = lax.broadcasted_iota(jnp.int32, (CH, CH), 0)
    col_id = lax.broadcasted_iota(jnp.int32, (CH, CH), 1)
    eye = (row_id == col_id).astype(bf16)

    @pl.when(j == 0)
    def _():
        mix[...] = jnp.zeros_like(mix)

    def one_block(i, carry):
        b = j * n_blk + i
        lanes = pl.ds(pl.multiple_of(i * CH, CH), CH)
        scores[...] = jnp.where(
            row_id <= col_id,
            lax.dot_general(b_in[b], c_in[b], NT, preferred_element_type=f32), 0.0)
        outer[...] = lax.dot_general(start[b].astype(bf16), c_in[b], NT, preferred_element_type=f32)
        a = cum[b]
        s = stp[b]
        a_col = jnp.transpose(jnp.concatenate([a, jnp.zeros((128 - heads, CH), f32)], axis=0))
        grow = jnp.exp2(a)
        for h in range(heads):
            rows = slice(h * 64, (h + 1) * 64)
            m = h % mix.shape[0]
            a_h = a[h : h + 1, :]
            for s0 in range(0, CH, 32):
                lo = (s0 // 128) * 128
                col = a_col[s0 : s0 + 32, h : h + 1]
                gap = jnp.minimum(a_h[:, lo:] - col, 0.0)
                mix[m, s0 : s0 + 32, lo:] = (jnp.exp2(gap) * scores[s0 : s0 + 32, lo:]).astype(bf16)
            x = inner[b, rows, :].astype(f32)
            intra = jnp.dot((x * s[h : h + 1, :]).astype(bf16), mix[m], preferred_element_type=f32)
            gate = xz_ref[h * 128 + 64 : (h + 1) * 128, lanes].astype(f32)
            ssd = intra + outer[rows, :] * grow[h : h + 1, :] + head_ref[h : h + 1, 2:3] * x
            gated_t[rows, :] = (ssd * (gate * sigmoid(gate))).astype(bf16)
        span = min(heads * 64, CH)
        for c in range(0, heads * 64, span):
            out = lax.dot_general(eye, gated_t[c : c + span, :], NT, preferred_element_type=f32)
            gated[j, lanes, c : c + span] = out.astype(bf16)
        return carry

    lax.fori_loop(0, n_blk, one_block, 0)


def scan_kernel(n_read, with_norm, *refs):
    (bounds_ref, readers_ref, xz_ref, bc_ref, step_ref, conv_ref, conv_bias_ref, head_ref, bconv_ref, bconv_bias_ref, gain_ref,
     result, handoff) = refs[:13]
    (tail, bpad, b_in, c_in, inner, start, cum, stp, wt, states, scores, mix, outer, gated_t, gated,
     state_send, state_recv, state_here, gated_send, gated_recv, gated_here, out_sem, conv_cols, head_cols, bconv) = refs[13:38]
    landing, normed = refs[38:] if with_norm else (result, None)
    sections, line = lax.axis_size("seq"), lax.axis_size("heads")
    s, z = lax.axis_index("seq"), lax.axis_index("heads")
    sub = line // sections
    j = pl.program_id(0)
    size = states.shape[2]
    to_sec = z // sub
    row = (z % sub) * sections + s

    def prepare():
        heads = head_cols.shape[0]
        taps, width = 4, heads * 64
        cols = pl.ds(pl.multiple_of(s * width, 128), width)
        stack = jnp.concatenate(
            [conv_ref[:, cols], conv_bias_ref[:, cols], jnp.zeros((123, width), jnp.float32)], axis=0)
        conv_cols[...] = jnp.transpose(stack)
        turned = jnp.transpose(head_ref[...])
        head_cols[...] = pltpu.roll(turned, (128 - s * heads) % 128, 0)[0:heads, :]
        group = (z * heads * sections + s * heads) // PER_GROUP
        lanes = pl.ds(pl.multiple_of(group * 2 * N, 2 * N), 2 * N)
        bconv[0:taps, :] = bconv_ref[:, lanes]
        bconv[taps : taps + 1, :] = bconv_bias_ref[:, lanes]

    def place(at, sec):
        return handoff.at[sec, pl.ds(pl.multiple_of(at * size, size), size)]

    def state_copy(r, sec):
        return pltpu.make_async_remote_copy(
            src_ref=states.at[r, sec], dst_ref=place(row, sec), send_sem=state_send.at[r, sec],
            recv_sem=state_recv.at[row, sec], device_id={"seq": to_sec, "heads": r}, device_id_type=MESH)

    def state_keep(sec):
        return pltpu.make_async_copy(states.at[z, sec], place(row, sec), state_here.at[sec])

    def gated_copy(sec, source):
        return pltpu.make_async_remote_copy(
            src_ref=gated.at[sec], dst_ref=landing.at[source], send_sem=gated_send.at[sec],
            recv_sem=gated_recv.at[source], device_id={"seq": sec}, device_id_type=MESH)

    gated_keep = lambda: pltpu.make_async_copy(gated.at[s], landing.at[s], gated_here.at[0])
    mine_too = to_sec == s

    @pl.when(j == 0)
    def _():
        prepare()
        barrier = pltpu.get_barrier_semaphore()
        for sec in range(sections):
            for k in range(sub):
                h = s * sub + k

                @pl.when((sec != s) | (h != z))
                def _():
                    pl.semaphore_signal(barrier, inc=1, device_id={"seq": sec, "heads": h}, device_id_type=MESH)

            @pl.when(sec != s)
            def _():
                pl.semaphore_signal(barrier, inc=1, device_id={"seq": sec}, device_id_type=MESH)

        pl.semaphore_wait(barrier, line + sections - 1 - mine_too.astype(jnp.int32))

    def send(r):
        @pl.when(mine_too & (r == z))
        def _():
            state_keep(j).start()

        @pl.when(jnp.logical_not(mine_too & (r == z)))
        def _():
            state_copy(r, j).start()

    scan_states(
        j, n_read, bounds_ref, readers_ref, xz_ref, bc_ref, step_ref, conv_cols, head_cols, bconv,
        tail, bpad, b_in, c_in, inner, start, cum, stp, wt, states, send)
    scan_outputs(j, xz_ref, head_cols, b_in, c_in, inner, start, cum, stp, scores, mix, outer, gated_t, gated)

    @pl.when(j == s)
    def _():
        gated_keep().start()

    @pl.when(j != s)
    def _():
        gated_copy(j, s).start()

    @pl.when(j == sections - 1)
    def _():
        gated_keep().wait()
        for sec in range(sections):
            @pl.when(sec != s)
            def _():
                gated_copy(sec, sec).wait_recv()

        if with_norm:
            norm_rows(landing, gain_ref, normed, result, out_sem)

        def drain(n, carry):
            r, sec = n // sections, n % sections

            @pl.when(jnp.logical_not(mine_too & (r == z)))
            def _():
                state_copy(r, sec).wait_send()

            return carry

        lax.fori_loop(0, n_read * sections, drain, 0)

        @pl.when(mine_too)
        def _():
            for sec in range(sections):
                state_keep(sec).wait()

        def arrive(n, carry):
            at, sec = n // sections, n % sections
            here = mine_too & (at == row)

            @pl.when(jnp.logical_not(here))
            def _():
                pltpu.make_async_remote_copy(
                    src_ref=states.at[0, sec], dst_ref=place(at, sec), send_sem=state_send.at[0, sec],
                    recv_sem=state_recv.at[at, sec], device_id={"seq": to_sec}, device_id_type=MESH).wait_recv()

            return carry

        lax.fori_loop(0, sub * sections * sections, arrive, 0)
        for sec in range(sections):
            @pl.when(sec != s)
            def _():
                gated_copy(sec, s).wait_send()


def norm_rows(x_ref, gain_ref, normed, result, out_sem):
    sources, rows_all, width = x_ref.shape
    per = (PER_GROUP * P_SIZE) // width
    tiles = out_sem.shape[0]
    tile = rows_all // tiles

    def one(t, carry):
        rows = pl.ds(pl.multiple_of(t * tile, tile), tile)
        for g in range(sources // per):
            square = jnp.zeros((tile, 1), jnp.float32)
            for n in range(per):
                p = x_ref[g * per + n, rows, :].astype(jnp.float32)
                square = square + jnp.sum(p * p, axis=1, keepdims=True)
            scale = lax.rsqrt(square / (PER_GROUP * P_SIZE) + EPSILON)
            for n in range(per):
                cols = slice((g * per + n) * width, (g * per + n + 1) * width)
                p = x_ref[g * per + n, rows, :].astype(jnp.float32)
                normed[rows, cols] = (p * scale * gain_ref[:, cols]).astype(jnp.bfloat16)
        pltpu.make_async_copy(normed.at[rows], result.at[rows], out_sem.at[t]).start()
        return carry

    lax.fori_loop(0, tiles, one, 0)

    def wait(t, carry):
        rows = pl.ds(pl.multiple_of(t * tile, tile), tile)
        pltpu.make_async_copy(normed.at[rows], result.at[rows], out_sem.at[t]).wait()
        return carry

    lax.fori_loop(0, tiles, wait, 0)


def scan_call(xz_t, bc_raw, step_t, conv, conv_bias, head_rows, bconv, bconv_bias, gain, bounds, readers):
    sections, line = lax.axis_size("seq"), lax.axis_size("heads")
    heads = step_t.shape[0]
    length = xz_t.shape[1]
    sec = length // sections
    n_read = bounds.shape[0] // sections
    sub = line // sections
    n_blk, blocks = sec // CH, length // CH
    with_norm = sections * heads % PER_GROUP == 0
    f32, bf16 = jnp.float32, jnp.bfloat16
    dma = pltpu.SemaphoreType.DMA
    whole = lambda a: pl.BlockSpec(a.shape, lambda i: (0,) * a.ndim)
    smem = pl.BlockSpec(memory_space=pltpu.SMEM)
    hbm = pl.BlockSpec(memory_space=pl.ANY)
    width = heads * 64
    result = (sec, sections * width) if with_norm else (sections, sec, width)
    tiles = 16
    scratch = [
        pltpu.VMEM((width, 128), bf16),
        pltpu.VMEM((sec + 8, 2 * N), f32),
        pltpu.VMEM((blocks, CH, N), bf16),
        pltpu.VMEM((blocks, CH, N), bf16),
        pltpu.VMEM((blocks, width, CH), bf16),
        pltpu.VMEM((blocks + 1, width, N), f32),
        pltpu.VMEM((blocks, heads, CH), f32),
        pltpu.VMEM((blocks, heads, CH), f32),
        pltpu.VMEM((2, width, CH), bf16),
        pltpu.VMEM((n_read, sections, width, N), bf16),
        pltpu.VMEM((CH, CH), f32),
        pltpu.VMEM((4, CH, CH), bf16),
        pltpu.VMEM((width, CH), f32),
        pltpu.VMEM((width, CH), bf16),
        pltpu.VMEM((sections, sec, width), bf16),
        dma((n_read, sections)),
        dma((sub * sections, sections)),
        dma((sections,)),
        dma((sections,)),
        dma((sections,)),
        dma((1,)),
        dma((tiles,)),
        pltpu.VMEM((width, 128), f32),
        pltpu.VMEM((heads, 128), f32),
        pltpu.VMEM((8, 2 * N), f32),
    ]
    if with_norm:
        scratch += [pltpu.VMEM((sections, sec, width), bf16), pltpu.VMEM(result, bf16)]
    return pl.pallas_call(
        functools.partial(scan_kernel, n_read, with_norm),
        grid=(sections,),
        in_specs=[
            smem,
            smem,
            pl.BlockSpec((heads * 128, sec), lambda i: (0, i)),
            pl.BlockSpec((sec, 2 * N), lambda i: (i, 0)),
            pl.BlockSpec((heads, sec), lambda i: (0, i)),
            whole(conv),
            whole(conv_bias),
            whole(head_rows),
            whole(bconv),
            whole(bconv_bias),
            whole(gain),
        ],
        out_specs=[hbm, hbm],
        out_shape=[
            jax.ShapeDtypeStruct(result, bf16),
            jax.ShapeDtypeStruct((sections, sub * sections * width, N), bf16),
        ],
        scratch_shapes=scratch,
        compiler_params=pltpu.CompilerParams(
            collective_id=1, has_side_effects=True, vmem_limit_bytes=56 * 1024 * 1024),
        cost_estimate=pl.CostEstimate(flops=10_000_000_000, bytes_accessed=30_000_000, transcendentals=0),
        name="scan",
    )(bounds, readers, xz_t, bc_raw, step_t, conv, conv_bias, head_rows, bconv, bconv_bias, gain)


def fast_shards(
    tokens,
    xz_weight,
    bc_weight,
    step_weight,
    step_bias,
    decay_log,
    skip_gain,
    conv_weight,
    conv_bias,
    bc_conv_weight,
    bc_conv_bias,
    norm_gain,
    step_bounds,
    readers,
):
    head_devices = lax.axis_size("heads")
    sections = lax.axis_size("seq")
    section = lax.axis_index("seq")
    head_block = lax.axis_index("heads")
    block_heads = H // head_devices
    mine = block_heads // sections
    first_mine = section * mine
    group = (head_block * block_heads + first_mine) // PER_GROUP
    own = lambda a, width, axis: lax.dynamic_slice_in_dim(a, first_mine * width, mine * width, axis)
    head_rows = jnp.pad(jnp.stack([step_bias, decay_log, skip_gain]), ((0, 125), (0, 128 - block_heads)))

    if head_devices == 4 and sections == 4:
        xz_t, bc_raw, step_t = gather_project(tokens, xz_weight, bc_weight, step_weight, mine)
    else:
        small_step = own(step_weight, 1, 1)
        xz_t, bc_raw, step_t = project_parts(tokens, xz_weight, bc_weight, small_step, group)

    result, handoff = scan_call(
        xz_t, bc_raw, step_t, conv_weight, conv_bias[None], head_rows, bc_conv_weight, bc_conv_bias[None],
        norm_gain[None], step_bounds, readers)
    if block_heads % PER_GROUP == 0:
        mixed, handoff = place_results(result, handoff.reshape(-1, N))
    else:
        mixed = norm_split(result, norm_gain)
    return (mixed, handoff.reshape(1, sections, -1, P_SIZE, N))


def place_results(mixed, handoff):
    def kernel(a_ref, b_ref, a_out, b_out):
        a_out[...] = a_ref[...]
        b_out[...] = b_ref[...]

    parts = 4
    specs = [pl.BlockSpec((a.shape[0] // parts, a.shape[1]), lambda i: (i, 0)) for a in (mixed, handoff)]
    return pl.pallas_call(
        kernel,
        grid=(parts,),
        in_specs=specs,
        out_specs=specs,
        out_shape=[jax.ShapeDtypeStruct(a.shape, a.dtype) for a in (mixed, handoff)],
        compiler_params=pltpu.CompilerParams(vmem_limit_bytes=32 * 1024 * 1024),
        name="place_results",
    )(mixed, handoff)


def project_parts(tokens, xz_weight, bc_weight, step_weight, group):
    head_block = lax.axis_index("heads")
    width_bc = bc_weight.shape[1]
    whole_group = width_bc >= 2 * N
    if whole_group:
        bc_weight = lax.dynamic_slice_in_dim(bc_weight, group * 2 * N - head_block * width_bc, 2 * N, 1)
    bc_width = bc_weight.shape[1]
    xz, small = project(tokens, xz_weight, jnp.concatenate([bc_weight, step_weight], axis=1), 4)
    bc_raw = small[:, :bc_width].astype(jnp.bfloat16)
    if not whole_group:
        bc_raw = lax.all_gather(bc_raw, "heads", axis=1, tiled=True)
        bc_raw = lax.dynamic_slice_in_dim(bc_raw, group * 2 * N, 2 * N, 1)
    return jnp.transpose(xz), bc_raw, jnp.transpose(small[:, bc_width:])


def norm_split(gathered, gain):
    wide = jnp.moveaxis(gathered, 0, 1).reshape(gathered.shape[1], -1).astype(jnp.float32)
    first_group = lax.axis_index("heads") * wide.shape[1] // (PER_GROUP * P_SIZE)
    at_group = lax.broadcasted_iota(jnp.int32, (1, G), 1) == first_group
    square = jnp.sum(jnp.square(wide), axis=1, keepdims=True)
    square = lax.psum(jnp.where(at_group, square, 0.0), "heads")
    square = jnp.sum(jnp.where(at_group, square, 0.0), axis=1, keepdims=True)
    scale = lax.rsqrt(square / (PER_GROUP * P_SIZE) + EPSILON)
    return (wide * scale * gain[None]).astype(jnp.bfloat16)


def solution(mesh):
    in_specs = (
        P(("groups", "seq"), "heads"),
        P(None, ("heads", "seq")),
        P(None, "heads"),
        P(None, "heads"),
        P("heads"),
        P("heads"),
        P("heads"),
        P(None, "heads"),
        P("heads"),
        P(),
        P(),
        P("heads"),
        P("groups"),
        P("groups"),
    )
    out_specs = (P(("groups", "seq"), "heads"), P(("groups", "heads"), None, "seq", None, None))
    return jax.shard_map(fast_shards, mesh=mesh, in_specs=in_specs, out_specs=out_specs, check_vma=False)
```

```python
import functools

import jax
import jax.numpy as jnp
from jax import lax
from jax.experimental import pallas as pl
from jax.experimental.pallas import tpu as pltpu
from jax.sharding import PartitionSpec as P

H = 256
P_SIZE = 64
N = 128
G = 8
CH = 256
PER_GROUP = H // G
EPSILON = 1e-05


def project(tokens, xz_weight, small_weight, chunks):
    sections, head_devices = lax.axis_size("seq"), lax.axis_size("heads")
    rows = tokens.shape[0] // chunks
    width = tokens.shape[1]
    pieces = [tokens[c * rows : (c + 1) * rows] for c in range(chunks)]
    xz, small = [], []
    for c in range(chunks):
        part = lax.all_gather(pieces[c], ("seq", "heads"), axis=0)
        part = part.reshape(sections, head_devices, rows, width)
        dot = lambda w: lax.dot_general(
            part,
            w.reshape(head_devices, width, w.shape[1]),
            (((1, 3), (0, 1)), ((), ())),
            preferred_element_type=jnp.float32,
        )
        xz.append(dot(xz_weight).astype(jnp.bfloat16))
        small.append(dot(small_weight))
        if c + 2 < chunks:
            pieces[c + 2], xz[c], small[c] = lax.optimization_barrier(
                (pieces[c + 2], xz[c], small[c])
            )
    whole = lambda parts: jnp.concatenate(parts, axis=1).reshape(-1, parts[0].shape[-1])
    return whole(xz), whole(small)


MESH = pl.DeviceIdType.MESH
SPAN = 2048


def nearest_first(z, k, count):
    h = jnp.int32(0)
    for at in range(count):
        order = sorted(range(count), key=lambda q: (abs(q - at), min(q, count - 1 - q)))
        for i, q in enumerate(order):
            if q:
                h = h + jnp.where((z == at) & (k == i), q, 0)
    return h


def gather_project_kernel(
    pieces, tok, xw, bw, sw, xz_out, bc_out, st_out, every,
    wx, wb, ws, tile, ax, ab, ast, ox, ob, ost,
    recv, up_sem, down_sem, x_sem, c_sem, on_sem, w_sem, tile_sem, out_sem,
):
    f32, bf16 = jnp.float32, jnp.bfloat16
    s, z = lax.axis_index("seq"), lax.axis_index("heads")
    line = lax.axis_size("heads")
    other = (s + 2) % 4
    sib = s + 1 - 2 * (s % 2)
    far = (sib + 2) % 4
    rows_all, depth = tok.shape
    halves = pieces // 2
    rows = rows_all // halves
    strip = rows_all // pieces
    part = lambda p: pl.ds(pl.multiple_of(p * strip, strip), strip)
    half = lambda n: pl.ds(pl.multiple_of(n * rows, rows), rows)
    below, above = z > 0, z < line - 1

    barrier = pltpu.get_barrier_semaphore()
    for partner in (other, sib):
        pl.semaphore_signal(barrier, inc=1, device_id={"seq": partner}, device_id_type=MESH)

    @pl.when(above)
    def _():
        pl.semaphore_signal(barrier, inc=1, device_id={"heads": z + 1}, device_id_type=MESH)

    @pl.when(below)
    def _():
        pl.semaphore_signal(barrier, inc=1, device_id={"heads": z - 1}, device_id_type=MESH)

    pl.semaphore_wait(barrier, 2 + above.astype(jnp.int32) + below.astype(jnp.int32))

    def copy(src, sec, h, p, sem, to):
        return pltpu.make_async_remote_copy(
            src_ref=src, dst_ref=every.at[h, sec, part(p)], send_sem=sem, recv_sem=recv.at[sec, h, p],
            device_id=to, device_id_type=MESH,
        )

    held = lambda sec, h, p: every.at[h, sec, part(p)]
    go_up = lambda src, h, p: copy(src, s, h, p, up_sem.at[h, p], {"heads": z + 1})
    go_down = lambda src, h, p: copy(src, s, h, p, down_sem.at[h, p], {"heads": z - 1})
    go_x = lambda src, h, p: copy(src, s, h, p, x_sem.at[h, p], {"seq": other})
    go_c = lambda src, sec, i, h, p: copy(src, sec, h, p, c_sem.at[i, h, p], {"seq": sib})
    def by_line(h, p):
        return (p % 2 == 1) & (((h == line - 1) & (z != line - 1)) | ((h == 0) & (z != 0)))

    def go_on(end, n, p):
        return copy(held(other, end, p), other, end, p, on_sem.at[n, p], {"heads": z + 1 if end == 0 else z - 1})

    arrived = lambda sec, h, p: copy(held(sec, h, p), sec, h, p, x_sem.at[h, p], {"seq": other}).wait_recv()

    def weights(h, slot):
        src = pl.ds(pl.multiple_of(h * depth, depth), depth)
        return [
            pltpu.make_async_copy(xw.at[src], wx.at[slot], w_sem.at[slot, 0]),
            pltpu.make_async_copy(
                bw.at[src, pl.ds(pl.multiple_of((s // 2) * 2 * N, 2 * N), 2 * N)], wb.at[slot], w_sem.at[slot, 1]),
            pltpu.make_async_copy(sw.at[:, src], ws.at[slot], w_sem.at[slot, 2]),
        ]

    load = lambda src, b, n: pltpu.make_async_copy(src, tile.at[b, pl.ds(n * rows, rows)], tile_sem.at[b, n])

    def send_own(p):
        own = tok.at[part(p)]

        @pl.when(above)
        def _():
            go_up(own, z, p).start()

        @pl.when(below)
        def _():
            go_down(own, z, p).start()

        go_x(own, z, p).start()
        go_c(own, s, 0, z, p).start()

    for p in range(pieces):
        send_own(p)
    for k in range(2):
        for c in weights(nearest_first(z, k, line), k):
            c.start()

    ab[...] = jnp.zeros_like(ab)
    ast[...] = jnp.zeros_like(ast)

    def clear(i, carry):
        ax[i // 8, pl.ds(pl.multiple_of((i % 8) * (rows_all // 8), rows_all // 8), rows_all // 8), :] = jnp.zeros(
            (rows_all // 8, ax.shape[2]), f32)
        return carry

    lax.fori_loop(0, 4 * 8, clear, 0)

    wide = min(256, ax.shape[2])
    span = min(SPAN, ax.shape[2])

    def multiply(b, slot, pair, p, first=0, between=None):
        block = pl.ds(first * rows, len(pair) * rows)

        def add(acc, w, cols, turned=False):
            dims = NT if turned else (((1,), (0,)), ((), ()))
            both = lax.dot_general(tile[b, block, :], w, dims, preferred_element_type=f32)
            for n, sec in enumerate(pair):
                acc[sec, half(p), cols] += both[n * rows : (n + 1) * rows]

        def one(n, carry):
            cols = pl.ds(pl.multiple_of(n * span, span), span)
            add(ax, wx[slot, :, cols], cols)
            return carry

        lax.fori_loop(0, ax.shape[2] // span, one, 0)
        if between is not None:
            between()
        add(ab, wb[slot], slice(None))
        add(ast, ws[slot], slice(0, ws.shape[1]), True)

    mine = st_out.shape[0]
    eye = (
        lax.broadcasted_iota(jnp.int32, (wide, wide), 0) == lax.broadcasted_iota(jnp.int32, (wide, wide), 1)
    ).astype(bf16)

    def results(q, sec, p):
        at = pl.ds(pl.multiple_of(sec * rows_all + p * rows, rows), rows)
        return [
            pltpu.make_async_copy(ox.at[q], xz_out.at[:, at], out_sem.at[q, 0]),
            pltpu.make_async_copy(ob.at[q], bc_out.at[at], out_sem.at[q, 1]),
            pltpu.make_async_copy(
                ost.at[q, pl.ds(pl.multiple_of(s * mine, 8), mine)], st_out.at[:, at], out_sem.at[q, 2]),
        ]

    def finish(q, sec, p):
        def one(n, carry):
            cols = pl.ds(pl.multiple_of(n * wide, wide), wide)
            block = ax[sec, half(p), cols].astype(bf16)
            turned = lax.dot_general(eye, block, NT, preferred_element_type=f32)
            ox[q, cols, :] = turned.astype(bf16)
            return carry

        lax.fori_loop(0, ax.shape[2] // wide, one, 0, unroll=True)
        ob[q] = ab[sec, half(p), :].astype(bf16)
        ost[q] = jnp.transpose(ast[sec, half(p), :])
        for c in results(q, sec, p):
            c.start()

    def step(i, carry):
        u, n = i // halves, i % halves
        h_new = nearest_first(z, u, line)
        h_old = nearest_first(z, u - 1, line)
        new, old = u < line, u >= 1
        rows_of = lambda sec, h: every.at[h, sec, half(n)]

        def pass_on(p):
            for turn in (1, -1):
                sign = turn * jnp.where(2 * z < line, -1, 1)
                h = z + sign * u

                @pl.when((u >= 1) & (h >= 0) & (h < line))
                def _():
                    arrived(s, h, p)
                    src = held(s, h, p)

                    @pl.when((sign < 0) & above)
                    def _():
                        go_up(src, h, p).start()

                    @pl.when((sign > 0) & below)
                    def _():
                        go_down(src, h, p).start()

                    @pl.when(jnp.logical_not(by_line(h, p)))
                    def _():
                        go_x(src, h, p).start()

                    go_c(src, s, 0, h, p).start()

            @pl.when(old & jnp.logical_not(by_line(h_old, p)))
            def _():
                arrived(other, h_old, p)
                go_c(held(other, h_old, p), other, 1, h_old, p).start()

            for end, at, on, sem in ((line - 1, line - z, below, 1), (0, z + 1, above, 0)):
                @pl.when((u == jnp.where(z == end, 1, at)) & (p % 2 == 1))
                def _():
                    @pl.when(z != end)
                    def _():
                        arrived(other, end, p)
                        go_c(held(other, end, p), other, 1, end, p).start()

                    @pl.when(on)
                    def _():
                        go_on(end, sem, p).start()

        def pass_two(m, carry):
            pass_on(2 * n + m)
            return carry

        lax.fori_loop(0, 2, pass_two, 0)

        @pl.when(u == 0)
        def _():
            load(tok.at[half(n)], 0, 0).start()

        @pl.when(new & old)
        def _():
            load(rows_of(s, h_new), 0, 0).start()

        @pl.when(old)
        def _():
            load(rows_of(other, h_old), 1, 0).start()

        @pl.when(new & (n == 0))
        def _():
            for c in weights(h_new, u % 2):
                c.wait()

        def take_far():
            for m in range(2):
                arrived(far, h_old, 2 * n + m)
            load(rows_of(far, h_old), 1, 1).start()

        pl.when(old & new)(take_far)

        @pl.when(new)
        def _():
            for m in range(2):
                arrived(sib, h_new, 2 * n + m)
            load(rows_of(sib, h_new), 0, 1).start()
            for m in range(2):
                load(rows_of(sib, h_new), 0, m).wait()
            multiply(0, u % 2, (s, sib), n)

        @pl.when(old & new)
        def _():
            for m in range(2):
                load(rows_of(far, h_old), 1, m).wait()
            multiply(1, (u - 1) % 2, (other, far), n)

        @pl.when(jnp.logical_not(new))
        def _():
            load(rows_of(other, h_old), 1, 0).wait()
            multiply(1, (u - 1) % 2, (other,), n, 0, take_far)
            load(rows_of(far, h_old), 1, 1).wait()
            multiply(1, (u - 1) % 2, (far,), n, 1)

        @pl.when(old & (u < line - 1) & (n == halves - 1))
        def _():
            for c in weights(nearest_first(z, u + 1, line), (u + 1) % 2):
                c.start()

        @pl.when(u >= line - 1)
        def _():
            last = u == line
            first_sec, second_sec = jnp.where(last, other, s), jnp.where(last, far, sib)

            def one(q, carry):
                sec = jnp.where(q == 0, first_sec, second_sec)

                @pl.when(i > (line - 1) * halves)
                def _():
                    for c in results(q, sec, n):
                        c.wait()

                finish(q, sec, n)
                return carry

            lax.fori_loop(0, 2, one, 0)

        return carry

    lax.fori_loop(0, (line + 1) * halves, step, 0)

    for q in range(2):
        for c in results(q, s, 0):
            c.wait()

    def drain(i, carry):
        h, p = i // pieces, i % pieces
        src = held(s, h, p)

        @pl.when(above & (h <= z))
        def _():
            go_up(src, h, p).wait_send()

        @pl.when(below & (h >= z))
        def _():
            go_down(src, h, p).wait_send()

        @pl.when(jnp.logical_not(by_line(h, p)))
        def _():
            go_x(src, h, p).wait_send()

        go_c(src, s, 0, h, p).wait_send()
        go_c(src, s, 1, h, p).wait_send()
        return carry

    lax.fori_loop(0, line * pieces, drain, 0)

    for p in range(1, pieces, 2):
        @pl.when(above)
        def _():
            go_on(0, 0, p).wait_send()

        @pl.when(below)
        def _():
            go_on(line - 1, 1, p).wait_send()


def gather_project(tokens, xz_weight, bc_weight, step_weight, mine):
    pieces = 4
    sections, line = lax.axis_size("seq"), lax.axis_size("heads")
    rows_all, depth = tokens.shape
    rows = rows_all // (pieces // 2)
    width = xz_weight.shape[1]
    steps = step_weight.shape[1]
    length = rows_all * sections
    f32, bf16 = jnp.float32, jnp.bfloat16
    hbm = pl.BlockSpec(memory_space=pl.ANY)
    dma = pltpu.SemaphoreType.DMA
    wide = min(256, width)
    flops = 2 * length * depth * line * (width + 2 * N + steps)
    return pl.pallas_call(
        functools.partial(gather_project_kernel, pieces),
        in_specs=[hbm] * 4,
        out_specs=[hbm] * 4,
        out_shape=[
            jax.ShapeDtypeStruct((width, length), bf16),
            jax.ShapeDtypeStruct((length, 2 * N), bf16),
            jax.ShapeDtypeStruct((mine, length), f32),
            jax.ShapeDtypeStruct((line, sections, rows_all, depth), bf16),
        ],
        scratch_shapes=[
            pltpu.VMEM((2, depth, width), bf16),
            pltpu.VMEM((2, depth, 2 * N), bf16),
            pltpu.VMEM((2, steps, depth), bf16),
            pltpu.VMEM((2, 2 * rows, depth), bf16),
            pltpu.VMEM((sections, rows_all, width), f32),
            pltpu.VMEM((sections, rows_all, 2 * N), f32),
            pltpu.VMEM((sections, rows_all, 128), f32),
            pltpu.VMEM((2, width, rows), bf16),
            pltpu.VMEM((2, rows, 2 * N), bf16),
            pltpu.VMEM((2, 128, rows), f32),
            dma((sections, line, pieces)),
            dma((line, pieces)),
            dma((line, pieces)),
            dma((line, pieces)),
            dma((2, line, pieces)),
            dma((2, pieces)),
            dma((2, 3)),
            dma((2, 2)),
            dma((2, 3)),
        ],
        compiler_params=pltpu.CompilerParams(
            collective_id=0, has_side_effects=True, vmem_limit_bytes=60 * 1024 * 1024),
        cost_estimate=pl.CostEstimate(flops=flops, bytes_accessed=100_000_000, transcendentals=0),
        name="gather_project",
    )(tokens, xz_weight, bc_weight, jnp.transpose(step_weight))[:3]


LOG2E = 1.4426950408889634
NT = (((1,), (1,)), ((), ()))


def sigmoid(x):
    return 0.5 * jnp.tanh(0.5 * x) + 0.5


def scan_states(
    j, n_read, bounds_ref, readers_ref, xz_ref, bc_ref, step_ref, conv_ref, head_ref, bconv_ref,
    tail, bpad, b_in, c_in, inner, start, cum, stp, wt, states, send,
):
    f32, bf16 = jnp.float32, jnp.bfloat16
    heads = head_ref.shape[0]
    sec = xz_ref.shape[1]
    n_blk = sec // CH
    first = j * n_blk
    taps = 4

    @pl.when(j == 0)
    def _():
        tail[...] = jnp.zeros_like(tail)
        bpad[0:8, :] = jnp.zeros((8, 2 * N), f32)
        start[0] = jnp.zeros(start.shape[1:], f32)

    bpad[8 : 8 + sec, :] = bc_ref[...].astype(f32)
    for i in range(n_blk):
        y = jnp.broadcast_to(bconv_ref[taps : taps + 1, :], (CH, 2 * N))
        for k in range(taps):
            y = y + bconv_ref[k : k + 1, :] * bpad[i * CH + 5 + k : i * CH + 5 + k + CH, :]
        y = (y * sigmoid(y)).astype(bf16)
        b_in[first + i] = y[:, :N]
        c_in[first + i] = y[:, N:]
    bpad[0:8, :] = bpad[sec : sec + 8, :]

    def conv_strip(i, carry):
        row = pl.multiple_of(i * 32, 32)
        src = pl.multiple_of((i // 2) * 128 + (i % 2) * 32, 32)
        raw = xz_ref[pl.ds(src, 32), :]
        both = jnp.concatenate([tail[pl.ds(row, 32), :], raw], axis=1).astype(f32)
        w = conv_ref[pl.ds(row, 32), :]
        y = w[:, 4:5] + w[:, 3:4] * both[:, 128:]
        for d in range(1, taps):
            y = y + w[:, 3 - d : 4 - d] * pltpu.roll(both, d, 1)[:, 128:]
        y = (y * sigmoid(y)).astype(bf16)
        for b in range(n_blk):
            inner[first + b, pl.ds(row, 32), :] = y[:, b * CH : (b + 1) * CH]
        tail[pl.ds(row, 32), :] = raw[:, sec - 128 :]
        return carry

    lax.fori_loop(0, heads * 2, conv_strip, 0, unroll=2)

    raw = step_ref[...] + head_ref[:, 0:1]
    size = jnp.maximum(raw, 0.0) + jnp.log1p(jnp.exp(-jnp.abs(raw)))
    total = (-LOG2E * jnp.exp(head_ref[:, 1:2])) * size
    lane = lax.broadcasted_iota(jnp.int32, (heads, sec), 1) % CH
    d = 1
    while d < CH:
        total = total + jnp.where(lane >= d, pltpu.roll(total, d, 1), 0.0)
        d *= 2
    for b in range(n_blk):
        cum[first + b] = total[:, b * CH : (b + 1) * CH]
        stp[first + b] = size[:, b * CH : (b + 1) * CH]

    def one_block(i, carry):
        b = first + i
        a = cum[b]
        last = a[:, CH - 1 : CH]
        w = jnp.exp2(last - a) * stp[b]
        keep = jnp.exp2(last)
        for h in range(heads):
            rows = slice(h * 64, (h + 1) * 64)
            wt[0, rows, :] = (inner[b, rows, :].astype(f32) * w[h : h + 1, :]).astype(bf16)
        added = jnp.dot(wt[0], b_in[b], preferred_element_type=f32)
        for h in range(heads):
            rows = slice(h * 64, (h + 1) * 64)
            start[b + 1, rows, :] = start[b, rows, :] * keep[h : h + 1, :] + added[rows, :]
        return carry

    lax.fori_loop(0, n_blk, one_block, 0)

    lane_b = lax.broadcasted_iota(jnp.int32, (heads, CH), 1)

    def one_bound(k, carry):
        r = (lax.axis_index("heads") + n_read // 2 + k) % n_read
        q = jnp.int32(0)
        for i in range(n_read):
            q = q + jnp.where(readers_ref[j * n_read + i] == r, bounds_ref[j * n_read + i], 0)
        b = q // CH
        off = q % CH
        a = cum[b]
        at = jnp.sum(jnp.where(lane_b == off, a, 0.0), axis=1, keepdims=True)
        w = jnp.where(lane_b <= off, jnp.exp2(jnp.minimum(at - a, 0.0)), 0.0) * stp[b]
        keep = jnp.exp2(at)
        slot = k % 2
        for h in range(heads):
            rows = slice(h * 64, (h + 1) * 64)
            wt[slot, rows, :] = (inner[b, rows, :].astype(f32) * w[h : h + 1, :]).astype(bf16)
        inside = jnp.dot(wt[slot], b_in[b], preferred_element_type=f32)
        for h in range(heads):
            rows = slice(h * 64, (h + 1) * 64)
            states[r, j, rows, :] = (start[b, rows, :] * keep[h : h + 1, :] + inside[rows, :]).astype(bf16)
        send(r)
        return carry

    lax.fori_loop(0, n_read, one_bound, 0)


def scan_outputs(j, xz_ref, head_ref, b_in, c_in, inner, start, cum, stp, scores, mix, outer, gated_t, gated):
    f32, bf16 = jnp.float32, jnp.bfloat16
    heads = head_ref.shape[0]
    n_blk = xz_ref.shape[1] // CH
    row_id = lax.broadcasted_iota(jnp.int32, (CH, CH), 0)
    col_id = lax.broadcasted_iota(jnp.int32, (CH, CH), 1)
    eye = (row_id == col_id).astype(bf16)

    @pl.when(j == 0)
    def _():
        mix[...] = jnp.zeros_like(mix)

    def one_block(i, carry):
        b = j * n_blk + i
        lanes = pl.ds(pl.multiple_of(i * CH, CH), CH)
        scores[...] = jnp.where(
            row_id <= col_id,
            lax.dot_general(b_in[b], c_in[b], NT, preferred_element_type=f32), 0.0)
        outer[...] = lax.dot_general(start[b].astype(bf16), c_in[b], NT, preferred_element_type=f32)
        a = cum[b]
        s = stp[b]
        a_col = jnp.transpose(jnp.concatenate([a, jnp.zeros((128 - heads, CH), f32)], axis=0))
        grow = jnp.exp2(a)
        for h in range(heads):
            rows = slice(h * 64, (h + 1) * 64)
            m = h % mix.shape[0]
            a_h = a[h : h + 1, :]
            for s0 in range(0, CH, 32):
                lo = (s0 // 128) * 128
                col = a_col[s0 : s0 + 32, h : h + 1]
                gap = jnp.minimum(a_h[:, lo:] - col, 0.0)
                mix[m, s0 : s0 + 32, lo:] = (jnp.exp2(gap) * scores[s0 : s0 + 32, lo:]).astype(bf16)
            x = inner[b, rows, :].astype(f32)
            intra = jnp.dot((x * s[h : h + 1, :]).astype(bf16), mix[m], preferred_element_type=f32)
            gate = xz_ref[h * 128 + 64 : (h + 1) * 128, lanes].astype(f32)
            ssd = intra + outer[rows, :] * grow[h : h + 1, :] + head_ref[h : h + 1, 2:3] * x
            gated_t[rows, :] = (ssd * (gate * sigmoid(gate))).astype(bf16)
        span = min(heads * 64, CH)
        for c in range(0, heads * 64, span):
            out = lax.dot_general(eye, gated_t[c : c + span, :], NT, preferred_element_type=f32)
            gated[j, lanes, c : c + span] = out.astype(bf16)
        return carry

    lax.fori_loop(0, n_blk, one_block, 0)


def scan_kernel(n_read, with_norm, *refs):
    (bounds_ref, readers_ref, xz_ref, bc_ref, step_ref, conv_ref, conv_bias_ref, head_ref, bconv_ref, bconv_bias_ref, gain_ref,
     result, handoff) = refs[:13]
    (tail, bpad, b_in, c_in, inner, start, cum, stp, wt, states, scores, mix, outer, gated_t, gated,
     state_send, state_recv, state_here, gated_send, gated_recv, gated_here, out_sem, conv_cols, head_cols, bconv) = refs[13:38]
    landing, normed = refs[38:] if with_norm else (result, None)
    sections, line = lax.axis_size("seq"), lax.axis_size("heads")
    s, z = lax.axis_index("seq"), lax.axis_index("heads")
    sub = line // sections
    j = pl.program_id(0)
    size = states.shape[2]
    to_sec = z // sub
    row = (z % sub) * sections + s

    def prepare():
        heads = head_cols.shape[0]
        taps, width = 4, heads * 64
        cols = pl.ds(pl.multiple_of(s * width, 128), width)
        stack = jnp.concatenate(
            [conv_ref[:, cols], conv_bias_ref[:, cols], jnp.zeros((123, width), jnp.float32)], axis=0)
        conv_cols[...] = jnp.transpose(stack)
        turned = jnp.transpose(head_ref[...])
        head_cols[...] = pltpu.roll(turned, (128 - s * heads) % 128, 0)[0:heads, :]
        group = (z * heads * sections + s * heads) // PER_GROUP
        lanes = pl.ds(pl.multiple_of(group * 2 * N, 2 * N), 2 * N)
        bconv[0:taps, :] = bconv_ref[:, lanes]
        bconv[taps : taps + 1, :] = bconv_bias_ref[:, lanes]

    def place(at, sec):
        return handoff.at[sec, pl.ds(pl.multiple_of(at * size, size), size)]

    def state_copy(r, sec):
        return pltpu.make_async_remote_copy(
            src_ref=states.at[r, sec], dst_ref=place(row, sec), send_sem=state_send.at[r, sec],
            recv_sem=state_recv.at[row, sec], device_id={"seq": to_sec, "heads": r}, device_id_type=MESH)

    def state_keep(sec):
        return pltpu.make_async_copy(states.at[z, sec], place(row, sec), state_here.at[sec])

    def gated_copy(sec, source):
        return pltpu.make_async_remote_copy(
            src_ref=gated.at[sec], dst_ref=landing.at[source], send_sem=gated_send.at[sec],
            recv_sem=gated_recv.at[source], device_id={"seq": sec}, device_id_type=MESH)

    gated_keep = lambda: pltpu.make_async_copy(gated.at[s], landing.at[s], gated_here.at[0])
    mine_too = to_sec == s

    @pl.when(j == 0)
    def _():
        prepare()
        barrier = pltpu.get_barrier_semaphore()
        for sec in range(sections):
            for k in range(sub):
                h = s * sub + k

                @pl.when((sec != s) | (h != z))
                def _():
                    pl.semaphore_signal(barrier, inc=1, device_id={"seq": sec, "heads": h}, device_id_type=MESH)

            @pl.when(sec != s)
            def _():
                pl.semaphore_signal(barrier, inc=1, device_id={"seq": sec}, device_id_type=MESH)

        pl.semaphore_wait(barrier, line + sections - 1 - mine_too.astype(jnp.int32))

    def send(r):
        @pl.when(mine_too & (r == z))
        def _():
            state_keep(j).start()

        @pl.when(jnp.logical_not(mine_too & (r == z)))
        def _():
            state_copy(r, j).start()

    scan_states(
        j, n_read, bounds_ref, readers_ref, xz_ref, bc_ref, step_ref, conv_cols, head_cols, bconv,
        tail, bpad, b_in, c_in, inner, start, cum, stp, wt, states, send)
    scan_outputs(j, xz_ref, head_cols, b_in, c_in, inner, start, cum, stp, scores, mix, outer, gated_t, gated)

    @pl.when(j == s)
    def _():
        gated_keep().start()

    @pl.when(j != s)
    def _():
        gated_copy(j, s).start()

    @pl.when(j == sections - 1)
    def _():
        gated_keep().wait()
        for sec in range(sections):
            @pl.when(sec != s)
            def _():
                gated_copy(sec, sec).wait_recv()

        if with_norm:
            norm_rows(landing, gain_ref, normed, result, out_sem)

        def drain(n, carry):
            r, sec = n // sections, n % sections

            @pl.when(jnp.logical_not(mine_too & (r == z)))
            def _():
                state_copy(r, sec).wait_send()

            return carry

        lax.fori_loop(0, n_read * sections, drain, 0)

        @pl.when(mine_too)
        def _():
            for sec in range(sections):
                state_keep(sec).wait()

        def arrive(n, carry):
            at, sec = n // sections, n % sections
            here = mine_too & (at == row)

            @pl.when(jnp.logical_not(here))
            def _():
                pltpu.make_async_remote_copy(
                    src_ref=states.at[0, sec], dst_ref=place(at, sec), send_sem=state_send.at[0, sec],
                    recv_sem=state_recv.at[at, sec], device_id={"seq": to_sec}, device_id_type=MESH).wait_recv()

            return carry

        lax.fori_loop(0, sub * sections * sections, arrive, 0)
        for sec in range(sections):
            @pl.when(sec != s)
            def _():
                gated_copy(sec, s).wait_send()


def norm_rows(x_ref, gain_ref, normed, result, out_sem):
    sources, rows_all, width = x_ref.shape
    per = (PER_GROUP * P_SIZE) // width
    tiles = out_sem.shape[0]
    tile = rows_all // tiles

    def one(t, carry):
        rows = pl.ds(pl.multiple_of(t * tile, tile), tile)
        for g in range(sources // per):
            square = jnp.zeros((tile, 1), jnp.float32)
            for n in range(per):
                p = x_ref[g * per + n, rows, :].astype(jnp.float32)
                square = square + jnp.sum(p * p, axis=1, keepdims=True)
            scale = lax.rsqrt(square / (PER_GROUP * P_SIZE) + EPSILON)
            for n in range(per):
                cols = slice((g * per + n) * width, (g * per + n + 1) * width)
                p = x_ref[g * per + n, rows, :].astype(jnp.float32)
                normed[rows, cols] = (p * scale * gain_ref[:, cols]).astype(jnp.bfloat16)
        pltpu.make_async_copy(normed.at[rows], result.at[rows], out_sem.at[t]).start()
        return carry

    lax.fori_loop(0, tiles, one, 0)

    def wait(t, carry):
        rows = pl.ds(pl.multiple_of(t * tile, tile), tile)
        pltpu.make_async_copy(normed.at[rows], result.at[rows], out_sem.at[t]).wait()
        return carry

    lax.fori_loop(0, tiles, wait, 0)


def scan_call(xz_t, bc_raw, step_t, conv, conv_bias, head_rows, bconv, bconv_bias, gain, bounds, readers):
    sections, line = lax.axis_size("seq"), lax.axis_size("heads")
    heads = step_t.shape[0]
    length = xz_t.shape[1]
    sec = length // sections
    n_read = bounds.shape[0] // sections
    sub = line // sections
    n_blk, blocks = sec // CH, length // CH
    with_norm = sections * heads % PER_GROUP == 0
    f32, bf16 = jnp.float32, jnp.bfloat16
    dma = pltpu.SemaphoreType.DMA
    whole = lambda a: pl.BlockSpec(a.shape, lambda i: (0,) * a.ndim)
    smem = pl.BlockSpec(memory_space=pltpu.SMEM)
    hbm = pl.BlockSpec(memory_space=pl.ANY)
    width = heads * 64
    result = (sec, sections * width) if with_norm else (sections, sec, width)
    tiles = 16
    scratch = [
        pltpu.VMEM((width, 128), bf16),
        pltpu.VMEM((sec + 8, 2 * N), f32),
        pltpu.VMEM((blocks, CH, N), bf16),
        pltpu.VMEM((blocks, CH, N), bf16),
        pltpu.VMEM((blocks, width, CH), bf16),
        pltpu.VMEM((blocks + 1, width, N), f32),
        pltpu.VMEM((blocks, heads, CH), f32),
        pltpu.VMEM((blocks, heads, CH), f32),
        pltpu.VMEM((2, width, CH), bf16),
        pltpu.VMEM((n_read, sections, width, N), bf16),
        pltpu.VMEM((CH, CH), f32),
        pltpu.VMEM((4, CH, CH), bf16),
        pltpu.VMEM((width, CH), f32),
        pltpu.VMEM((width, CH), bf16),
        pltpu.VMEM((sections, sec, width), bf16),
        dma((n_read, sections)),
        dma((sub * sections, sections)),
        dma((sections,)),
        dma((sections,)),
        dma((sections,)),
        dma((1,)),
        dma((tiles,)),
        pltpu.VMEM((width, 128), f32),
        pltpu.VMEM((heads, 128), f32),
        pltpu.VMEM((8, 2 * N), f32),
    ]
    if with_norm:
        scratch += [pltpu.VMEM((sections, sec, width), bf16), pltpu.VMEM(result, bf16)]
    return pl.pallas_call(
        functools.partial(scan_kernel, n_read, with_norm),
        grid=(sections,),
        in_specs=[
            smem,
            smem,
            pl.BlockSpec((heads * 128, sec), lambda i: (0, i)),
            pl.BlockSpec((sec, 2 * N), lambda i: (i, 0)),
            pl.BlockSpec((heads, sec), lambda i: (0, i)),
            whole(conv),
            whole(conv_bias),
            whole(head_rows),
            whole(bconv),
            whole(bconv_bias),
            whole(gain),
        ],
        out_specs=[hbm, hbm],
        out_shape=[
            jax.ShapeDtypeStruct(result, bf16),
            jax.ShapeDtypeStruct((sections, sub * sections * width, N), bf16),
        ],
        scratch_shapes=scratch,
        compiler_params=pltpu.CompilerParams(
            collective_id=1, has_side_effects=True, vmem_limit_bytes=56 * 1024 * 1024),
        cost_estimate=pl.CostEstimate(flops=10_000_000_000, bytes_accessed=30_000_000, transcendentals=0),
        name="scan",
    )(bounds, readers, xz_t, bc_raw, step_t, conv, conv_bias, head_rows, bconv, bconv_bias, gain)


def fast_shards(
    tokens,
    xz_weight,
    bc_weight,
    step_weight,
    step_bias,
    decay_log,
    skip_gain,
    conv_weight,
    conv_bias,
    bc_conv_weight,
    bc_conv_bias,
    norm_gain,
    step_bounds,
    readers,
):
    head_devices = lax.axis_size("heads")
    sections = lax.axis_size("seq")
    section = lax.axis_index("seq")
    head_block = lax.axis_index("heads")
    block_heads = H // head_devices
    mine = block_heads // sections
    first_mine = section * mine
    group = (head_block * block_heads + first_mine) // PER_GROUP
    own = lambda a, width, axis: lax.dynamic_slice_in_dim(a, first_mine * width, mine * width, axis)
    head_rows = jnp.pad(jnp.stack([step_bias, decay_log, skip_gain]), ((0, 125), (0, 128 - block_heads)))

    if head_devices == 4 and sections == 4:
        xz_t, bc_raw, step_t = gather_project(tokens, xz_weight, bc_weight, step_weight, mine)
    else:
        small_step = own(step_weight, 1, 1)
        xz_t, bc_raw, step_t = project_parts(tokens, xz_weight, bc_weight, small_step, group)

    result, handoff = scan_call(
        xz_t, bc_raw, step_t, conv_weight, conv_bias[None], head_rows, bc_conv_weight, bc_conv_bias[None],
        norm_gain[None], step_bounds, readers)
    if block_heads % PER_GROUP == 0:
        mixed, handoff = place_results(result, handoff.reshape(-1, N))
    else:
        mixed = norm_split(result, norm_gain)
    return (mixed, handoff.reshape(1, sections, -1, P_SIZE, N))


def place_results(mixed, handoff):
    def kernel(a_ref, b_ref, a_out, b_out):
        a_out[...] = a_ref[...]
        b_out[...] = b_ref[...]

    parts = 4
    specs = [pl.BlockSpec((a.shape[0] // parts, a.shape[1]), lambda i: (i, 0)) for a in (mixed, handoff)]
    return pl.pallas_call(
        kernel,
        grid=(parts,),
        in_specs=specs,
        out_specs=specs,
        out_shape=[jax.ShapeDtypeStruct(a.shape, a.dtype) for a in (mixed, handoff)],
        compiler_params=pltpu.CompilerParams(vmem_limit_bytes=62 * 1024 * 1024),
        name="place_results",
    )(mixed, handoff)


def project_parts(tokens, xz_weight, bc_weight, step_weight, group):
    head_block = lax.axis_index("heads")
    width_bc = bc_weight.shape[1]
    whole_group = width_bc >= 2 * N
    if whole_group:
        bc_weight = lax.dynamic_slice_in_dim(bc_weight, group * 2 * N - head_block * width_bc, 2 * N, 1)
    bc_width = bc_weight.shape[1]
    xz, small = project(tokens, xz_weight, jnp.concatenate([bc_weight, step_weight], axis=1), 4)
    bc_raw = small[:, :bc_width].astype(jnp.bfloat16)
    if not whole_group:
        bc_raw = lax.all_gather(bc_raw, "heads", axis=1, tiled=True)
        bc_raw = lax.dynamic_slice_in_dim(bc_raw, group * 2 * N, 2 * N, 1)
    return jnp.transpose(xz), bc_raw, jnp.transpose(small[:, bc_width:])


def norm_split(gathered, gain):
    wide = jnp.moveaxis(gathered, 0, 1).reshape(gathered.shape[1], -1).astype(jnp.float32)
    first_group = lax.axis_index("heads") * wide.shape[1] // (PER_GROUP * P_SIZE)
    at_group = lax.broadcasted_iota(jnp.int32, (1, G), 1) == first_group
    square = jnp.sum(jnp.square(wide), axis=1, keepdims=True)
    square = lax.psum(jnp.where(at_group, square, 0.0), "heads")
    square = jnp.sum(jnp.where(at_group, square, 0.0), axis=1, keepdims=True)
    scale = lax.rsqrt(square / (PER_GROUP * P_SIZE) + EPSILON)
    return (wide * scale * gain[None]).astype(jnp.bfloat16)


def solution(mesh):
    in_specs = (
        P(("groups", "seq"), "heads"),
        P(None, ("heads", "seq")),
        P(None, "heads"),
        P(None, "heads"),
        P("heads"),
        P("heads"),
        P("heads"),
        P(None, "heads"),
        P("heads"),
        P(),
        P(),
        P("heads"),
        P("groups"),
        P("groups"),
    )
    out_specs = (P(("groups", "seq"), "heads"), P(("groups", "heads"), None, "seq", None, None))
    return jax.shard_map(fast_shards, mesh=mesh, in_specs=in_specs, out_specs=out_specs, check_vma=False)
```

```python
import functools

import jax
import jax.numpy as jnp
from jax import lax
from jax.experimental import pallas as pl
from jax.experimental.pallas import tpu as pltpu
from jax.sharding import PartitionSpec as P

H = 256
P_SIZE = 64
N = 128
G = 8
CH = 256
PER_GROUP = H // G
EPSILON = 1e-05


def project(tokens, xz_weight, small_weight, chunks):
    sections, head_devices = lax.axis_size("seq"), lax.axis_size("heads")
    rows = tokens.shape[0] // chunks
    width = tokens.shape[1]
    pieces = [tokens[c * rows : (c + 1) * rows] for c in range(chunks)]
    xz, small = [], []
    for c in range(chunks):
        part = lax.all_gather(pieces[c], ("seq", "heads"), axis=0)
        part = part.reshape(sections, head_devices, rows, width)
        dot = lambda w: lax.dot_general(
            part,
            w.reshape(head_devices, width, w.shape[1]),
            (((1, 3), (0, 1)), ((), ())),
            preferred_element_type=jnp.float32,
        )
        xz.append(dot(xz_weight).astype(jnp.bfloat16))
        small.append(dot(small_weight))
        if c + 2 < chunks:
            pieces[c + 2], xz[c], small[c] = lax.optimization_barrier(
                (pieces[c + 2], xz[c], small[c])
            )
    whole = lambda parts: jnp.concatenate(parts, axis=1).reshape(-1, parts[0].shape[-1])
    return whole(xz), whole(small)


MESH = pl.DeviceIdType.MESH
SPAN = 2048


def nearest_first(z, k, count):
    h = jnp.int32(0)
    for at in range(count):
        order = sorted(range(count), key=lambda q: (abs(q - at), min(q, count - 1 - q)))
        for i, q in enumerate(order):
            if q:
                h = h + jnp.where((z == at) & (k == i), q, 0)
    return h


def gather_project_kernel(
    pieces, tok, xw, bw, sw, xz_out, bc_out, st_out, every,
    wx, wb, ws, tile, ax, ab, ast, ox, ob, ost,
    recv, up_sem, down_sem, x_sem, c_sem, on_sem, w_sem, tile_sem, out_sem,
):
    f32, bf16 = jnp.float32, jnp.bfloat16
    s, z = lax.axis_index("seq"), lax.axis_index("heads")
    line = lax.axis_size("heads")
    other = (s + 2) % 4
    sib = s + 1 - 2 * (s % 2)
    far = (sib + 2) % 4
    rows_all, depth = tok.shape
    halves = pieces // 2
    rows = rows_all // halves
    strip = rows_all // pieces
    part = lambda p: pl.ds(pl.multiple_of(p * strip, strip), strip)
    half = lambda n: pl.ds(pl.multiple_of(n * rows, rows), rows)
    below, above = z > 0, z < line - 1

    barrier = pltpu.get_barrier_semaphore()
    for partner in (other, sib):
        pl.semaphore_signal(barrier, inc=1, device_id={"seq": partner}, device_id_type=MESH)

    @pl.when(above)
    def _():
        pl.semaphore_signal(barrier, inc=1, device_id={"heads": z + 1}, device_id_type=MESH)

    @pl.when(below)
    def _():
        pl.semaphore_signal(barrier, inc=1, device_id={"heads": z - 1}, device_id_type=MESH)

    pl.semaphore_wait(barrier, 2 + above.astype(jnp.int32) + below.astype(jnp.int32))

    def copy(src, sec, h, p, sem, to):
        return pltpu.make_async_remote_copy(
            src_ref=src, dst_ref=every.at[h, sec, part(p)], send_sem=sem, recv_sem=recv.at[sec, h, p],
            device_id=to, device_id_type=MESH,
        )

    held = lambda sec, h, p: every.at[h, sec, part(p)]
    go_up = lambda src, h, p: copy(src, s, h, p, up_sem.at[h, p], {"heads": z + 1})
    go_down = lambda src, h, p: copy(src, s, h, p, down_sem.at[h, p], {"heads": z - 1})
    go_x = lambda src, h, p: copy(src, s, h, p, x_sem.at[h, p], {"seq": other})
    go_c = lambda src, sec, i, h, p: copy(src, sec, h, p, c_sem.at[i, h, p], {"seq": sib})
    def by_line(h, p):
        return (p % 2 == 1) & (((h == line - 1) & (z != line - 1)) | ((h == 0) & (z != 0)))

    def go_on(end, n, p):
        return copy(held(other, end, p), other, end, p, on_sem.at[n, p], {"heads": z + 1 if end == 0 else z - 1})

    arrived = lambda sec, h, p: copy(held(sec, h, p), sec, h, p, x_sem.at[h, p], {"seq": other}).wait_recv()

    def weights(h, slot):
        src = pl.ds(pl.multiple_of(h * depth, depth), depth)
        return [
            pltpu.make_async_copy(xw.at[src], wx.at[slot], w_sem.at[slot, 0]),
            pltpu.make_async_copy(
                bw.at[src, pl.ds(pl.multiple_of((s // 2) * 2 * N, 2 * N), 2 * N)], wb.at[slot], w_sem.at[slot, 1]),
            pltpu.make_async_copy(sw.at[:, src], ws.at[slot], w_sem.at[slot, 2]),
        ]

    load = lambda src, b, n: pltpu.make_async_copy(src, tile.at[b, pl.ds(n * rows, rows)], tile_sem.at[b, n])

    def send_own(p):
        own = tok.at[part(p)]

        @pl.when(above)
        def _():
            go_up(own, z, p).start()

        @pl.when(below)
        def _():
            go_down(own, z, p).start()

        go_x(own, z, p).start()
        go_c(own, s, 0, z, p).start()

    for p in range(pieces):
        send_own(p)
    for k in range(2):
        for c in weights(nearest_first(z, k, line), k):
            c.start()

    ab[...] = jnp.zeros_like(ab)
    ast[...] = jnp.zeros_like(ast)

    def clear(i, carry):
        ax[i // 8, pl.ds(pl.multiple_of((i % 8) * (rows_all // 8), rows_all // 8), rows_all // 8), :] = jnp.zeros(
            (rows_all // 8, ax.shape[2]), f32)
        return carry

    lax.fori_loop(0, 4 * 8, clear, 0)

    wide = min(256, ax.shape[2])
    span = min(SPAN, ax.shape[2])

    def multiply(b, slot, pair, p, first=0, between=None):
        block = pl.ds(first * rows, len(pair) * rows)

        def add(acc, w, cols, turned=False):
            dims = NT if turned else (((1,), (0,)), ((), ()))
            both = lax.dot_general(tile[b, block, :], w, dims, preferred_element_type=f32)
            for n, sec in enumerate(pair):
                acc[sec, half(p), cols] += both[n * rows : (n + 1) * rows]

        def one(n, carry):
            cols = pl.ds(pl.multiple_of(n * span, span), span)
            add(ax, wx[slot, :, cols], cols)
            return carry

        lax.fori_loop(0, ax.shape[2] // span, one, 0)
        if between is not None:
            between()
        add(ab, wb[slot], slice(None))
        add(ast, ws[slot], slice(0, ws.shape[1]), True)

    mine = st_out.shape[0]
    eye = (
        lax.broadcasted_iota(jnp.int32, (wide, wide), 0) == lax.broadcasted_iota(jnp.int32, (wide, wide), 1)
    ).astype(bf16)

    def results(q, sec, p):
        at = pl.ds(pl.multiple_of(sec * rows_all + p * rows, rows), rows)
        return [
            pltpu.make_async_copy(ox.at[q], xz_out.at[:, at], out_sem.at[q, 0]),
            pltpu.make_async_copy(ob.at[q], bc_out.at[at], out_sem.at[q, 1]),
            pltpu.make_async_copy(
                ost.at[q, pl.ds(pl.multiple_of(s * mine, 8), mine)], st_out.at[:, at], out_sem.at[q, 2]),
        ]

    def finish(q, sec, p):
        def one(n, carry):
            cols = pl.ds(pl.multiple_of(n * wide, wide), wide)
            block = ax[sec, half(p), cols].astype(bf16)
            turned = lax.dot_general(eye, block, NT, preferred_element_type=f32)
            ox[q, cols, :] = turned.astype(bf16)
            return carry

        lax.fori_loop(0, ax.shape[2] // wide, one, 0, unroll=True)
        ob[q] = ab[sec, half(p), :].astype(bf16)
        ost[q] = jnp.transpose(ast[sec, half(p), :])
        for c in results(q, sec, p):
            c.start()

    def step(i, carry):
        u, n = i // halves, i % halves
        h_new = nearest_first(z, u, line)
        h_old = nearest_first(z, u - 1, line)
        new, old = u < line, u >= 1
        rows_of = lambda sec, h: every.at[h, sec, half(n)]

        def pass_on(p):
            for turn in (1, -1):
                sign = turn * jnp.where(2 * z < line, -1, 1)
                h = z + sign * u

                @pl.when((u >= 1) & (h >= 0) & (h < line))
                def _():
                    arrived(s, h, p)
                    src = held(s, h, p)

                    @pl.when((sign < 0) & above)
                    def _():
                        go_up(src, h, p).start()

                    @pl.when((sign > 0) & below)
                    def _():
                        go_down(src, h, p).start()

                    @pl.when(jnp.logical_not(by_line(h, p)))
                    def _():
                        go_x(src, h, p).start()

                    go_c(src, s, 0, h, p).start()

            @pl.when(old & jnp.logical_not(by_line(h_old, p)))
            def _():
                arrived(other, h_old, p)
                go_c(held(other, h_old, p), other, 1, h_old, p).start()

            for end, at, on, sem in ((line - 1, line - z, below, 1), (0, z + 1, above, 0)):
                @pl.when((u == jnp.where(z == end, 1, at)) & (p % 2 == 1))
                def _():
                    @pl.when(z != end)
                    def _():
                        arrived(other, end, p)
                        go_c(held(other, end, p), other, 1, end, p).start()

                    @pl.when(on)
                    def _():
                        go_on(end, sem, p).start()

        def pass_two(m, carry):
            pass_on(2 * n + m)
            return carry

        lax.fori_loop(0, 2, pass_two, 0)

        @pl.when(u == 0)
        def _():
            load(tok.at[half(n)], 0, 0).start()

        @pl.when(new & old)
        def _():
            load(rows_of(s, h_new), 0, 0).start()

        @pl.when(old)
        def _():
            load(rows_of(other, h_old), 1, 0).start()

        @pl.when(new & (n == 0))
        def _():
            for c in weights(h_new, u % 2):
                c.wait()

        def take_far():
            for m in range(2):
                arrived(far, h_old, 2 * n + m)
            load(rows_of(far, h_old), 1, 1).start()

        pl.when(old & new)(take_far)

        @pl.when(new)
        def _():
            for m in range(2):
                arrived(sib, h_new, 2 * n + m)
            load(rows_of(sib, h_new), 0, 1).start()
            for m in range(2):
                load(rows_of(sib, h_new), 0, m).wait()
            multiply(0, u % 2, (s, sib), n)

        @pl.when(old & new)
        def _():
            for m in range(2):
                load(rows_of(far, h_old), 1, m).wait()
            multiply(1, (u - 1) % 2, (other, far), n)

        @pl.when(jnp.logical_not(new))
        def _():
            load(rows_of(other, h_old), 1, 0).wait()
            multiply(1, (u - 1) % 2, (other,), n, 0, take_far)
            load(rows_of(far, h_old), 1, 1).wait()
            multiply(1, (u - 1) % 2, (far,), n, 1)

        @pl.when(old & (u < line - 1) & (n == halves - 1))
        def _():
            for c in weights(nearest_first(z, u + 1, line), (u + 1) % 2):
                c.start()

        @pl.when(u >= line - 1)
        def _():
            last = u == line
            first_sec, second_sec = jnp.where(last, other, s), jnp.where(last, far, sib)

            def one(q, carry):
                sec = jnp.where(q == 0, first_sec, second_sec)

                @pl.when(i > (line - 1) * halves)
                def _():
                    for c in results(q, sec, n):
                        c.wait()

                finish(q, sec, n)
                return carry

            lax.fori_loop(0, 2, one, 0)

        return carry

    lax.fori_loop(0, (line + 1) * halves, step, 0)

    for q in range(2):
        for c in results(q, s, 0):
            c.wait()

    def drain(i, carry):
        h, p = i // pieces, i % pieces
        src = held(s, h, p)

        @pl.when(above & (h <= z))
        def _():
            go_up(src, h, p).wait_send()

        @pl.when(below & (h >= z))
        def _():
            go_down(src, h, p).wait_send()

        @pl.when(jnp.logical_not(by_line(h, p)))
        def _():
            go_x(src, h, p).wait_send()

        go_c(src, s, 0, h, p).wait_send()
        go_c(src, s, 1, h, p).wait_send()
        return carry

    lax.fori_loop(0, line * pieces, drain, 0)

    for p in range(1, pieces, 2):
        @pl.when(above)
        def _():
            go_on(0, 0, p).wait_send()

        @pl.when(below)
        def _():
            go_on(line - 1, 1, p).wait_send()


def gather_project(tokens, xz_weight, bc_weight, step_weight, mine):
    pieces = 4
    sections, line = lax.axis_size("seq"), lax.axis_size("heads")
    rows_all, depth = tokens.shape
    rows = rows_all // (pieces // 2)
    width = xz_weight.shape[1]
    steps = step_weight.shape[1]
    length = rows_all * sections
    f32, bf16 = jnp.float32, jnp.bfloat16
    hbm = pl.BlockSpec(memory_space=pl.ANY)
    dma = pltpu.SemaphoreType.DMA
    wide = min(256, width)
    flops = 2 * length * depth * line * (width + 2 * N + steps)
    return pl.pallas_call(
        functools.partial(gather_project_kernel, pieces),
        in_specs=[hbm] * 4,
        out_specs=[hbm] * 4,
        out_shape=[
            jax.ShapeDtypeStruct((width, length), bf16),
            jax.ShapeDtypeStruct((length, 2 * N), bf16),
            jax.ShapeDtypeStruct((mine, length), f32),
            jax.ShapeDtypeStruct((line, sections, rows_all, depth), bf16),
        ],
        scratch_shapes=[
            pltpu.VMEM((2, depth, width), bf16),
            pltpu.VMEM((2, depth, 2 * N), bf16),
            pltpu.VMEM((2, steps, depth), bf16),
            pltpu.VMEM((2, 2 * rows, depth), bf16),
            pltpu.VMEM((sections, rows_all, width), f32),
            pltpu.VMEM((sections, rows_all, 2 * N), f32),
            pltpu.VMEM((sections, rows_all, 128), f32),
            pltpu.VMEM((2, width, rows), bf16),
            pltpu.VMEM((2, rows, 2 * N), bf16),
            pltpu.VMEM((2, 128, rows), f32),
            dma((sections, line, pieces)),
            dma((line, pieces)),
            dma((line, pieces)),
            dma((line, pieces)),
            dma((2, line, pieces)),
            dma((2, pieces)),
            dma((2, 3)),
            dma((2, 2)),
            dma((2, 3)),
        ],
        compiler_params=pltpu.CompilerParams(
            collective_id=0, has_side_effects=True, vmem_limit_bytes=60 * 1024 * 1024),
        cost_estimate=pl.CostEstimate(flops=flops, bytes_accessed=100_000_000, transcendentals=0),
        name="gather_project",
    )(tokens, xz_weight, bc_weight, jnp.transpose(step_weight))[:3]


LOG2E = 1.4426950408889634
NT = (((1,), (1,)), ((), ()))


def sigmoid(x):
    return 0.5 * jnp.tanh(0.5 * x) + 0.5


def scan_states(
    j, n_read, bounds_ref, readers_ref, xz_ref, bc_ref, step_ref, conv_ref, head_ref, bconv_ref,
    tail, bpad, b_in, c_in, inner, start, cum, stp, wt, states, send,
):
    f32, bf16 = jnp.float32, jnp.bfloat16
    heads = head_ref.shape[0]
    sec = xz_ref.shape[1]
    n_blk = sec // CH
    first = j * n_blk
    taps = 4

    @pl.when(j == 0)
    def _():
        tail[...] = jnp.zeros_like(tail)
        bpad[0:8, :] = jnp.zeros((8, 2 * N), f32)
        start[0] = jnp.zeros(start.shape[1:], f32)

    bpad[8 : 8 + sec, :] = bc_ref[...].astype(f32)
    for i in range(n_blk):
        y = jnp.broadcast_to(bconv_ref[taps : taps + 1, :], (CH, 2 * N))
        for k in range(taps):
            y = y + bconv_ref[k : k + 1, :] * bpad[i * CH + 5 + k : i * CH + 5 + k + CH, :]
        y = (y * sigmoid(y)).astype(bf16)
        b_in[first + i] = y[:, :N]
        c_in[first + i] = y[:, N:]
    bpad[0:8, :] = bpad[sec : sec + 8, :]

    def conv_strip(i, carry):
        row = pl.multiple_of(i * 32, 32)
        src = pl.multiple_of((i // 2) * 128 + (i % 2) * 32, 32)
        raw = xz_ref[pl.ds(src, 32), :]
        both = jnp.concatenate([tail[pl.ds(row, 32), :], raw], axis=1).astype(f32)
        w = conv_ref[pl.ds(row, 32), :]
        y = w[:, 4:5] + w[:, 3:4] * both[:, 128:]
        for d in range(1, taps):
            y = y + w[:, 3 - d : 4 - d] * pltpu.roll(both, d, 1)[:, 128:]
        y = (y * sigmoid(y)).astype(bf16)
        for b in range(n_blk):
            inner[first + b, pl.ds(row, 32), :] = y[:, b * CH : (b + 1) * CH]
        tail[pl.ds(row, 32), :] = raw[:, sec - 128 :]
        return carry

    lax.fori_loop(0, heads * 2, conv_strip, 0, unroll=4)

    raw = step_ref[...] + head_ref[:, 0:1]
    size = jnp.maximum(raw, 0.0) + jnp.log1p(jnp.exp(-jnp.abs(raw)))
    total = (-LOG2E * jnp.exp(head_ref[:, 1:2])) * size
    lane = lax.broadcasted_iota(jnp.int32, (heads, sec), 1) % CH
    d = 1
    while d < CH:
        total = total + jnp.where(lane >= d, pltpu.roll(total, d, 1), 0.0)
        d *= 2
    for b in range(n_blk):
        cum[first + b] = total[:, b * CH : (b + 1) * CH]
        stp[first + b] = size[:, b * CH : (b + 1) * CH]

    def one_block(i, carry):
        b = first + i
        a = cum[b]
        last = a[:, CH - 1 : CH]
        w = jnp.exp2(last - a) * stp[b]
        keep = jnp.exp2(last)
        for h in range(heads):
            rows = slice(h * 64, (h + 1) * 64)
            wt[0, rows, :] = (inner[b, rows, :].astype(f32) * w[h : h + 1, :]).astype(bf16)
        added = jnp.dot(wt[0], b_in[b], preferred_element_type=f32)
        for h in range(heads):
            rows = slice(h * 64, (h + 1) * 64)
            start[b + 1, rows, :] = start[b, rows, :] * keep[h : h + 1, :] + added[rows, :]
        return carry

    lax.fori_loop(0, n_blk, one_block, 0)

    lane_b = lax.broadcasted_iota(jnp.int32, (heads, CH), 1)

    def one_bound(k, carry):
        r = (lax.axis_index("heads") + n_read // 2 + k) % n_read
        q = jnp.int32(0)
        for i in range(n_read):
            q = q + jnp.where(readers_ref[j * n_read + i] == r, bounds_ref[j * n_read + i], 0)
        b = q // CH
        off = q % CH
        a = cum[b]
        at = jnp.sum(jnp.where(lane_b == off, a, 0.0), axis=1, keepdims=True)
        w = jnp.where(lane_b <= off, jnp.exp2(jnp.minimum(at - a, 0.0)), 0.0) * stp[b]
        keep = jnp.exp2(at)
        slot = k % 2
        for h in range(heads):
            rows = slice(h * 64, (h + 1) * 64)
            wt[slot, rows, :] = (inner[b, rows, :].astype(f32) * w[h : h + 1, :]).astype(bf16)
        inside = jnp.dot(wt[slot], b_in[b], preferred_element_type=f32)
        for h in range(heads):
            rows = slice(h * 64, (h + 1) * 64)
            states[r, j, rows, :] = (start[b, rows, :] * keep[h : h + 1, :] + inside[rows, :]).astype(bf16)
        send(r)
        return carry

    lax.fori_loop(0, n_read, one_bound, 0)


def scan_outputs(j, xz_ref, head_ref, b_in, c_in, inner, start, cum, stp, scores, mix, outer, gated_t, gated):
    f32, bf16 = jnp.float32, jnp.bfloat16
    heads = head_ref.shape[0]
    n_blk = xz_ref.shape[1] // CH
    row_id = lax.broadcasted_iota(jnp.int32, (CH, CH), 0)
    col_id = lax.broadcasted_iota(jnp.int32, (CH, CH), 1)
    eye = (row_id == col_id).astype(bf16)

    @pl.when(j == 0)
    def _():
        mix[...] = jnp.zeros_like(mix)

    def one_block(i, carry):
        b = j * n_blk + i
        lanes = pl.ds(pl.multiple_of(i * CH, CH), CH)
        scores[...] = jnp.where(
            row_id <= col_id,
            lax.dot_general(b_in[b], c_in[b], NT, preferred_element_type=f32), 0.0)
        outer[...] = lax.dot_general(start[b].astype(bf16), c_in[b], NT, preferred_element_type=f32)
        a = cum[b]
        s = stp[b]
        a_col = jnp.transpose(jnp.concatenate([a, jnp.zeros((128 - heads, CH), f32)], axis=0))
        grow = jnp.exp2(a)
        for h in range(heads):
            rows = slice(h * 64, (h + 1) * 64)
            m = h % mix.shape[0]
            a_h = a[h : h + 1, :]
            for s0 in range(0, CH, 32):
                lo = (s0 // 128) * 128
                col = a_col[s0 : s0 + 32, h : h + 1]
                gap = jnp.minimum(a_h[:, lo:] - col, 0.0)
                mix[m, s0 : s0 + 32, lo:] = (jnp.exp2(gap) * scores[s0 : s0 + 32, lo:]).astype(bf16)
            x = inner[b, rows, :].astype(f32)
            intra = jnp.dot((x * s[h : h + 1, :]).astype(bf16), mix[m], preferred_element_type=f32)
            gate = xz_ref[h * 128 + 64 : (h + 1) * 128, lanes].astype(f32)
            ssd = intra + outer[rows, :] * grow[h : h + 1, :] + head_ref[h : h + 1, 2:3] * x
            gated_t[rows, :] = (ssd * (gate * sigmoid(gate))).astype(bf16)
        span = min(heads * 64, CH)
        for c in range(0, heads * 64, span):
            out = lax.dot_general(eye, gated_t[c : c + span, :], NT, preferred_element_type=f32)
            gated[j, lanes, c : c + span] = out.astype(bf16)
        return carry

    lax.fori_loop(0, n_blk, one_block, 0)


def scan_kernel(n_read, with_norm, *refs):
    (bounds_ref, readers_ref, xz_ref, bc_ref, step_ref, conv_ref, conv_bias_ref, head_ref, bconv_ref, bconv_bias_ref, gain_ref,
     result, handoff) = refs[:13]
    (tail, bpad, b_in, c_in, inner, start, cum, stp, wt, states, scores, mix, outer, gated_t, gated,
     state_send, state_recv, state_here, gated_send, gated_recv, gated_here, out_sem, conv_cols, head_cols, bconv) = refs[13:38]
    landing, normed = refs[38:] if with_norm else (result, None)
    sections, line = lax.axis_size("seq"), lax.axis_size("heads")
    s, z = lax.axis_index("seq"), lax.axis_index("heads")
    sub = line // sections
    j = pl.program_id(0)
    size = states.shape[2]
    to_sec = z // sub
    row = (z % sub) * sections + s

    def prepare():
        heads = head_cols.shape[0]
        taps, width = 4, heads * 64
        cols = pl.ds(pl.multiple_of(s * width, 128), width)
        stack = jnp.concatenate(
            [conv_ref[:, cols], conv_bias_ref[:, cols], jnp.zeros((123, width), jnp.float32)], axis=0)
        conv_cols[...] = jnp.transpose(stack)
        turned = jnp.transpose(head_ref[...])
        head_cols[...] = pltpu.roll(turned, (128 - s * heads) % 128, 0)[0:heads, :]
        group = (z * heads * sections + s * heads) // PER_GROUP
        lanes = pl.ds(pl.multiple_of(group * 2 * N, 2 * N), 2 * N)
        bconv[0:taps, :] = bconv_ref[:, lanes]
        bconv[taps : taps + 1, :] = bconv_bias_ref[:, lanes]

    def place(at, sec):
        return handoff.at[sec, pl.ds(pl.multiple_of(at * size, size), size)]

    def state_copy(r, sec):
        return pltpu.make_async_remote_copy(
            src_ref=states.at[r, sec], dst_ref=place(row, sec), send_sem=state_send.at[r, sec],
            recv_sem=state_recv.at[row, sec], device_id={"seq": to_sec, "heads": r}, device_id_type=MESH)

    def state_keep(sec):
        return pltpu.make_async_copy(states.at[z, sec], place(row, sec), state_here.at[sec])

    def gated_copy(sec, source):
        return pltpu.make_async_remote_copy(
            src_ref=gated.at[sec], dst_ref=landing.at[source], send_sem=gated_send.at[sec],
            recv_sem=gated_recv.at[source], device_id={"seq": sec}, device_id_type=MESH)

    gated_keep = lambda: pltpu.make_async_copy(gated.at[s], landing.at[s], gated_here.at[0])
    mine_too = to_sec == s

    @pl.when(j == 0)
    def _():
        prepare()
        barrier = pltpu.get_barrier_semaphore()
        for sec in range(sections):
            for k in range(sub):
                h = s * sub + k

                @pl.when((sec != s) | (h != z))
                def _():
                    pl.semaphore_signal(barrier, inc=1, device_id={"seq": sec, "heads": h}, device_id_type=MESH)

            @pl.when(sec != s)
            def _():
                pl.semaphore_signal(barrier, inc=1, device_id={"seq": sec}, device_id_type=MESH)

        pl.semaphore_wait(barrier, line + sections - 1 - mine_too.astype(jnp.int32))

    def send(r):
        @pl.when(mine_too & (r == z))
        def _():
            state_keep(j).start()

        @pl.when(jnp.logical_not(mine_too & (r == z)))
        def _():
            state_copy(r, j).start()

    scan_states(
        j, n_read, bounds_ref, readers_ref, xz_ref, bc_ref, step_ref, conv_cols, head_cols, bconv,
        tail, bpad, b_in, c_in, inner, start, cum, stp, wt, states, send)
    scan_outputs(j, xz_ref, head_cols, b_in, c_in, inner, start, cum, stp, scores, mix, outer, gated_t, gated)

    @pl.when(j == s)
    def _():
        gated_keep().start()

    @pl.when(j != s)
    def _():
        gated_copy(j, s).start()

    @pl.when(j == sections - 1)
    def _():
        gated_keep().wait()
        for sec in range(sections):
            @pl.when(sec != s)
            def _():
                gated_copy(sec, sec).wait_recv()

        if with_norm:
            norm_rows(landing, gain_ref, normed, result, out_sem)

        def drain(n, carry):
            r, sec = n // sections, n % sections

            @pl.when(jnp.logical_not(mine_too & (r == z)))
            def _():
                state_copy(r, sec).wait_send()

            return carry

        lax.fori_loop(0, n_read * sections, drain, 0)

        @pl.when(mine_too)
        def _():
            for sec in range(sections):
                state_keep(sec).wait()

        def arrive(n, carry):
            at, sec = n // sections, n % sections
            here = mine_too & (at == row)

            @pl.when(jnp.logical_not(here))
            def _():
                pltpu.make_async_remote_copy(
                    src_ref=states.at[0, sec], dst_ref=place(at, sec), send_sem=state_send.at[0, sec],
                    recv_sem=state_recv.at[at, sec], device_id={"seq": to_sec}, device_id_type=MESH).wait_recv()

            return carry

        lax.fori_loop(0, sub * sections * sections, arrive, 0)
        for sec in range(sections):
            @pl.when(sec != s)
            def _():
                gated_copy(sec, s).wait_send()


def norm_rows(x_ref, gain_ref, normed, result, out_sem):
    sources, rows_all, width = x_ref.shape
    per = (PER_GROUP * P_SIZE) // width
    tiles = out_sem.shape[0]
    tile = rows_all // tiles

    def one(t, carry):
        rows = pl.ds(pl.multiple_of(t * tile, tile), tile)
        for g in range(sources // per):
            square = jnp.zeros((tile, 1), jnp.float32)
            for n in range(per):
                p = x_ref[g * per + n, rows, :].astype(jnp.float32)
                square = square + jnp.sum(p * p, axis=1, keepdims=True)
            scale = lax.rsqrt(square / (PER_GROUP * P_SIZE) + EPSILON)
            for n in range(per):
                cols = slice((g * per + n) * width, (g * per + n + 1) * width)
                p = x_ref[g * per + n, rows, :].astype(jnp.float32)
                normed[rows, cols] = (p * scale * gain_ref[:, cols]).astype(jnp.bfloat16)
        pltpu.make_async_copy(normed.at[rows], result.at[rows], out_sem.at[t]).start()
        return carry

    lax.fori_loop(0, tiles, one, 0)

    def wait(t, carry):
        rows = pl.ds(pl.multiple_of(t * tile, tile), tile)
        pltpu.make_async_copy(normed.at[rows], result.at[rows], out_sem.at[t]).wait()
        return carry

    lax.fori_loop(0, tiles, wait, 0)


def scan_call(xz_t, bc_raw, step_t, conv, conv_bias, head_rows, bconv, bconv_bias, gain, bounds, readers):
    sections, line = lax.axis_size("seq"), lax.axis_size("heads")
    heads = step_t.shape[0]
    length = xz_t.shape[1]
    sec = length // sections
    n_read = bounds.shape[0] // sections
    sub = line // sections
    n_blk, blocks = sec // CH, length // CH
    with_norm = sections * heads % PER_GROUP == 0
    f32, bf16 = jnp.float32, jnp.bfloat16
    dma = pltpu.SemaphoreType.DMA
    whole = lambda a: pl.BlockSpec(a.shape, lambda i: (0,) * a.ndim)
    smem = pl.BlockSpec(memory_space=pltpu.SMEM)
    hbm = pl.BlockSpec(memory_space=pl.ANY)
    width = heads * 64
    result = (sec, sections * width) if with_norm else (sections, sec, width)
    tiles = 16
    scratch = [
        pltpu.VMEM((width, 128), bf16),
        pltpu.VMEM((sec + 8, 2 * N), f32),
        pltpu.VMEM((blocks, CH, N), bf16),
        pltpu.VMEM((blocks, CH, N), bf16),
        pltpu.VMEM((blocks, width, CH), bf16),
        pltpu.VMEM((blocks + 1, width, N), f32),
        pltpu.VMEM((blocks, heads, CH), f32),
        pltpu.VMEM((blocks, heads, CH), f32),
        pltpu.VMEM((2, width, CH), bf16),
        pltpu.VMEM((n_read, sections, width, N), bf16),
        pltpu.VMEM((CH, CH), f32),
        pltpu.VMEM((4, CH, CH), bf16),
        pltpu.VMEM((width, CH), f32),
        pltpu.VMEM((width, CH), bf16),
        pltpu.VMEM((sections, sec, width), bf16),
        dma((n_read, sections)),
        dma((sub * sections, sections)),
        dma((sections,)),
        dma((sections,)),
        dma((sections,)),
        dma((1,)),
        dma((tiles,)),
        pltpu.VMEM((width, 128), f32),
        pltpu.VMEM((heads, 128), f32),
        pltpu.VMEM((8, 2 * N), f32),
    ]
    if with_norm:
        scratch += [pltpu.VMEM((sections, sec, width), bf16), pltpu.VMEM(result, bf16)]
    return pl.pallas_call(
        functools.partial(scan_kernel, n_read, with_norm),
        grid=(sections,),
        in_specs=[
            smem,
            smem,
            pl.BlockSpec((heads * 128, sec), lambda i: (0, i)),
            pl.BlockSpec((sec, 2 * N), lambda i: (i, 0)),
            pl.BlockSpec((heads, sec), lambda i: (0, i)),
            whole(conv),
            whole(conv_bias),
            whole(head_rows),
            whole(bconv),
            whole(bconv_bias),
            whole(gain),
        ],
        out_specs=[hbm, hbm],
        out_shape=[
            jax.ShapeDtypeStruct(result, bf16),
            jax.ShapeDtypeStruct((sections, sub * sections * width, N), bf16),
        ],
        scratch_shapes=scratch,
        compiler_params=pltpu.CompilerParams(
            collective_id=1, has_side_effects=True, vmem_limit_bytes=56 * 1024 * 1024),
        cost_estimate=pl.CostEstimate(flops=10_000_000_000, bytes_accessed=30_000_000, transcendentals=0),
        name="scan",
    )(bounds, readers, xz_t, bc_raw, step_t, conv, conv_bias, head_rows, bconv, bconv_bias, gain)


def fast_shards(
    tokens,
    xz_weight,
    bc_weight,
    step_weight,
    step_bias,
    decay_log,
    skip_gain,
    conv_weight,
    conv_bias,
    bc_conv_weight,
    bc_conv_bias,
    norm_gain,
    step_bounds,
    readers,
):
    head_devices = lax.axis_size("heads")
    sections = lax.axis_size("seq")
    section = lax.axis_index("seq")
    head_block = lax.axis_index("heads")
    block_heads = H // head_devices
    mine = block_heads // sections
    first_mine = section * mine
    group = (head_block * block_heads + first_mine) // PER_GROUP
    own = lambda a, width, axis: lax.dynamic_slice_in_dim(a, first_mine * width, mine * width, axis)
    head_rows = jnp.pad(jnp.stack([step_bias, decay_log, skip_gain]), ((0, 125), (0, 128 - block_heads)))

    if head_devices == 4 and sections == 4:
        xz_t, bc_raw, step_t = gather_project(tokens, xz_weight, bc_weight, step_weight, mine)
    else:
        small_step = own(step_weight, 1, 1)
        xz_t, bc_raw, step_t = project_parts(tokens, xz_weight, bc_weight, small_step, group)

    result, handoff = scan_call(
        xz_t, bc_raw, step_t, conv_weight, conv_bias[None], head_rows, bc_conv_weight, bc_conv_bias[None],
        norm_gain[None], step_bounds, readers)
    if block_heads % PER_GROUP == 0:
        mixed, handoff = place_results(result, handoff.reshape(-1, N))
    else:
        mixed = norm_split(result, norm_gain)
    return (mixed, handoff.reshape(1, sections, -1, P_SIZE, N))


def place_results(mixed, handoff):
    def kernel(a_ref, b_ref, a_out, b_out):
        a_out[...] = a_ref[...]
        b_out[...] = b_ref[...]

    parts = 8
    specs = [pl.BlockSpec((a.shape[0] // parts, a.shape[1]), lambda i: (i, 0)) for a in (mixed, handoff)]
    return pl.pallas_call(
        kernel,
        grid=(parts,),
        in_specs=specs,
        out_specs=specs,
        out_shape=[jax.ShapeDtypeStruct(a.shape, a.dtype) for a in (mixed, handoff)],
        compiler_params=pltpu.CompilerParams(vmem_limit_bytes=62 * 1024 * 1024),
        name="place_results",
    )(mixed, handoff)


def project_parts(tokens, xz_weight, bc_weight, step_weight, group):
    head_block = lax.axis_index("heads")
    width_bc = bc_weight.shape[1]
    whole_group = width_bc >= 2 * N
    if whole_group:
        bc_weight = lax.dynamic_slice_in_dim(bc_weight, group * 2 * N - head_block * width_bc, 2 * N, 1)
    bc_width = bc_weight.shape[1]
    xz, small = project(tokens, xz_weight, jnp.concatenate([bc_weight, step_weight], axis=1), 4)
    bc_raw = small[:, :bc_width].astype(jnp.bfloat16)
    if not whole_group:
        bc_raw = lax.all_gather(bc_raw, "heads", axis=1, tiled=True)
        bc_raw = lax.dynamic_slice_in_dim(bc_raw, group * 2 * N, 2 * N, 1)
    return jnp.transpose(xz), bc_raw, jnp.transpose(small[:, bc_width:])


def norm_split(gathered, gain):
    wide = jnp.moveaxis(gathered, 0, 1).reshape(gathered.shape[1], -1).astype(jnp.float32)
    first_group = lax.axis_index("heads") * wide.shape[1] // (PER_GROUP * P_SIZE)
    at_group = lax.broadcasted_iota(jnp.int32, (1, G), 1) == first_group
    square = jnp.sum(jnp.square(wide), axis=1, keepdims=True)
    square = lax.psum(jnp.where(at_group, square, 0.0), "heads")
    square = jnp.sum(jnp.where(at_group, square, 0.0), axis=1, keepdims=True)
    scale = lax.rsqrt(square / (PER_GROUP * P_SIZE) + EPSILON)
    return (wide * scale * gain[None]).astype(jnp.bfloat16)


def solution(mesh):
    in_specs = (
        P(("groups", "seq"), "heads"),
        P(None, ("heads", "seq")),
        P(None, "heads"),
        P(None, "heads"),
        P("heads"),
        P("heads"),
        P("heads"),
        P(None, "heads"),
        P("heads"),
        P(),
        P(),
        P("heads"),
        P("groups"),
        P("groups"),
    )
    out_specs = (P(("groups", "seq"), "heads"), P(("groups", "heads"), None, "seq", None, None))
    return jax.shard_map(fast_shards, mesh=mesh, in_specs=in_specs, out_specs=out_specs, check_vma=False)
```
